128 devices in a mesh: tm: 32 (over z, y, core), chan: 4 (over x).
Axes of the slice: x: 4, y: 4, z: 4, core: 2. Of those that a mesh axis runs over, the one named last changes fastest.
Arguments:
- coarse: bfloat16 [2, 98304, 4096], P(None, 'tm', 'chan'), may hold values from -6 to 6
- prototype: float32 [16, 1024], replicated, may hold values from -4 to 4
- req_block: int32 [4, 4], replicated, may hold values from 0 to 31, as said below
- req_start: int32 [4, 4], replicated, may hold values from 0 to 80, as said below
- req_frames: int32 [4, 4], replicated, may hold values from 1 to 81
- req_count: int32 [4], replicated, may hold values from 1 to 4, as said below
Outputs:
- spectra: bfloat16 [96, 4, 4, 2, 1024, 128], P('tm', 'chan')
The draws below stay inside these ranges and needn't reach their ends.
Inputs may be any that keep to these rules, and one draw needn't show every extreme that they name: `req_block`: among the live slots of one owner at most 2 name blocks b with the same b // 8; in every draw some owner reaches 2. req_start + req_frames <= 81 in every slot; in every draw some live slot starts at hop 81 - 1 and some live slot spans all 81 frames. Slots q < req_count[c] of owner c are live, the others are empty; in every draw some owner has 4 live slots.
All inputs are finite; a program needn't handle non-finite values.
Results may differ from the reference program's by a relative error of at most 0.001.
Values may be sent and summed in bfloat16 or wider, within the bound.
No kernel may reach another device: no remote copies, remote signals or barrier semaphores. Data moves between devices by JAX's collectives and lax.ppermute only.
A program may use at most 256 MiB of HBM per device.

```python
import math
import jax
import jax.numpy as jnp
from jax import lax

CHANNELS = 4096
BLOCKW = 128
NFINE = 1024
TAPS = 16
MAXREQ = 4
PAIR = 2
OWNERS = 4
BPC = 8
TOTHOPS = 96
TIME = 98304
FRMAX = 81


def request_tables(key):
    count_key = jax.random.fold_in(key, 101)
    full_key = jax.random.fold_in(key, 102)
    base_key = jax.random.fold_in(key, 103)
    order_key = jax.random.fold_in(key, 104)
    inner_key = jax.random.fold_in(key, 105)
    frame_key = jax.random.fold_in(key, 106)
    start_key = jax.random.fold_in(key, 107)
    other_key = jax.random.fold_in(key, 108)
    lower_key = jax.random.fold_in(key, 109)
    owner_line = jnp.arange(OWNERS)
    slot_line = jnp.arange(MAXREQ)
    counts = jax.random.randint(count_key, (OWNERS,), 1, MAXREQ + 1)
    fullest = jax.random.randint(full_key, (), 0, OWNERS)
    smaller = (fullest + 1 + jax.random.randint(other_key, (), 0, OWNERS - 1)) % OWNERS
    lower_count = jax.random.randint(lower_key, (), 1, MAXREQ)
    counts = jnp.where(owner_line == smaller, lower_count, counts)
    counts = jnp.where(owner_line == fullest, MAXREQ, counts).astype(jnp.int32)
    bases = jax.random.randint(base_key, (OWNERS, 1), 0, OWNERS)
    order_keys = jax.random.split(order_key, OWNERS)
    orders = jax.vmap(lambda single: jax.random.permutation(single, MAXREQ))(order_keys)
    sources = (bases + orders // PAIR) % OWNERS
    blocks = (sources * BPC + jax.random.randint(inner_key, (OWNERS, MAXREQ), 0, BPC)).astype(jnp.int32)
    frames = jax.random.randint(frame_key, (OWNERS, MAXREQ), 1, FRMAX + 1)
    starts = jax.random.randint(start_key, (OWNERS, MAXREQ), 0, FRMAX + 1 - frames)
    is_full = owner_line[:, None] == fullest
    last_slot = is_full & (slot_line[None, :] == 0)
    whole_slot = is_full & (slot_line[None, :] == 1)
    frames = jnp.where(last_slot, 1, frames)
    frames = jnp.where(whole_slot, FRMAX, frames).astype(jnp.int32)
    starts = jnp.where(last_slot, FRMAX - 1, starts)
    starts = jnp.where(whole_slot, 0, starts).astype(jnp.int32)
    return (blocks, starts, frames, counts)


def draw_req_block(key, part):
    return request_tables(key)[0]


def draw_req_start(key, part):
    return request_tables(key)[1]


def draw_req_frames(key, part):
    return request_tables(key)[2]


def draw_req_count(key, part):
    return request_tables(key)[3]


def block_levels(own_key, extent, cuts, least, top_value):
    def one(dim, blocks):
        heights = jax.random.uniform(jax.random.fold_in(jax.random.fold_in(own_key, 6), dim), (blocks,), jnp.float32, least / len(cuts), top_value / len(cuts))
        return jnp.repeat(jnp.exp(heights), extent[dim] // blocks).reshape((-1,) + (1,) * (len(extent) - dim - 1))

    gain = one(*cuts[0])
    for cut in cuts[1:]:
        gain = gain * one(*cut)
    return gain


def scatter_about(key, extent, width, limit, cuts=(), kind=jnp.bfloat16):
    level = block_levels(key, extent, cuts, -0.22, 0.18) if cuts else 1.0
    values = jax.random.normal(key, extent, jnp.float32) * width * level
    return jnp.minimum(jnp.maximum(values, -limit), limit).astype(kind)


def setup_inputs(seed: int = 0) -> dict:
    seeds = jax.random.split(jax.random.key(seed), 7)
    return {
        "coarse": scatter_about(seeds[0], (2, TIME, CHANNELS), 1.0, 6.0, ((1, 32), (2, 4))),
        "prototype": scatter_about(seeds[1], (TAPS, NFINE), (TAPS ** -0.5), 4.0, (), jnp.float32),
        "req_block": draw_req_block(jax.random.fold_in(seeds[6], 71), 0),
        "req_start": draw_req_start(jax.random.fold_in(seeds[6], 71), 0),
        "req_frames": draw_req_frames(jax.random.fold_in(seeds[6], 71), 0),
        "req_count": draw_req_count(jax.random.fold_in(seeds[6], 71), 0),
    }


def reference(coarse, prototype, req_block, req_start, req_frames, req_count):
    hop_ids = jnp.arange(TOTHOPS, dtype=jnp.int32)
    results = []
    for owner in range(OWNERS):
        for slot_index in range(MAXREQ):
            first_col = (req_block[owner, slot_index] * BLOCKW).astype(jnp.int32)
            block_data = lax.dynamic_slice(coarse, (jnp.int32(0), jnp.int32(0), first_col), (2, TIME, BLOCKW))
            block_data = block_data.astype(jnp.float32).reshape(2, TOTHOPS, NFINE, BLOCKW)
            padding = jnp.zeros((2, TAPS - 1, NFINE, BLOCKW), jnp.float32)
            padded = jnp.concatenate([block_data, padding.astype(block_data.dtype)], axis=1)
            filtered = jnp.zeros((2, TOTHOPS, NFINE, BLOCKW), block_data.dtype)
            for tap_index in range(TAPS):
                weights = prototype[tap_index][None, None, :, None]
                filtered = filtered + weights * padded[:, tap_index:tap_index + TOTHOPS]
            transformed = jnp.fft.fft(filtered[0] + 1j * filtered[1], axis=1) / math.sqrt(NFINE)
            stacked = jnp.stack([jnp.real(transformed), jnp.imag(transformed)], axis=1)
            begin = req_start[owner, slot_index]
            active = (slot_index < req_count[owner]) & (hop_ids >= begin) & (hop_ids < begin + req_frames[owner, slot_index])
            masked = jnp.where(active[:, None, None, None], stacked, jnp.zeros_like(stacked))
            results.append(masked.astype(jnp.bfloat16))
    spectra = jnp.stack(results, axis=1)
    return spectra.reshape(TOTHOPS, OWNERS, MAXREQ, 2, NFINE, BLOCKW)
```

```python
import math

import jax
import jax.numpy as jnp
import ml_dtypes
import numpy as np
from jax import lax
from jax.experimental import pallas as pl
from jax.experimental.pallas import tpu as pltpu
from jax.sharding import PartitionSpec as P

BLOCKW = 128
NFINE = 1024
TAPS = 16
HOPS_DEV = 3
MAXREQ = 4
PAIR = 2
TM = 32
OWNERS = 4
BPC = 8
HOPS = 96
SHARE = BLOCKW // TM
ROWS = 2 * SHARE
RADIX = 8
LANES = 128
FRAMES = 84
GROUP = 12


def pick_matrix():
    pick = np.zeros((2 * BLOCKW, 2 * BLOCKW), np.float32)
    for device in range(TM):
        for part in range(2):
            for column in range(SHARE):
                pick[device * ROWS + part * SHARE + column, part * BLOCKW + device * SHARE + column] = 1
    return pick.astype(ml_dtypes.bfloat16)


def dft_tables():
    k2 = np.arange(LANES)[None, :, None]
    m = np.arange(RADIX)[:, None, None] + RADIX * np.arange(LANES)[None, None, :]
    angles = (k2 * m % NFINE) * (2.0 * math.pi / NFINE)
    table = np.concatenate([np.cos(angles), np.sin(angles)], axis=2) / math.sqrt(NFINE)
    high = table.astype(np.float32).astype(ml_dtypes.bfloat16)
    low = (table - high.astype(np.float64)).astype(np.float32).astype(ml_dtypes.bfloat16)
    return np.concatenate([high, high], axis=1), low


def pack_kernel(block_ref, count_ref, column_ref, x_ref, pick_ref, out_ref):
    for hop in range(HOPS_DEV):
        rows = pl.ds(hop * NFINE, NFINE)
        both = jnp.concatenate([x_ref[0, rows, :], x_ref[1, rows, :]], axis=1)
        turned = lax.dot_general(
            pick_ref[...], both, (((1,), (1,)), ((), ())), preferred_element_type=jnp.float32
        )
        out_ref[:, 0, 0, hop] = turned.reshape(TM, ROWS, NFINE).astype(jnp.bfloat16)


def wanted_block(owner, rank, block_ref, count_ref, column_ref):
    seen = jnp.int32(0)
    chosen = jnp.int32(0)
    for slot in range(MAXREQ):
        block = block_ref[owner, slot]
        mine = (slot < count_ref[owner]) & (block // BPC == column_ref[0])
        chosen = jnp.where(mine & (seen == rank), block % BPC, chosen)
        seen = seen + mine.astype(jnp.int32)
    return chosen


def pack(coarse, pick, req_block, req_count, column):
    return pl.pallas_call(
        pack_kernel,
        out_shape=jax.ShapeDtypeStruct((TM, OWNERS, PAIR, HOPS_DEV, ROWS, NFINE), jnp.bfloat16),
        grid_spec=pltpu.PrefetchScalarGridSpec(
            num_scalar_prefetch=3,
            grid=(OWNERS, PAIR),
            in_specs=[
                pl.BlockSpec(
                    (2, HOPS_DEV * NFINE, BLOCKW),
                    lambda c, r, *refs: (0, 0, wanted_block(c, r, *refs)),
                ),
                pl.BlockSpec((2 * BLOCKW, 2 * BLOCKW), lambda c, r, *refs: (0, 0)),
            ],
            out_specs=pl.BlockSpec(
                (TM, 1, 1, HOPS_DEV, ROWS, NFINE), lambda c, r, *refs: (0, c, r, 0, 0, 0)
            ),
        ),
        name="pack",
    )(req_block, req_count, column, coarse, pick)


def turn(value, sign):
    return pltpu.roll(value, SHARE, value.ndim - 2) * sign


def dft4(a, b, c, d, sign):
    s02, d02, s13, d13 = a + c, a - c, b + d, turn(b - d, sign)
    return s02 + s13, d02 + d13, s02 - s13, d02 - d13


def dft8(x, sign):
    half = math.sqrt(0.5)
    low = [x[i] + x[i + 4] for i in range(4)]
    high = [x[i] - x[i + 4] for i in range(4)]
    high[1] = (high[1] + turn(high[1], sign)) * half
    high[2] = turn(high[2], sign)
    high[3] = (turn(high[3], sign) - high[3]) * half
    even, odd = dft4(*low, sign), dft4(*high, sign)
    return [pair for both in zip(even, odd) for pair in both]


def filter_kernel(block_ref, count_ref, column_ref, x_ref, proto_ref, tall_ref, low_ref, out_ref, wide_ref, fir_ref, split_ref):
    sign = jnp.where(lax.broadcasted_iota(jnp.int32, (ROWS, LANES), 0) < SHARE, 1.0, -1.0)
    wide_ref[HOPS:, :, :] = jnp.zeros((FRAMES + TAPS - 1 - HOPS, ROWS, LANES), jnp.float32)
    for tile in range(RADIX):
        lanes = pl.ds(tile * LANES, LANES)
        wide_ref[:HOPS] = x_ref[:, 0, 0, :, :, lanes].astype(jnp.float32).reshape(HOPS, ROWS, LANES)
        weights = [jnp.broadcast_to(proto_ref[tap, lanes].reshape(1, LANES), (ROWS, LANES)) for tap in range(TAPS)]

        def fir(step, carry):
            first = step * GROUP
            samples = wide_ref[pl.ds(first, GROUP + TAPS - 1)]
            total = samples[:GROUP] * weights[0]
            for tap in range(1, TAPS):
                total = total + samples[tap : tap + GROUP] * weights[tap]
            fir_ref[pl.ds(first, GROUP), :, lanes] = total
            return carry

        lax.fori_loop(0, FRAMES // GROUP, fir, 0)

    def butterflies(step, carry):
        first = step * 2
        parts = [fir_ref[pl.ds(first, 2), :, tile * LANES : (tile + 1) * LANES] for tile in range(RADIX)]
        rows = pl.ds(pl.multiple_of(first * ROWS, 2 * ROWS), 2 * ROWS)
        for m1, value in enumerate(dft8(parts, sign)):
            value = value.reshape(2 * ROWS, LANES)
            high = value.astype(jnp.bfloat16)
            split_ref[m1, rows, :LANES] = high
            split_ref[m1, rows, LANES:] = (value - high.astype(jnp.float32)).astype(jnp.bfloat16)
        return carry

    lax.fori_loop(0, FRAMES // 2, butterflies, 0)
    for m1 in range(RADIX):
        both = split_ref[m1]
        product = jnp.dot(both, tall_ref[m1], preferred_element_type=jnp.float32)
        product = product + jnp.dot(both[:, :LANES], low_ref[m1], preferred_element_type=jnp.float32)
        cosines = product[:, :LANES].reshape(FRAMES, ROWS, LANES)
        sines = product[:, LANES:].reshape(FRAMES, ROWS, LANES)
        result = (cosines + turn(sines, sign)).astype(jnp.bfloat16)
        out_ref[: FRAMES // HOPS_DEV, :, 0, :, m1 * LANES : (m1 + 1) * LANES] = result.reshape(
            FRAMES // HOPS_DEV, HOPS_DEV, ROWS, LANES
        )


def arrival(slot, block_ref, count_ref, column_ref):
    owner = column_ref[0]
    source = block_ref[owner, slot] // BPC
    rank = jnp.int32(0)
    for other in range(MAXREQ - 1):
        same = (other < slot) & (block_ref[owner, other] // BPC == source)
        rank = rank + same.astype(jnp.int32)
    return source, jnp.minimum(rank, PAIR - 1)


def filter_and_transform(arrived, prototype, tall, low, req_block, req_count, column):
    def arrived_map(q, *refs):
        source, rank = arrival(q, *refs)
        return (0, source, rank, 0, 0, 0)

    return pl.pallas_call(
        filter_kernel,
        out_shape=jax.ShapeDtypeStruct((TM, HOPS_DEV, MAXREQ, ROWS, NFINE), jnp.bfloat16),
        grid_spec=pltpu.PrefetchScalarGridSpec(
            num_scalar_prefetch=3,
            grid=(MAXREQ,),
            in_specs=[
                pl.BlockSpec((TM, 1, 1, HOPS_DEV, ROWS, NFINE), arrived_map),
                pl.BlockSpec((TAPS, NFINE), lambda q, *refs: (0, 0)),
                pl.BlockSpec((RADIX, 2 * LANES, 2 * LANES), lambda q, *refs: (0, 0, 0)),
                pl.BlockSpec((RADIX, LANES, 2 * LANES), lambda q, *refs: (0, 0, 0)),
            ],
            out_specs=pl.BlockSpec(
                (TM, HOPS_DEV, 1, ROWS, NFINE), lambda q, *refs: (0, 0, q, 0, 0)
            ),
            scratch_shapes=[
                pltpu.VMEM((FRAMES + TAPS - 1, ROWS, LANES), jnp.float32),
                pltpu.VMEM((FRAMES, ROWS, NFINE), jnp.float32),
                pltpu.VMEM((RADIX, FRAMES * ROWS, 2 * LANES), jnp.bfloat16),
            ],
        ),
        name="filter",
    )(req_block, req_count, column, arrived, prototype, tall, low)


def unpack_kernel(start_ref, frames_ref, count_ref, place_ref, y_ref, pick_ref, out_ref, turned_ref):
    slot = pl.program_id(1)
    owner = place_ref[0]
    hop = place_ref[1] * HOPS_DEV + pl.program_id(0)
    begin = start_ref[owner, slot]
    active = (slot < count_ref[owner]) & (hop >= begin) & (hop < begin + frames_ref[owner, slot])

    @pl.when(active)
    def _():
        rows = y_ref[:, 0, 0].astype(jnp.float32).reshape(TM * ROWS, NFINE).astype(jnp.bfloat16)
        for m1 in range(RADIX):
            columns = lax.dot_general(
                rows[:, m1 * LANES : (m1 + 1) * LANES],
                pick_ref[...],
                (((0,), (0,)), ((), ())),
                preferred_element_type=jnp.float32,
            )
            for part in range(2):
                turned_ref[part, pl.ds(m1, LANES, stride=RADIX), :] = columns[:, part * LANES : (part + 1) * LANES]
        out_ref[0, 0, 0] = turned_ref[...].astype(jnp.bfloat16)

    @pl.when(jnp.logical_not(active))
    def _():
        out_ref[...] = jnp.zeros_like(out_ref)


def unpack(returned, pick, req_start, req_frames, req_count, place):
    return pl.pallas_call(
        unpack_kernel,
        out_shape=jax.ShapeDtypeStruct((HOPS_DEV, 1, MAXREQ, 2, NFINE, BLOCKW), jnp.bfloat16),
        grid_spec=pltpu.PrefetchScalarGridSpec(
            num_scalar_prefetch=4,
            grid=(HOPS_DEV, MAXREQ),
            in_specs=[
                pl.BlockSpec((TM, 1, 1, ROWS, NFINE), lambda h, q, *refs: (0, h, q, 0, 0)),
                pl.BlockSpec((2 * BLOCKW, 2 * BLOCKW), lambda h, q, *refs: (0, 0)),
            ],
            out_specs=pl.BlockSpec(
                (1, 1, 1, 2, NFINE, BLOCKW), lambda h, q, *refs: (h, 0, q, 0, 0, 0)
            ),
            scratch_shapes=[pltpu.VMEM((2, NFINE, BLOCKW), jnp.float32)],
        ),
        name="unpack",
    )(req_start, req_frames, req_count, place, returned, pick)


def shards(coarse, prototype, req_block, req_start, req_frames, req_count):
    column = lax.axis_index("chan").astype(jnp.int32)
    place = jnp.stack([column, lax.axis_index("tm").astype(jnp.int32)])
    pick = jnp.asarray(pick_matrix())
    tall, low = (jnp.asarray(table) for table in dft_tables())
    outgoing = pack(coarse, pick, req_block, req_count, place)
    outgoing = outgoing.reshape(TM * OWNERS, PAIR, HOPS_DEV, ROWS, NFINE)
    arrived = lax.all_to_all(outgoing, ("tm", "chan"), split_axis=0, concat_axis=0, tiled=True)
    arrived = arrived.reshape(TM, OWNERS, PAIR, HOPS_DEV, ROWS, NFINE)
    result = filter_and_transform(arrived, prototype, tall, low, req_block, req_count, place)
    returned = lax.all_to_all(result, "tm", split_axis=0, concat_axis=0, tiled=True)
    return unpack(returned, pick, req_start, req_frames, req_count, place)


def solution(mesh):
    return jax.shard_map(
        shards,
        mesh=mesh,
        in_specs=(P(None, "tm", "chan"), P(), P(), P(), P(), P()),
        out_specs=P("tm", "chan", None, None, None, None),
        check_vma=False,
    )
```

```python
import math

import jax
import jax.numpy as jnp
import ml_dtypes
import numpy as np
from jax import lax
from jax.experimental import pallas as pl
from jax.experimental.pallas import tpu as pltpu
from jax.sharding import PartitionSpec as P

BLOCKW = 128
NFINE = 1024
TAPS = 16
HOPS_DEV = 3
MAXREQ = 4
PAIR = 2
TM = 32
OWNERS = 4
BPC = 8
HOPS = 96
HALF = BLOCKW // 2
SHARE = HALF // TM
ROWS = 8
RADIX = 8
LANES = 128
FRAMES = 84
GROUP = 12


def late_pick():
    pick = np.zeros((TM, 2, PAIR, SHARE, PAIR, 2, BLOCKW), np.float32)
    for device, part, rank, column in np.ndindex(TM, 2, PAIR, SHARE):
        pick[device, part, rank, column, rank, part, HALF + device * SHARE + column] = 1
    return pick.reshape(TM * ROWS, PAIR * 2 * BLOCKW).astype(ml_dtypes.bfloat16)


def early_pick():
    pick = np.zeros((TM, 2, 2, SHARE, 2, 2, HALF), np.float32)
    for device, part, slot, column in np.ndindex(TM, 2, 2, SHARE):
        pick[device, part, slot, column, slot, part, device * SHARE + column] = 1
    return pick.reshape(TM * ROWS, 2 * BLOCKW).astype(ml_dtypes.bfloat16)


def lower_half():
    pick = np.zeros((2, BLOCKW, 2, HALF), np.float32)
    for part, column in np.ndindex(2, HALF):
        pick[part, column, part, column] = 1
    return pick.reshape(2 * BLOCKW, BLOCKW).astype(ml_dtypes.bfloat16)


def dft_tables():
    k2 = np.arange(LANES)[None, :, None]
    m = np.arange(RADIX)[:, None, None] + RADIX * np.arange(LANES)[None, None, :]
    angles = (k2 * m % NFINE) * (2.0 * math.pi / NFINE)
    table = np.concatenate([np.cos(angles), np.sin(angles)], axis=2) / math.sqrt(NFINE)
    high = table.astype(np.float32).astype(ml_dtypes.bfloat16)
    low = (table - high.astype(np.float64)).astype(np.float32).astype(ml_dtypes.bfloat16)
    return high, low


def wanted_block(shift, rank, block_ref, count_ref, place_ref):
    owner = (place_ref[0] + shift) % OWNERS
    seen = jnp.int32(0)
    chosen = jnp.int32(0)
    for slot in range(MAXREQ):
        block = block_ref[owner, slot]
        mine = (slot < count_ref[owner]) & (block // BPC == place_ref[0])
        chosen = jnp.where(mine & (seen == rank), block % BPC, chosen)
        seen = seen + mine.astype(jnp.int32)
    return chosen


def pack_early_kernel(block_ref, count_ref, place_ref, x_ref, lower_ref, *out_refs):
    def write(out_ref):
        for hop in range(HOPS_DEV):
            rows = pl.ds(hop * NFINE, NFINE)
            both = jnp.concatenate([x_ref[0, rows, :], x_ref[1, rows, :]], axis=1)
            out_ref[0, hop] = jnp.dot(both, lower_ref[...], preferred_element_type=jnp.float32).astype(jnp.bfloat16)

    for shift, out_ref in enumerate(out_refs):
        pl.when(pl.program_id(0) == shift)(lambda out_ref=out_ref: write(out_ref))


def pack_early(coarse, lower, req_block, req_count, place):
    def out_map(own, d, r):
        return (jnp.where(d < own, 0, jnp.where(d > own, PAIR - 1, r)), 0, 0, 0)

    return pl.pallas_call(
        pack_early_kernel,
        out_shape=[jax.ShapeDtypeStruct((PAIR, HOPS_DEV, NFINE, BLOCKW), jnp.bfloat16)] * OWNERS,
        grid_spec=pltpu.PrefetchScalarGridSpec(
            num_scalar_prefetch=3,
            grid=(OWNERS, PAIR),
            in_specs=[
                pl.BlockSpec(
                    (2, HOPS_DEV * NFINE, BLOCKW),
                    lambda d, r, *refs: (0, 0, wanted_block(d, r, *refs)),
                ),
                pl.BlockSpec((2 * BLOCKW, BLOCKW), lambda d, r, *refs: (0, 0)),
            ],
            out_specs=[
                pl.BlockSpec(
                    (1, HOPS_DEV, NFINE, BLOCKW), lambda d, r, *refs, own=own: out_map(own, d, r)
                )
                for own in range(OWNERS)
            ],
        ),
        name="pack_early",
    )(req_block, req_count, place, coarse, lower)


def pack_late_kernel(block_ref, count_ref, place_ref, x0_ref, x1_ref, pick_ref, out_ref):
    for hop in range(HOPS_DEV):
        rows = pl.ds(hop * NFINE, NFINE)
        wide = jnp.concatenate([x0_ref[0, rows, :], x0_ref[1, rows, :], x1_ref[0, rows, :], x1_ref[1, rows, :]], axis=1)
        turned = lax.dot_general(
            pick_ref[...], wide, (((1,), (1,)), ((), ())), preferred_element_type=jnp.float32
        )
        out_ref[:, 0, hop] = turned.reshape(TM, ROWS, NFINE).astype(jnp.bfloat16)


def pack_late(coarse, pick, req_block, req_count, place):
    def block_spec(rank):
        return pl.BlockSpec(
            (2, HOPS_DEV * NFINE, BLOCKW), lambda d, *refs: (0, 0, wanted_block(d, rank, *refs))
        )

    return pl.pallas_call(
        pack_late_kernel,
        out_shape=jax.ShapeDtypeStruct((TM, OWNERS, HOPS_DEV, ROWS, NFINE), jnp.bfloat16),
        grid_spec=pltpu.PrefetchScalarGridSpec(
            num_scalar_prefetch=3,
            grid=(OWNERS,),
            in_specs=[
                block_spec(0),
                block_spec(1),
                pl.BlockSpec((TM * ROWS, PAIR * 2 * BLOCKW), lambda d, *refs: (0, 0)),
            ],
            out_specs=pl.BlockSpec(
                (TM, 1, HOPS_DEV, ROWS, NFINE), lambda d, *refs: (0, d, 0, 0, 0)
            ),
        ),
        name="pack_late",
    )(req_block, req_count, place, coarse, coarse, pick)


def arrival(slot, block_ref, place_ref):
    owner = place_ref[0]
    source = block_ref[owner, slot] // BPC
    rank = jnp.int32(0)
    for other in range(slot):
        rank = rank + (block_ref[owner, other] // BPC == source).astype(jnp.int32)
    return (owner - source + OWNERS) % OWNERS, jnp.minimum(rank, PAIR - 1)


def choose_kernel(block_ref, place_ref, a0, a1, a2, a3, pick_ref, out_ref, held_ref, sem):
    pair, hop = pl.program_id(0), pl.program_id(1)

    @pl.when((pair == 0) & (hop == 0))
    def _():
        for slot in range(MAXREQ):
            shift, rank = arrival(slot, block_ref, place_ref)
            for own, ref in enumerate((a0, a1, a2, a3)):

                @pl.when(shift == own)
                def _():
                    pltpu.make_async_copy(ref.at[rank], held_ref.at[slot], sem.at[slot]).start()

    @pl.when(hop == 0)
    def _():
        for slot in range(2):
            at = pair * 2 + slot
            pltpu.make_async_copy(a0.at[0], held_ref.at[at], sem.at[at]).wait()

    both = jnp.concatenate([held_ref[pair * 2, hop], held_ref[pair * 2 + 1, hop]], axis=1)
    turned = lax.dot_general(
        pick_ref[...], both, (((1,), (1,)), ((), ())), preferred_element_type=jnp.float32
    )
    out_ref[:, 0, 0] = turned.reshape(TM, ROWS, NFINE).astype(jnp.bfloat16)


def choose(arrived, pick, req_block, place):
    return pl.pallas_call(
        choose_kernel,
        out_shape=jax.ShapeDtypeStruct((TM, MAXREQ // 2, HOPS_DEV, ROWS, NFINE), jnp.bfloat16),
        grid_spec=pltpu.PrefetchScalarGridSpec(
            num_scalar_prefetch=2,
            grid=(MAXREQ // 2, HOPS_DEV),
            in_specs=[pl.BlockSpec(memory_space=pl.ANY)] * OWNERS
            + [pl.BlockSpec((TM * ROWS, 2 * BLOCKW), lambda p, h, *refs: (0, 0))],
            out_specs=pl.BlockSpec(
                (TM, 1, 1, ROWS, NFINE), lambda p, h, *refs: (0, p, h, 0, 0)
            ),
            scratch_shapes=[
                pltpu.VMEM((MAXREQ, HOPS_DEV, NFINE, BLOCKW), jnp.bfloat16),
                pltpu.SemaphoreType.DMA((MAXREQ,)),
            ],
        ),
        name="choose",
    )(req_block, place, *arrived, pick)


def turn(value, sign):
    return pltpu.roll(value, ROWS // 2, value.ndim - 2) * sign


def dft4(a, b, c, d, sign):
    s02, d02, s13, d13 = a + c, a - c, b + d, turn(b - d, sign)
    return s02 + s13, d02 + d13, s02 - s13, d02 - d13


def dft8(x, sign):
    half = math.sqrt(0.5)
    low = [x[i] + x[i + 4] for i in range(4)]
    high = [x[i] - x[i + 4] for i in range(4)]
    high[1] = (high[1] + turn(high[1], sign)) * half
    high[2] = turn(high[2], sign)
    high[3] = (turn(high[3], sign) - high[3]) * half
    even, odd = dft4(*low, sign), dft4(*high, sign)
    return [pair for both in zip(even, odd) for pair in both]


def transform(load, proto_ref, high_ref, low_ref, out_ref, wide_ref, fir_ref, split_ref):
    sign = jnp.where(lax.broadcasted_iota(jnp.int32, (ROWS, LANES), 0) < ROWS // 2, 1.0, -1.0)
    wide_ref[HOPS:, :, :] = jnp.zeros((FRAMES + TAPS - 1 - HOPS, ROWS, LANES), jnp.float32)
    def taps(tile, carry):
        lanes = pl.ds(pl.multiple_of(tile * LANES, LANES), LANES)
        wide_ref[:HOPS] = load(lanes)
        weights = [jnp.broadcast_to(proto_ref[tap, lanes].reshape(1, LANES), (ROWS, LANES)) for tap in range(TAPS)]

        def fir(step, inner):
            first = step * GROUP
            samples = wide_ref[pl.ds(first, GROUP + TAPS - 1)]
            total = samples[:GROUP] * weights[0]
            for tap in range(1, TAPS):
                total = total + samples[tap : tap + GROUP] * weights[tap]
            fir_ref[pl.ds(first, GROUP), :, lanes] = total
            return inner

        return lax.fori_loop(0, FRAMES // GROUP, fir, carry)

    lax.fori_loop(0, RADIX, taps, 0)

    def butterflies(step, carry):
        first = step * 2
        parts = [fir_ref[pl.ds(first, 2), :, tile * LANES : (tile + 1) * LANES] for tile in range(RADIX)]
        rows = pl.ds(pl.multiple_of(first * ROWS, 2 * ROWS), 2 * ROWS)
        for m1, value in enumerate(dft8(parts, sign)):
            value = value.reshape(2 * ROWS, LANES)
            high = value.astype(jnp.bfloat16)
            split_ref[m1, rows, :LANES] = high
            split_ref[m1, rows, LANES:] = (value - high.astype(jnp.float32)).astype(jnp.bfloat16)
        return carry

    lax.fori_loop(0, FRAMES // 2, butterflies, 0)
    for m1 in range(RADIX):
        both = split_ref[m1]
        high = high_ref[m1]
        product = jnp.dot(both, jnp.concatenate([high, high], axis=0), preferred_element_type=jnp.float32)
        product = product + jnp.dot(both[:, :LANES], low_ref[m1], preferred_element_type=jnp.float32)
        cosines = product[:, :LANES].reshape(FRAMES, ROWS, LANES)
        sines = product[:, LANES:].reshape(FRAMES, ROWS, LANES)
        result = (cosines + turn(sines, sign)).astype(jnp.bfloat16)
        out_ref[: FRAMES // HOPS_DEV, :, 0, :, m1 * LANES : (m1 + 1) * LANES] = result.reshape(
            FRAMES // HOPS_DEV, HOPS_DEV, ROWS, LANES
        )


def early_kernel(x_ref, *refs):
    def load(lanes):
        return x_ref[:, 0, :, :, lanes].astype(jnp.float32).reshape(HOPS, ROWS, LANES)

    transform(load, *refs)


def late_kernel(block_ref, place_ref, a0, a1, a2, a3, proto_ref, high_ref, low_ref, out_ref, wide_ref, fir_ref, split_ref, held_ref, sem):
    pair = pl.program_id(0)

    @pl.when(pair == 0)
    def _():
        for slot in range(MAXREQ):
            shift, _ = arrival(slot, block_ref, place_ref)
            for own, ref in enumerate((a0.at[:, 0], a1, a2, a3)):

                @pl.when(shift == own)
                def _():
                    pltpu.make_async_copy(ref, held_ref.at[slot], sem.at[slot]).start()

    for slot in range(2):
        at = pair * 2 + slot
        pltpu.make_async_copy(a1, held_ref.at[at], sem.at[at]).wait()

    ranks = [arrival(slot, block_ref, place_ref)[1] for slot in range(MAXREQ)]
    first_rank = jnp.where(pair == 0, ranks[0], ranks[2])
    second_rank = jnp.where(pair == 0, ranks[1], ranks[3])
    is_second = (lax.broadcasted_iota(jnp.int32, (HOPS, ROWS, LANES), 1) // SHARE) % 2 == 1

    def load(lanes):
        first = held_ref[pair * 2, :, :, :, lanes].astype(jnp.float32).reshape(HOPS, ROWS, LANES)
        second = held_ref[pair * 2 + 1, :, :, :, lanes].astype(jnp.float32).reshape(HOPS, ROWS, LANES)
        first = jnp.where(first_rank == 0, first, pltpu.roll(first, ROWS - SHARE, 1))
        second = jnp.where(second_rank == 1, second, pltpu.roll(second, SHARE, 1))
        return jnp.where(is_second, second, first)

    transform(load, proto_ref, high_ref, low_ref, out_ref, wide_ref, fir_ref, split_ref)


def table_specs():
    return [
        pl.BlockSpec((TAPS, NFINE), lambda p, *refs: (0, 0)),
        pl.BlockSpec((RADIX, LANES, 2 * LANES), lambda p, *refs: (0, 0, 0)),
        pl.BlockSpec((RADIX, LANES, 2 * LANES), lambda p, *refs: (0, 0, 0)),
    ]


RESULT = jax.ShapeDtypeStruct((TM, HOPS_DEV, MAXREQ // 2, ROWS, NFINE), jnp.bfloat16)


def result_spec():
    return pl.BlockSpec((TM, HOPS_DEV, 1, ROWS, NFINE), lambda p, *refs: (0, 0, p, 0, 0))


def work_space():
    return [
        pltpu.VMEM((FRAMES + TAPS - 1, ROWS, LANES), jnp.float32),
        pltpu.VMEM((FRAMES, ROWS, NFINE), jnp.float32),
        pltpu.VMEM((RADIX, FRAMES * ROWS, 2 * LANES), jnp.bfloat16),
    ]


def filter_early(gathered, tables):
    return pl.pallas_call(
        early_kernel,
        out_shape=RESULT,
        grid=(MAXREQ // 2,),
        in_specs=[
            pl.BlockSpec((TM, 1, HOPS_DEV, ROWS, NFINE), lambda p: (0, p, 0, 0, 0)),
            *table_specs(),
        ],
        out_specs=result_spec(),
        scratch_shapes=work_space(),
        name="filter_early",
    )(gathered, *tables)


def filter_late(arrived, tables, req_block, place):
    return pl.pallas_call(
        late_kernel,
        out_shape=RESULT,
        grid_spec=pltpu.PrefetchScalarGridSpec(
            num_scalar_prefetch=2,
            grid=(MAXREQ // 2,),
            in_specs=[pl.BlockSpec(memory_space=pl.ANY)] * OWNERS + table_specs(),
            out_specs=result_spec(),
            scratch_shapes=work_space()
            + [
                pltpu.VMEM((MAXREQ, TM, HOPS_DEV, ROWS, NFINE), jnp.bfloat16),
                pltpu.SemaphoreType.DMA((MAXREQ,)),
            ],
        ),
        name="filter_late",
    )(req_block, place, *arrived, *tables)


def final_pick(slot):
    shape = (2 * TM * ROWS, 2 * BLOCKW)
    row, column = (lax.broadcasted_iota(jnp.int32, shape, dim) for dim in range(2))
    place = (row // ROWS) * SHARE + row % SHARE + BLOCKW * ((row // 4) % 2)
    return jnp.where((place == column) & ((row // 2) % 2 == slot), 1.0, 0.0).astype(jnp.bfloat16)


def unpack_kernel(start_ref, frames_ref, count_ref, place_ref, early_ref, late_ref, out_ref, turned_ref, pick_ref):
    slot = pl.program_id(1)

    @pl.when((slot == 0) & (pl.program_id(0) == 0))
    def _():
        for which in range(2):
            pick_ref[which] = final_pick(which)

    owner = place_ref[0]
    hop = place_ref[1] * HOPS_DEV + pl.program_id(0)
    begin = start_ref[owner, slot]
    active = (slot < count_ref[owner]) & (hop >= begin) & (hop < begin + frames_ref[owner, slot])

    @pl.when(active)
    def _():
        rows = jnp.concatenate([early_ref[:, 0, 0], late_ref[:, 0, 0]], axis=0)
        rows = rows.astype(jnp.float32).reshape(2 * TM * ROWS, NFINE).astype(jnp.bfloat16)
        for m1 in range(RADIX):
            columns = lax.dot_general(
                rows[:, m1 * LANES : (m1 + 1) * LANES],
                pick_ref[slot % 2],
                (((0,), (0,)), ((), ())),
                preferred_element_type=jnp.float32,
            )
            for part in range(2):
                turned_ref[part, pl.ds(m1, LANES, stride=RADIX), :] = columns[:, part * LANES : (part + 1) * LANES]
        out_ref[0, 0, 0] = turned_ref[...].astype(jnp.bfloat16)

    @pl.when(jnp.logical_not(active))
    def _():
        out_ref[...] = jnp.zeros_like(out_ref)


def unpack(early, late, req_start, req_frames, req_count, place):
    back_spec = pl.BlockSpec((TM, 1, 1, ROWS, NFINE), lambda h, q, *refs: (0, h, q // 2, 0, 0))
    return pl.pallas_call(
        unpack_kernel,
        out_shape=jax.ShapeDtypeStruct((HOPS_DEV, 1, MAXREQ, 2, NFINE, BLOCKW), jnp.bfloat16),
        grid_spec=pltpu.PrefetchScalarGridSpec(
            num_scalar_prefetch=4,
            grid=(HOPS_DEV, MAXREQ),
            in_specs=[
                back_spec,
                back_spec,
            ],
            out_specs=pl.BlockSpec(
                (1, 1, 1, 2, NFINE, BLOCKW), lambda h, q, *refs: (h, 0, q, 0, 0, 0)
            ),
            scratch_shapes=[
                pltpu.VMEM((2, NFINE, BLOCKW), jnp.float32),
                pltpu.VMEM((2, 2 * TM * ROWS, 2 * BLOCKW), jnp.bfloat16),
            ],
        ),
        name="unpack",
    )(req_start, req_frames, req_count, place, early, late)


def over_tm(array):
    return lax.all_to_all(array, "tm", split_axis=0, concat_axis=0, tiled=True)


def along_chan(arrays):
    return [arrays[0]] + [
        lax.ppermute(arrays[d], "chan", [(s, (s + d) % OWNERS) for s in range(OWNERS)])
        for d in range(1, OWNERS)
    ]


def shards(coarse, prototype, req_block, req_start, req_frames, req_count):
    column = lax.axis_index("chan").astype(jnp.int32)
    place = jnp.stack([column, lax.axis_index("tm").astype(jnp.int32)])
    tables = (prototype, *(jnp.asarray(table) for table in dft_tables()))
    late = pack_late(coarse, jnp.asarray(late_pick()), req_block, req_count, place)
    early = pack_early(coarse, jnp.asarray(lower_half()), req_block, req_count, place)
    late = over_tm(late)
    early = choose(along_chan(early), jnp.asarray(early_pick()), req_block, place)
    late, early = lax.optimization_barrier((late, early))
    early = over_tm(early)
    late = along_chan([late] + [late[:, d] for d in range(1, OWNERS)])
    early = filter_early(early, tables)
    _, *late = lax.optimization_barrier((early, *late))
    early = over_tm(early)
    late = over_tm(filter_late(late, tables, req_block, place))
    return unpack(early, late, req_start, req_frames, req_count, place)


def solution(mesh):
    return jax.shard_map(
        shards,
        mesh=mesh,
        in_specs=(P(None, "tm", "chan"), P(), P(), P(), P(), P()),
        out_specs=P("tm", "chan", None, None, None, None),
        check_vma=False,
    )
```

```python
import math

import jax
import jax.numpy as jnp
import ml_dtypes
import numpy as np
from jax import lax
from jax.experimental import pallas as pl
from jax.experimental.pallas import tpu as pltpu
from jax.sharding import PartitionSpec as P

BLOCKW = 128
NFINE = 1024
TAPS = 16
HOPS_DEV = 3
MAXREQ = 4
PAIR = 2
TM = 32
OWNERS = 4
BPC = 8
HOPS = 96
HALF = BLOCKW // 2
SHARE = HALF // TM
ROWS = 8
RADIX = 8
LANES = 128
FRAMES = 84
GROUP = 12


def late_pick():
    pick = np.zeros((TM, 2, PAIR, SHARE, PAIR, 2, BLOCKW), np.float32)
    for device, part, rank, column in np.ndindex(TM, 2, PAIR, SHARE):
        pick[device, part, rank, column, rank, part, HALF + device * SHARE + column] = 1
    return pick.reshape(TM * ROWS, PAIR * 2 * BLOCKW).astype(ml_dtypes.bfloat16)


def early_pick():
    pick = np.zeros((TM, 2, 2, SHARE, 2, 2, HALF), np.float32)
    for device, part, slot, column in np.ndindex(TM, 2, 2, SHARE):
        pick[device, part, slot, column, slot, part, device * SHARE + column] = 1
    return pick.reshape(TM * ROWS, 2 * BLOCKW).astype(ml_dtypes.bfloat16)


def dft_tables():
    k2 = np.arange(LANES)[None, :, None]
    m = np.arange(RADIX)[:, None, None] + RADIX * np.arange(LANES)[None, None, :]
    angles = (k2 * m % NFINE) * (2.0 * math.pi / NFINE)
    table = np.concatenate([np.cos(angles), np.sin(angles)], axis=2) / math.sqrt(NFINE)
    high = table.astype(np.float32).astype(ml_dtypes.bfloat16)
    low = (table - high.astype(np.float64)).astype(np.float32).astype(ml_dtypes.bfloat16)
    return high, low


def wanted_block(shift, rank, block_ref, count_ref, place_ref):
    owner = (place_ref[0] + shift) % OWNERS
    seen = jnp.int32(0)
    chosen = jnp.int32(0)
    for slot in range(MAXREQ):
        block = block_ref[owner, slot]
        mine = (slot < count_ref[owner]) & (block // BPC == place_ref[0])
        chosen = jnp.where(mine & (seen == rank), block % BPC, chosen)
        seen = seen + mine.astype(jnp.int32)
    return chosen


def pack_early_kernel(block_ref, count_ref, place_ref, x_ref, *out_refs):
    def write(out_ref):
        for hop in range(HOPS_DEV):
            rows = pl.ds(hop * NFINE, NFINE)
            out_ref[0, hop] = jnp.concatenate([x_ref[0, rows, :HALF], x_ref[1, rows, :HALF]], axis=1)

    for shift, out_ref in enumerate(out_refs):
        pl.when(pl.program_id(0) == shift)(lambda out_ref=out_ref: write(out_ref))


def pack_early(coarse, req_block, req_count, place):
    def out_map(own, d, r):
        return (jnp.where(d < own, 0, jnp.where(d > own, PAIR - 1, r)), 0, 0, 0)

    return pl.pallas_call(
        pack_early_kernel,
        out_shape=[jax.ShapeDtypeStruct((PAIR, HOPS_DEV, NFINE, BLOCKW), jnp.bfloat16)] * OWNERS,
        grid_spec=pltpu.PrefetchScalarGridSpec(
            num_scalar_prefetch=3,
            grid=(OWNERS, PAIR),
            in_specs=[
                pl.BlockSpec(
                    (2, HOPS_DEV * NFINE, BLOCKW),
                    lambda d, r, *refs: (0, 0, wanted_block(d, r, *refs)),
                ),
            ],
            out_specs=[
                pl.BlockSpec(
                    (1, HOPS_DEV, NFINE, BLOCKW), lambda d, r, *refs, own=own: out_map(own, d, r)
                )
                for own in range(OWNERS)
            ],
        ),
        name="pack_early",
    )(req_block, req_count, place, coarse)


def pack_late_kernel(block_ref, count_ref, place_ref, x0_ref, x1_ref, pick_ref, out_ref):
    wide = jnp.concatenate([x0_ref[0], x0_ref[1], x1_ref[0], x1_ref[1]], axis=1)
    turned = lax.dot_general(
        pick_ref[...], wide, (((1,), (1,)), ((), ())), preferred_element_type=jnp.float32
    )
    out_ref[:, 0, 0] = turned.reshape(TM, ROWS, NFINE).astype(jnp.bfloat16)


def pack_late(coarse, pick, req_block, req_count, place):
    def block_spec(rank):
        return pl.BlockSpec(
            (2, NFINE, BLOCKW), lambda d, h, *refs: (0, h, wanted_block(d, rank, *refs))
        )

    return pl.pallas_call(
        pack_late_kernel,
        out_shape=jax.ShapeDtypeStruct((TM, OWNERS, HOPS_DEV, ROWS, NFINE), jnp.bfloat16),
        grid_spec=pltpu.PrefetchScalarGridSpec(
            num_scalar_prefetch=3,
            grid=(OWNERS, HOPS_DEV),
            in_specs=[
                block_spec(0),
                block_spec(1),
                pl.BlockSpec((TM * ROWS, PAIR * 2 * BLOCKW), lambda d, h, *refs: (0, 0)),
            ],
            out_specs=pl.BlockSpec(
                (TM, 1, 1, ROWS, NFINE), lambda d, h, *refs: (0, d, h, 0, 0)
            ),
        ),
        name="pack_late",
    )(req_block, req_count, place, coarse, coarse, pick)


def arrival(slot, block_ref, place_ref):
    owner = place_ref[0]
    source = block_ref[owner, slot] // BPC
    rank = jnp.int32(0)
    for other in range(slot):
        rank = rank + (block_ref[owner, other] // BPC == source).astype(jnp.int32)
    return (owner - source + OWNERS) % OWNERS, jnp.minimum(rank, PAIR - 1)


def choose_kernel(block_ref, place_ref, a0, a1, a2, a3, pick_ref, out_ref, held_ref, sem):
    pair, hop = pl.program_id(0), pl.program_id(1)

    @pl.when((pair == 0) & (hop == 0))
    def _():
        for slot in range(MAXREQ):
            shift, rank = arrival(slot, block_ref, place_ref)
            for own, ref in enumerate((a0, a1, a2, a3)):

                @pl.when(shift == own)
                def _():
                    pltpu.make_async_copy(ref.at[rank], held_ref.at[slot], sem.at[slot]).start()

    @pl.when(hop == 0)
    def _():
        for slot in range(2):
            at = pair * 2 + slot
            pltpu.make_async_copy(a0.at[0], held_ref.at[at], sem.at[at]).wait()

    both = jnp.concatenate([held_ref[pair * 2, hop], held_ref[pair * 2 + 1, hop]], axis=1)
    turned = lax.dot_general(
        pick_ref[...], both, (((1,), (1,)), ((), ())), preferred_element_type=jnp.float32
    )
    out_ref[:, 0, 0] = turned.reshape(TM, ROWS, NFINE).astype(jnp.bfloat16)


def choose(arrived, pick, req_block, place):
    return pl.pallas_call(
        choose_kernel,
        out_shape=jax.ShapeDtypeStruct((TM, MAXREQ // 2, HOPS_DEV, ROWS, NFINE), jnp.bfloat16),
        grid_spec=pltpu.PrefetchScalarGridSpec(
            num_scalar_prefetch=2,
            grid=(MAXREQ // 2, HOPS_DEV),
            in_specs=[pl.BlockSpec(memory_space=pl.ANY)] * OWNERS
            + [pl.BlockSpec((TM * ROWS, 2 * BLOCKW), lambda p, h, *refs: (0, 0))],
            out_specs=pl.BlockSpec(
                (TM, 1, 1, ROWS, NFINE), lambda p, h, *refs: (0, p, h, 0, 0)
            ),
            scratch_shapes=[
                pltpu.VMEM((MAXREQ, HOPS_DEV, NFINE, BLOCKW), jnp.bfloat16),
                pltpu.SemaphoreType.DMA((MAXREQ,)),
            ],
        ),
        name="choose",
    )(req_block, place, *arrived, pick)


def turn(value, sign):
    return pltpu.roll(value, ROWS // 2, value.ndim - 2) * sign


def dft4(a, b, c, d, sign):
    s02, d02, s13, d13 = a + c, a - c, b + d, turn(b - d, sign)
    return s02 + s13, d02 + d13, s02 - s13, d02 - d13


def dft8(x, sign):
    half = math.sqrt(0.5)
    low = [x[i] + x[i + 4] for i in range(4)]
    high = [x[i] - x[i + 4] for i in range(4)]
    high[1] = (high[1] + turn(high[1], sign)) * half
    high[2] = turn(high[2], sign)
    high[3] = (turn(high[3], sign) - high[3]) * half
    even, odd = dft4(*low, sign), dft4(*high, sign)
    return [pair for both in zip(even, odd) for pair in both]


def transform(load, proto_ref, high_ref, low_ref, out_ref, wide_ref, fir_ref, split_ref):
    sign = jnp.where(lax.broadcasted_iota(jnp.int32, (ROWS, LANES), 0) < ROWS // 2, 1.0, -1.0)
    wide_ref[HOPS:, :, :] = jnp.zeros((FRAMES + TAPS - 1 - HOPS, ROWS, LANES), jnp.float32)
    def taps(tile, carry):
        lanes = pl.ds(pl.multiple_of(tile * LANES, LANES), LANES)
        wide_ref[:HOPS] = load(lanes)
        weights = [jnp.broadcast_to(proto_ref[tap, lanes].reshape(1, LANES), (ROWS, LANES)) for tap in range(TAPS)]

        def fir(step, inner):
            first = step * GROUP
            samples = wide_ref[pl.ds(first, GROUP + TAPS - 1)]
            total = samples[:GROUP] * weights[0]
            for tap in range(1, TAPS):
                total = total + samples[tap : tap + GROUP] * weights[tap]
            fir_ref[pl.ds(first, GROUP), :, lanes] = total
            return inner

        return lax.fori_loop(0, FRAMES // GROUP, fir, carry)

    lax.fori_loop(0, RADIX, taps, 0)

    def butterflies(step, carry):
        first = step * 2
        parts = [fir_ref[pl.ds(first, 2), :, tile * LANES : (tile + 1) * LANES] for tile in range(RADIX)]
        rows = pl.ds(pl.multiple_of(first * ROWS, 2 * ROWS), 2 * ROWS)
        for m1, value in enumerate(dft8(parts, sign)):
            value = value.reshape(2 * ROWS, LANES)
            high = value.astype(jnp.bfloat16)
            split_ref[m1, rows, :LANES] = high
            split_ref[m1, rows, LANES:] = (value - high.astype(jnp.float32)).astype(jnp.bfloat16)
        return carry

    lax.fori_loop(0, FRAMES // 2, butterflies, 0)
    for m1 in range(RADIX):
        both = split_ref[m1]
        high = high_ref[m1]
        product = jnp.dot(both, jnp.concatenate([high, high], axis=0), preferred_element_type=jnp.float32)
        product = product + jnp.dot(both[:, :LANES], low_ref[m1], preferred_element_type=jnp.float32)
        cosines = product[:, :LANES].reshape(FRAMES, ROWS, LANES)
        sines = product[:, LANES:].reshape(FRAMES, ROWS, LANES)
        result = (cosines + turn(sines, sign)).astype(jnp.bfloat16)
        out_ref[: FRAMES // HOPS_DEV, :, 0, :, m1 * LANES : (m1 + 1) * LANES] = result.reshape(
            FRAMES // HOPS_DEV, HOPS_DEV, ROWS, LANES
        )


def early_kernel(x_ref, *refs):
    def load(lanes):
        return x_ref[:, 0, :, :, lanes].astype(jnp.float32).reshape(HOPS, ROWS, LANES)

    transform(load, *refs)


def late_kernel(block_ref, place_ref, a0, a1, a2, a3, proto_ref, high_ref, low_ref, out_ref, wide_ref, fir_ref, split_ref, held_ref, sem):
    pair = pl.program_id(0)

    @pl.when(pair == 0)
    def _():
        for slot in range(MAXREQ):
            shift, _ = arrival(slot, block_ref, place_ref)
            for own, ref in enumerate((a0.at[:, 0], a1, a2, a3)):

                @pl.when(shift == own)
                def _():
                    pltpu.make_async_copy(ref, held_ref.at[slot], sem.at[slot]).start()

    for slot in range(2):
        at = pair * 2 + slot
        pltpu.make_async_copy(a1, held_ref.at[at], sem.at[at]).wait()

    ranks = [arrival(slot, block_ref, place_ref)[1] for slot in range(MAXREQ)]
    first_rank = jnp.where(pair == 0, ranks[0], ranks[2])
    second_rank = jnp.where(pair == 0, ranks[1], ranks[3])
    is_second = (lax.broadcasted_iota(jnp.int32, (HOPS, ROWS, LANES), 1) // SHARE) % 2 == 1

    def load(lanes):
        first = held_ref[pair * 2, :, :, :, lanes].astype(jnp.float32).reshape(HOPS, ROWS, LANES)
        second = held_ref[pair * 2 + 1, :, :, :, lanes].astype(jnp.float32).reshape(HOPS, ROWS, LANES)
        first = jnp.where(first_rank == 0, first, pltpu.roll(first, ROWS - SHARE, 1))
        second = jnp.where(second_rank == 1, second, pltpu.roll(second, SHARE, 1))
        return jnp.where(is_second, second, first)

    transform(load, proto_ref, high_ref, low_ref, out_ref, wide_ref, fir_ref, split_ref)


def table_specs():
    return [
        pl.BlockSpec((TAPS, NFINE), lambda p, *refs: (0, 0)),
        pl.BlockSpec((RADIX, LANES, 2 * LANES), lambda p, *refs: (0, 0, 0)),
        pl.BlockSpec((RADIX, LANES, 2 * LANES), lambda p, *refs: (0, 0, 0)),
    ]


COST = pl.CostEstimate(flops=18_000_000_000, transcendentals=0, bytes_accessed=2 * MAXREQ * HOPS * 4 * NFINE * 2)
RESULT = jax.ShapeDtypeStruct((TM, HOPS_DEV, MAXREQ // 2, ROWS, NFINE), jnp.bfloat16)


def result_spec():
    return pl.BlockSpec((TM, HOPS_DEV, 1, ROWS, NFINE), lambda p, *refs: (0, 0, p, 0, 0))


def work_space():
    return [
        pltpu.VMEM((FRAMES + TAPS - 1, ROWS, LANES), jnp.float32),
        pltpu.VMEM((FRAMES, ROWS, NFINE), jnp.float32),
        pltpu.VMEM((RADIX, FRAMES * ROWS, 2 * LANES), jnp.bfloat16),
    ]


def filter_early(gathered, tables):
    return pl.pallas_call(
        early_kernel,
        out_shape=RESULT,
        grid=(MAXREQ // 2,),
        in_specs=[
            pl.BlockSpec((TM, 1, HOPS_DEV, ROWS, NFINE), lambda p: (0, p, 0, 0, 0)),
            *table_specs(),
        ],
        out_specs=result_spec(),
        scratch_shapes=work_space(),
        cost_estimate=COST,
        name="filter_early",
    )(gathered, *tables)


def filter_late(arrived, tables, req_block, place):
    return pl.pallas_call(
        late_kernel,
        out_shape=RESULT,
        grid_spec=pltpu.PrefetchScalarGridSpec(
            num_scalar_prefetch=2,
            grid=(MAXREQ // 2,),
            in_specs=[pl.BlockSpec(memory_space=pl.ANY)] * OWNERS + table_specs(),
            out_specs=result_spec(),
            scratch_shapes=work_space()
            + [
                pltpu.VMEM((MAXREQ, TM, HOPS_DEV, ROWS, NFINE), jnp.bfloat16),
                pltpu.SemaphoreType.DMA((MAXREQ,)),
            ],
        ),
        cost_estimate=COST,
        name="filter_late",
    )(req_block, place, *arrived, *tables)


def final_pick(slot):
    shape = (2 * TM * ROWS, 2 * BLOCKW)
    row, column = (lax.broadcasted_iota(jnp.int32, shape, dim) for dim in range(2))
    place = (row // ROWS) * SHARE + row % SHARE + BLOCKW * ((row // 4) % 2)
    return jnp.where((place == column) & ((row // 2) % 2 == slot), 1.0, 0.0).astype(jnp.bfloat16)


def unpack_kernel(start_ref, frames_ref, count_ref, place_ref, early_ref, late_ref, out_ref, turned_ref, pick_ref):
    slot = pl.program_id(1)

    @pl.when((slot == 0) & (pl.program_id(0) == 0))
    def _():
        for which in range(2):
            pick_ref[which] = final_pick(which)

    owner = place_ref[0]
    hop = place_ref[1] * HOPS_DEV + pl.program_id(0)
    begin = start_ref[owner, slot]
    active = (slot < count_ref[owner]) & (hop >= begin) & (hop < begin + frames_ref[owner, slot])

    @pl.when(active)
    def _():
        rows = jnp.concatenate([early_ref[:, 0, 0], late_ref[:, 0, 0]], axis=0)
        rows = rows.astype(jnp.float32).reshape(2 * TM * ROWS, NFINE).astype(jnp.bfloat16)
        columns = lax.dot_general(
            rows, pick_ref[slot % 2], (((0,), (0,)), ((), ())), preferred_element_type=jnp.float32
        )
        for m1 in range(RADIX):
            for part in range(2):
                turned_ref[part, pl.ds(m1, LANES, stride=RADIX), :] = columns[
                    m1 * LANES : (m1 + 1) * LANES, part * BLOCKW : (part + 1) * BLOCKW
                ]
        out_ref[0, 0, 0] = turned_ref[...].astype(jnp.bfloat16)

    @pl.when(jnp.logical_not(active))
    def _():
        out_ref[...] = jnp.zeros_like(out_ref)


def unpack(early, late, req_start, req_frames, req_count, place):
    back_spec = pl.BlockSpec((TM, 1, 1, ROWS, NFINE), lambda h, q, *refs: (0, h, q // 2, 0, 0))
    return pl.pallas_call(
        unpack_kernel,
        out_shape=jax.ShapeDtypeStruct((HOPS_DEV, 1, MAXREQ, 2, NFINE, BLOCKW), jnp.bfloat16),
        grid_spec=pltpu.PrefetchScalarGridSpec(
            num_scalar_prefetch=4,
            grid=(HOPS_DEV, MAXREQ),
            in_specs=[
                back_spec,
                back_spec,
            ],
            out_specs=pl.BlockSpec(
                (1, 1, 1, 2, NFINE, BLOCKW), lambda h, q, *refs: (h, 0, q, 0, 0, 0)
            ),
            scratch_shapes=[
                pltpu.VMEM((2, NFINE, BLOCKW), jnp.float32),
                pltpu.VMEM((2, 2 * TM * ROWS, 2 * BLOCKW), jnp.bfloat16),
            ],
        ),
        name="unpack",
    )(req_start, req_frames, req_count, place, early, late)


def over_tm(array):
    return lax.all_to_all(array, "tm", split_axis=0, concat_axis=0, tiled=True)


def along_chan(arrays):
    return [arrays[0]] + [
        lax.ppermute(arrays[d], "chan", [(s, (s + d) % OWNERS) for s in range(OWNERS)])
        for d in range(1, OWNERS)
    ]


def shards(coarse, prototype, req_block, req_start, req_frames, req_count):
    column = lax.axis_index("chan").astype(jnp.int32)
    place = jnp.stack([column, lax.axis_index("tm").astype(jnp.int32)])
    tables = (prototype, *(jnp.asarray(table) for table in dft_tables()))
    late = pack_late(coarse, jnp.asarray(late_pick()), req_block, req_count, place)
    early = pack_early(coarse, req_block, req_count, place)
    late = over_tm(late)
    early = choose(along_chan(early), jnp.asarray(early_pick()), req_block, place)
    late, early = lax.optimization_barrier((late, early))
    early = over_tm(early)
    late = along_chan([late] + [late[:, d] for d in range(1, OWNERS)])
    early = filter_early(early, tables)
    _, *late = lax.optimization_barrier((early, *late))
    early, late = lax.optimization_barrier((over_tm(early), filter_late(late, tables, req_block, place)))
    late = over_tm(late)
    return unpack(early, late, req_start, req_frames, req_count, place)


def solution(mesh):
    return jax.shard_map(
        shards,
        mesh=mesh,
        in_specs=(P(None, "tm", "chan"), P(), P(), P(), P(), P()),
        out_specs=P("tm", "chan", None, None, None, None),
        check_vma=False,
    )
```

```python
import math

import jax
import jax.numpy as jnp
import ml_dtypes
import numpy as np
from jax import lax
from jax.experimental import pallas as pl
from jax.experimental.pallas import tpu as pltpu
from jax.sharding import PartitionSpec as P

BLOCKW = 128
NFINE = 1024
TAPS = 16
HOPS_DEV = 3
MAXREQ = 4
PAIR = 2
TM = 32
OWNERS = 4
BPC = 8
HOPS = 96
HALF = BLOCKW // 2
SHARE = HALF // TM
ROWS = 8
RADIX = 8
LANES = 128
FRAMES = 84
GROUP = 21


def late_pick():
    pick = np.zeros((TM, 2, PAIR, SHARE, PAIR, 2, BLOCKW), np.float32)
    for device, part, rank, column in np.ndindex(TM, 2, PAIR, SHARE):
        pick[device, part, rank, column, rank, part, HALF + device * SHARE + column] = 1
    return pick.reshape(TM * ROWS, PAIR * 2 * BLOCKW).astype(ml_dtypes.bfloat16)


def early_pick():
    pick = np.zeros((TM, 2, 2, SHARE, 2, 2, HALF), np.float32)
    for device, part, slot, column in np.ndindex(TM, 2, 2, SHARE):
        pick[device, part, slot, column, slot, part, device * SHARE + column] = 1
    return pick.reshape(TM * ROWS, 2 * BLOCKW).astype(ml_dtypes.bfloat16)


def dft_tables():
    k2 = np.arange(LANES)[None, :, None]
    m = np.arange(RADIX)[:, None, None] + RADIX * np.arange(LANES)[None, None, :]
    angles = (k2 * m % NFINE) * (2.0 * math.pi / NFINE)
    table = np.concatenate([np.cos(angles), np.sin(angles)], axis=2) / math.sqrt(NFINE)
    high = table.astype(np.float32).astype(ml_dtypes.bfloat16)
    low = (table - high.astype(np.float64)).astype(np.float32).astype(ml_dtypes.bfloat16)
    return high, low


def wanted_block(shift, rank, block_ref, count_ref, place_ref):
    owner = (place_ref[0] + shift) % OWNERS
    seen = jnp.int32(0)
    chosen = jnp.int32(0)
    for slot in range(MAXREQ):
        block = block_ref[owner, slot]
        mine = (slot < count_ref[owner]) & (block // BPC == place_ref[0])
        chosen = jnp.where(mine & (seen == rank), block % BPC, chosen)
        seen = seen + mine.astype(jnp.int32)
    return seen > rank, chosen


def pack_kernel(block_ref, count_ref, place_ref, x_ref, pick_ref, *refs):
    late_ref, *early_refs = refs[: 1 + OWNERS]
    block_buf, late_buf, early_buf, block_sem, late_sem, early_sem = refs[1 + OWNERS :]
    wanted = [[wanted_block(d, r, block_ref, count_ref, place_ref) for r in range(PAIR)] for d in range(OWNERS)]

    def block_copy(d, r):
        columns = pl.ds(pl.multiple_of(wanted[d][r][1] * BLOCKW, BLOCKW), BLOCKW)
        return pltpu.make_async_copy(x_ref.at[:, :, columns], block_buf.at[d, r], block_sem.at[d, r])

    def late_copy(d):
        return pltpu.make_async_copy(late_buf.at[d], late_ref.at[:, d], late_sem.at[d])

    def early_copy(d, r):
        return pltpu.make_async_copy(early_buf.at[d, r], early_refs[d].at[r], early_sem.at[d, r])

    order = [(d, r) for d in (1, 2, 3, 0) for r in range(PAIR)]
    for d, r in order:
        pl.when(wanted[d][r][0])(lambda d=d, r=r: block_copy(d, r).start())
    for d, r in order:
        if r == 0:
            pl.when(wanted[d][0][0])(lambda d=d: block_copy(d, 0).wait())
            continue

        @pl.when(wanted[d][0][0] & jnp.logical_not(wanted[d][1][0]))
        def _():
            block_buf[d, 1] = jnp.zeros((2, HOPS_DEV * NFINE, BLOCKW), jnp.bfloat16)

        pl.when(wanted[d][1][0])(lambda d=d: block_copy(d, 1).wait())
        for rank in range(PAIR):

            @pl.when(wanted[d][rank][0])
            def _():
                early_buf[d, rank] = jnp.concatenate(
                    [block_buf[d, rank, 0, :, :HALF], block_buf[d, rank, 1, :, :HALF]], axis=1
                ).reshape(HOPS_DEV, NFINE, BLOCKW)
                early_copy(d, rank).start()

        @pl.when(wanted[d][0][0])
        def _():
            def one_hop(hop, carry):
                rows = pl.ds(pl.multiple_of(hop * NFINE, NFINE), NFINE)
                wide = jnp.concatenate([block_buf[d, i // 2, i % 2, rows] for i in range(2 * PAIR)], axis=1)
                turned = lax.dot_general(
                    pick_ref[...], wide, (((1,), (1,)), ((), ())), preferred_element_type=jnp.float32
                )
                late_buf[d, :, hop] = turned.reshape(TM, ROWS, NFINE).astype(jnp.bfloat16)
                return carry

            lax.fori_loop(0, HOPS_DEV, one_hop, 0)
            late_copy(d).start()

    for d, r in order:
        pl.when(wanted[d][r][0])(lambda d=d, r=r: early_copy(d, r).wait())
        if r == 0:
            pl.when(wanted[d][0][0])(lambda d=d: late_copy(d).wait())


def pack(coarse, pick, req_block, req_count, place):
    anywhere = pl.BlockSpec(memory_space=pl.ANY)
    early = jax.ShapeDtypeStruct((PAIR, HOPS_DEV, NFINE, BLOCKW), jnp.bfloat16)
    return pl.pallas_call(
        pack_kernel,
        out_shape=[jax.ShapeDtypeStruct((TM, OWNERS, HOPS_DEV, ROWS, NFINE), jnp.bfloat16)] + [early] * OWNERS,
        grid_spec=pltpu.PrefetchScalarGridSpec(
            num_scalar_prefetch=3,
            grid=(1,),
            in_specs=[anywhere, pl.BlockSpec((TM * ROWS, PAIR * 2 * BLOCKW), lambda i, *refs: (0, 0))],
            out_specs=[anywhere] * (1 + OWNERS),
            scratch_shapes=[
                pltpu.VMEM((OWNERS, PAIR, 2, HOPS_DEV * NFINE, BLOCKW), jnp.bfloat16),
                pltpu.VMEM((OWNERS, TM, HOPS_DEV, ROWS, NFINE), jnp.bfloat16),
                pltpu.VMEM((OWNERS, PAIR, HOPS_DEV, NFINE, BLOCKW), jnp.bfloat16),
                pltpu.SemaphoreType.DMA((OWNERS, PAIR)),
                pltpu.SemaphoreType.DMA((OWNERS,)),
                pltpu.SemaphoreType.DMA((OWNERS, PAIR)),
            ],
        ),
        name="pack",
    )(req_block, req_count, place, coarse, pick)


def arrival(slot, block_ref, count_ref, place_ref):
    owner = place_ref[0]
    slot = jnp.where(slot < count_ref[owner], slot, 0)
    source = block_ref[owner, slot] // BPC
    rank = jnp.int32(0)
    for other in range(MAXREQ - 1):
        same = (other < slot) & (block_ref[owner, other] // BPC == source)
        rank = rank + same.astype(jnp.int32)
    return (owner - source + OWNERS) % OWNERS, jnp.minimum(rank, PAIR - 1)


def choose_kernel(block_ref, count_ref, place_ref, a0, a1, a2, a3, pick_ref, out_ref, held_ref, out_buf, held_sem, out_sem):
    for slot in range(MAXREQ):
        shift, rank = arrival(slot, block_ref, count_ref, place_ref)
        for own, ref in enumerate((a0, a1, a2, a3)):

            @pl.when(shift == own)
            def _():
                pltpu.make_async_copy(ref.at[rank], held_ref.at[slot], held_sem.at[slot]).start()

    def out_copy(pair, hop):
        return pltpu.make_async_copy(out_buf.at[pair, hop], out_ref.at[:, pair, hop], out_sem.at[pair, hop])

    for pair in range(MAXREQ // 2):
        for slot in (2 * pair, 2 * pair + 1):
            pltpu.make_async_copy(a0.at[0], held_ref.at[slot], held_sem.at[slot]).wait()
        for hop in range(HOPS_DEV):
            both = jnp.concatenate([held_ref[pair * 2, hop], held_ref[pair * 2 + 1, hop]], axis=1)
            turned = lax.dot_general(
                pick_ref[...], both, (((1,), (1,)), ((), ())), preferred_element_type=jnp.float32
            )
            out_buf[pair, hop] = turned.reshape(TM, ROWS, NFINE).astype(jnp.bfloat16)
            out_copy(pair, hop).start()
    for pair in range(MAXREQ // 2):
        for hop in range(HOPS_DEV):
            out_copy(pair, hop).wait()


def choose(arrived, pick, req_block, req_count, place):
    anywhere = pl.BlockSpec(memory_space=pl.ANY)
    return pl.pallas_call(
        choose_kernel,
        out_shape=jax.ShapeDtypeStruct((TM, MAXREQ // 2, HOPS_DEV, ROWS, NFINE), jnp.bfloat16),
        grid_spec=pltpu.PrefetchScalarGridSpec(
            num_scalar_prefetch=3,
            grid=(1,),
            in_specs=[anywhere] * OWNERS + [pl.BlockSpec((TM * ROWS, 2 * BLOCKW), lambda i, *refs: (0, 0))],
            out_specs=anywhere,
            scratch_shapes=[
                pltpu.VMEM((MAXREQ, HOPS_DEV, NFINE, BLOCKW), jnp.bfloat16),
                pltpu.VMEM((MAXREQ // 2, HOPS_DEV, TM, ROWS, NFINE), jnp.bfloat16),
                pltpu.SemaphoreType.DMA((MAXREQ,)),
                pltpu.SemaphoreType.DMA((MAXREQ // 2, HOPS_DEV)),
            ],
        ),
        name="choose",
    )(req_block, req_count, place, *arrived, pick)


def turn(value, sign):
    return pltpu.roll(value, ROWS // 2, value.ndim - 2) * sign


def dft4(a, b, c, d, sign):
    s02, d02, s13, d13 = a + c, a - c, b + d, turn(b - d, sign)
    return s02 + s13, d02 + d13, s02 - s13, d02 - d13


def dft8(x, sign):
    half = math.sqrt(0.5)
    low = [x[i] + x[i + 4] for i in range(4)]
    high = [x[i] - x[i + 4] for i in range(4)]
    high[1] = (high[1] + turn(high[1], sign)) * half
    high[2] = turn(high[2], sign)
    high[3] = (turn(high[3], sign) - high[3]) * half
    even, odd = dft4(*low, sign), dft4(*high, sign)
    return [pair for both in zip(even, odd) for pair in both]


def transform(load, proto_ref, high_ref, low_ref, out_ref, wide_ref, fir_ref, split_ref):
    sign = jnp.where(lax.broadcasted_iota(jnp.int32, (ROWS, LANES), 0) < ROWS // 2, 1.0, -1.0)
    wide_ref[HOPS:, :, :] = jnp.zeros((FRAMES + TAPS - 1 - HOPS, ROWS, LANES), jnp.float32)
    def taps(tile, carry):
        lanes = pl.ds(pl.multiple_of(tile * LANES, LANES), LANES)
        wide_ref[:HOPS] = load(lanes)
        weights = [jnp.broadcast_to(proto_ref[tap, lanes].reshape(1, LANES), (ROWS, LANES)) for tap in range(TAPS)]

        def fir(step, inner):
            first = step * GROUP
            samples = wide_ref[pl.ds(first, GROUP + TAPS - 1)]
            total = samples[:GROUP] * weights[0]
            for tap in range(1, TAPS):
                total = total + samples[tap : tap + GROUP] * weights[tap]
            fir_ref[pl.ds(first, GROUP), :, lanes] = total
            return inner

        return lax.fori_loop(0, FRAMES // GROUP, fir, carry)

    lax.fori_loop(0, RADIX, taps, 0)

    def butterflies(step, carry):
        first = step * 2
        parts = [fir_ref[pl.ds(first, 2), :, tile * LANES : (tile + 1) * LANES] for tile in range(RADIX)]
        rows = pl.ds(pl.multiple_of(first * ROWS, 2 * ROWS), 2 * ROWS)
        for m1, value in enumerate(dft8(parts, sign)):
            value = value.reshape(2 * ROWS, LANES)
            high = value.astype(jnp.bfloat16)
            split_ref[m1, rows, :LANES] = high
            split_ref[m1, rows, LANES : 2 * LANES] = (value - high.astype(jnp.float32)).astype(jnp.bfloat16)
            split_ref[m1, rows, 2 * LANES :] = high
        return carry

    lax.fori_loop(0, FRAMES // 2, butterflies, 0)
    for m1 in range(RADIX):
        high = high_ref[m1]
        product = jnp.dot(
            split_ref[m1], jnp.concatenate([high, high, low_ref[m1]], axis=0), preferred_element_type=jnp.float32
        )
        cosines = product[:, :LANES].reshape(FRAMES, ROWS, LANES)
        sines = product[:, LANES:].reshape(FRAMES, ROWS, LANES)
        result = (cosines + turn(sines, sign)).astype(jnp.bfloat16)
        out_ref[: FRAMES // HOPS_DEV, :, 0, :, m1 * LANES : (m1 + 1) * LANES] = result.reshape(
            FRAMES // HOPS_DEV, HOPS_DEV, ROWS, LANES
        )


def early_kernel(x_ref, *refs):
    def load(lanes):
        return x_ref[:, 0, :, :, lanes].astype(jnp.float32).reshape(HOPS, ROWS, LANES)

    transform(load, *refs)


def late_kernel(block_ref, count_ref, place_ref, a0, a1, a2, a3, proto_ref, high_ref, low_ref, out_ref, wide_ref, fir_ref, split_ref, held_ref, sem):
    pair = pl.program_id(0)

    @pl.when(pair == 0)
    def _():
        for slot in range(MAXREQ):
            shift, _ = arrival(slot, block_ref, count_ref, place_ref)
            for own, ref in enumerate((a0.at[:, 0], a1, a2, a3)):

                @pl.when(shift == own)
                def _():
                    pltpu.make_async_copy(ref, held_ref.at[slot], sem.at[slot]).start()

    for slot in range(2):
        at = pair * 2 + slot
        pltpu.make_async_copy(a1, held_ref.at[at], sem.at[at]).wait()

    ranks = [arrival(slot, block_ref, count_ref, place_ref)[1] for slot in range(MAXREQ)]
    first_rank = jnp.where(pair == 0, ranks[0], ranks[2])
    second_rank = jnp.where(pair == 0, ranks[1], ranks[3])
    is_second = (lax.broadcasted_iota(jnp.int32, (HOPS, ROWS, LANES), 1) // SHARE) % 2 == 1

    def load(lanes):
        first = held_ref[pair * 2, :, :, :, lanes].astype(jnp.float32).reshape(HOPS, ROWS, LANES)
        second = held_ref[pair * 2 + 1, :, :, :, lanes].astype(jnp.float32).reshape(HOPS, ROWS, LANES)
        first = jnp.where(first_rank == 0, first, pltpu.roll(first, ROWS - SHARE, 1))
        second = jnp.where(second_rank == 1, second, pltpu.roll(second, SHARE, 1))
        return jnp.where(is_second, second, first)

    transform(load, proto_ref, high_ref, low_ref, out_ref, wide_ref, fir_ref, split_ref)


def table_specs():
    return [
        pl.BlockSpec((TAPS, NFINE), lambda p, *refs: (0, 0)),
        pl.BlockSpec((RADIX, LANES, 2 * LANES), lambda p, *refs: (0, 0, 0)),
        pl.BlockSpec((RADIX, LANES, 2 * LANES), lambda p, *refs: (0, 0, 0)),
    ]


COST = pl.CostEstimate(flops=18_000_000_000, transcendentals=0, bytes_accessed=2 * MAXREQ * HOPS * 4 * NFINE * 2)
RESULT = jax.ShapeDtypeStruct((TM, HOPS_DEV, MAXREQ // 2, ROWS, NFINE), jnp.bfloat16)


def result_spec():
    return pl.BlockSpec((TM, HOPS_DEV, 1, ROWS, NFINE), lambda p, *refs: (0, 0, p, 0, 0))


def work_space():
    return [
        pltpu.VMEM((FRAMES + TAPS - 1, ROWS, LANES), jnp.float32),
        pltpu.VMEM((FRAMES, ROWS, NFINE), jnp.float32),
        pltpu.VMEM((RADIX, FRAMES * ROWS, 3 * LANES), jnp.bfloat16),
    ]


def filter_early(gathered, tables):
    return pl.pallas_call(
        early_kernel,
        out_shape=RESULT,
        grid=(MAXREQ // 2,),
        in_specs=[
            pl.BlockSpec((TM, 1, HOPS_DEV, ROWS, NFINE), lambda p: (0, p, 0, 0, 0)),
            *table_specs(),
        ],
        out_specs=result_spec(),
        scratch_shapes=work_space(),
        cost_estimate=COST,
        name="filter_early",
    )(gathered, *tables)


def filter_late(arrived, tables, req_block, req_count, place):
    return pl.pallas_call(
        late_kernel,
        out_shape=RESULT,
        grid_spec=pltpu.PrefetchScalarGridSpec(
            num_scalar_prefetch=3,
            grid=(MAXREQ // 2,),
            in_specs=[pl.BlockSpec(memory_space=pl.ANY)] * OWNERS + table_specs(),
            out_specs=result_spec(),
            scratch_shapes=work_space()
            + [
                pltpu.VMEM((MAXREQ, TM, HOPS_DEV, ROWS, NFINE), jnp.bfloat16),
                pltpu.SemaphoreType.DMA((MAXREQ,)),
            ],
        ),
        cost_estimate=COST,
        name="filter_late",
    )(req_block, req_count, place, *arrived, *tables)


def final_pick(slot):
    shape = (2 * TM * ROWS, 2 * BLOCKW)
    row, column = (lax.broadcasted_iota(jnp.int32, shape, dim) for dim in range(2))
    place = (row // ROWS) * SHARE + row % SHARE + BLOCKW * ((row // 4) % 2)
    return jnp.where((place == column) & ((row // 2) % 2 == slot), 1.0, 0.0).astype(jnp.bfloat16)


def unpack_kernel(start_ref, frames_ref, count_ref, place_ref, early_ref, late_ref, out_ref, back_buf, rows_ref, turned_ref, pick_ref, sem):
    owner = place_ref[0]
    step = pl.program_id(0)

    def is_active(hop, slot):
        frame = place_ref[1] * HOPS_DEV + hop
        begin = start_ref[owner, slot]
        return (slot < count_ref[owner]) & (frame >= begin) & (frame < begin + frames_ref[owner, slot])

    def back_copies(hop, pair):
        at = hop * (MAXREQ // 2) + pair
        return [
            pltpu.make_async_copy(ref.at[:, hop, pair], back_buf.at[at, half], sem.at[at, half])
            for half, ref in enumerate((early_ref, late_ref))
        ]

    @pl.when(step == 0)
    def _():
        for hop in range(HOPS_DEV):
            for pair in range(MAXREQ // 2):

                @pl.when(is_active(hop, 2 * pair) | is_active(hop, 2 * pair + 1))
                def _():
                    for copy in back_copies(hop, pair):
                        copy.start()

        for which in range(2):
            pick_ref[which] = final_pick(which)

    hop, pair = step // (MAXREQ // 2), step % (MAXREQ // 2)
    active = [is_active(hop, 2 * pair + which) for which in range(2)]

    @pl.when(active[0] | active[1])
    def _():
        for copy in back_copies(hop, pair):
            copy.wait()
        rows_ref[...] = back_buf[step].astype(jnp.float32).reshape(2 * TM * ROWS, NFINE).astype(jnp.bfloat16)

    for which in range(2):

        @pl.when(active[which])
        def _():
            columns = lax.dot_general(
                rows_ref[...], pick_ref[which], (((0,), (0,)), ((), ())), preferred_element_type=jnp.float32
            )
            for m1 in range(RADIX):
                for part in range(2):
                    turned_ref[part, pl.ds(m1, LANES, stride=RADIX), :] = columns[
                        m1 * LANES : (m1 + 1) * LANES, part * BLOCKW : (part + 1) * BLOCKW
                    ]
            out_ref[0, 0, which] = turned_ref[...].astype(jnp.bfloat16)

        @pl.when(jnp.logical_not(active[which]))
        def _():
            out_ref[0, 0, which] = jnp.zeros((2, NFINE, BLOCKW), jnp.bfloat16)


def unpack(early, late, req_start, req_frames, req_count, place):
    anywhere = pl.BlockSpec(memory_space=pl.ANY)
    steps = HOPS_DEV * MAXREQ // 2
    return pl.pallas_call(
        unpack_kernel,
        out_shape=jax.ShapeDtypeStruct((HOPS_DEV, 1, MAXREQ, 2, NFINE, BLOCKW), jnp.bfloat16),
        grid_spec=pltpu.PrefetchScalarGridSpec(
            num_scalar_prefetch=4,
            grid=(steps,),
            in_specs=[anywhere, anywhere],
            out_specs=pl.BlockSpec(
                (1, 1, 2, 2, NFINE, BLOCKW),
                lambda i, *refs: (i // (MAXREQ // 2), 0, i % (MAXREQ // 2), 0, 0, 0),
            ),
            scratch_shapes=[
                pltpu.VMEM((steps, 2, TM, ROWS, NFINE), jnp.bfloat16),
                pltpu.VMEM((2 * TM * ROWS, NFINE), jnp.bfloat16),
                pltpu.VMEM((2, NFINE, BLOCKW), jnp.float32),
                pltpu.VMEM((2, 2 * TM * ROWS, 2 * BLOCKW), jnp.bfloat16),
                pltpu.SemaphoreType.DMA((steps, 2)),
            ],
        ),
        name="unpack",
    )(req_start, req_frames, req_count, place, early, late)


def over_tm(array):
    return lax.all_to_all(array, "tm", split_axis=0, concat_axis=0, tiled=True)


def along_chan(arrays):
    return [arrays[0]] + [
        lax.ppermute(arrays[d], "chan", [(s, (s + d) % OWNERS) for s in range(OWNERS)])
        for d in range(1, OWNERS)
    ]


def shards(coarse, prototype, req_block, req_start, req_frames, req_count):
    column = lax.axis_index("chan").astype(jnp.int32)
    place = jnp.stack([column, lax.axis_index("tm").astype(jnp.int32)])
    tables = (prototype, *(jnp.asarray(table) for table in dft_tables()))
    late, *early = pack(coarse, jnp.asarray(late_pick()), req_block, req_count, place)
    late = over_tm(late)
    early = choose(along_chan(early), jnp.asarray(early_pick()), req_block, req_count, place)
    late, early = lax.optimization_barrier((late, early))
    early = over_tm(early)
    late = along_chan([late] + [late[:, d] for d in range(1, OWNERS)])
    early = filter_early(early, tables)
    _, *late = lax.optimization_barrier((early, *late))
    early, late = lax.optimization_barrier((over_tm(early), filter_late(late, tables, req_block, req_count, place)))
    late = over_tm(late)
    return unpack(early, late, req_start, req_frames, req_count, place)


def solution(mesh):
    return jax.shard_map(
        shards,
        mesh=mesh,
        in_specs=(P(None, "tm", "chan"), P(), P(), P(), P(), P()),
        out_specs=P("tm", "chan", None, None, None, None),
        check_vma=False,
    )
```

```python
import math

import jax
import jax.numpy as jnp
import ml_dtypes
import numpy as np
from jax import lax
from jax.experimental import pallas as pl
from jax.experimental.pallas import tpu as pltpu
from jax.sharding import PartitionSpec as P

BLOCKW = 128
NFINE = 1024
TAPS = 16
HOPS_DEV = 3
MAXREQ = 4
PAIR = 2
TM = 32
OWNERS = 4
BPC = 8
HOPS = 96
HALF = BLOCKW // 2
SHARE = HALF // TM
ROWS = 8
RADIX = 8
LANES = 128
FRAMES = 84
GROUP = 21
COST = pl.CostEstimate(flops=18_000_000_000, transcendentals=0, bytes_accessed=2 * MAXREQ * HOPS * 4 * NFINE * 2)


def late_pick():
    pick = np.zeros((TM, 2, PAIR, SHARE, PAIR, 2, BLOCKW), np.float32)
    for device, part, rank, column in np.ndindex(TM, 2, PAIR, SHARE):
        pick[device, part, rank, column, rank, part, HALF + device * SHARE + column] = 1
    return pick.reshape(TM * ROWS, PAIR * 2 * BLOCKW).astype(ml_dtypes.bfloat16)


def early_pick():
    pick = np.zeros((TM, 2, 2, SHARE, 2, 2, HALF), np.float32)
    for device, part, slot, column in np.ndindex(TM, 2, 2, SHARE):
        pick[device, part, slot, column, slot, part, device * SHARE + column] = 1
    return pick.reshape(TM * ROWS, 2 * BLOCKW).astype(ml_dtypes.bfloat16)


def dft_tables():
    k2 = np.arange(LANES)[None, :, None]
    m = np.arange(RADIX)[:, None, None] + RADIX * np.arange(LANES)[None, None, :]
    angles = (k2 * m % NFINE) * (2.0 * math.pi / NFINE)
    table = np.concatenate([np.cos(angles), np.sin(angles)], axis=2) / math.sqrt(NFINE)
    high = table.astype(np.float32).astype(ml_dtypes.bfloat16)
    low = (table - high.astype(np.float64)).astype(np.float32).astype(ml_dtypes.bfloat16)
    return high, low


def wanted_block(shift, rank, block_ref, count_ref, place_ref):
    owner = (place_ref[0] + shift) % OWNERS
    seen = jnp.int32(0)
    chosen = jnp.int32(0)
    for slot in range(MAXREQ):
        block = block_ref[owner, slot]
        mine = (slot < count_ref[owner]) & (block // BPC == place_ref[0])
        chosen = jnp.where(mine & (seen == rank), block % BPC, chosen)
        seen = seen + mine.astype(jnp.int32)
    return seen > rank, chosen


def pack_kernel(block_ref, count_ref, place_ref, x_ref, pick_ref, *refs):
    late_ref, *early_refs = refs[: 1 + OWNERS]
    block_buf, late_buf, early_buf, block_sem, late_sem, early_sem = refs[1 + OWNERS :]
    wanted = [[wanted_block(d, r, block_ref, count_ref, place_ref) for r in range(PAIR)] for d in range(OWNERS)]

    def block_copy(d, r):
        columns = pl.ds(pl.multiple_of(wanted[d][r][1] * BLOCKW, BLOCKW), BLOCKW)
        return pltpu.make_async_copy(x_ref.at[:, :, columns], block_buf.at[d, r], block_sem.at[d, r])

    def late_copy(d):
        return pltpu.make_async_copy(late_buf.at[d], late_ref.at[:, d], late_sem.at[d])

    def early_copy(d, r):
        return pltpu.make_async_copy(early_buf.at[d, r], early_refs[d].at[r], early_sem.at[d, r])

    order = [(d, r) for d in (1, 2, 3, 0) for r in range(PAIR)]
    for d, r in order:
        pl.when(wanted[d][r][0])(lambda d=d, r=r: block_copy(d, r).start())
    for d, r in order:
        if r == 0:
            pl.when(wanted[d][0][0])(lambda d=d: block_copy(d, 0).wait())
            continue

        @pl.when(wanted[d][0][0] & jnp.logical_not(wanted[d][1][0]))
        def _():
            block_buf[d, 1] = jnp.zeros((2, HOPS_DEV * NFINE, BLOCKW), jnp.bfloat16)

        pl.when(wanted[d][1][0])(lambda d=d: block_copy(d, 1).wait())
        for rank in range(PAIR):

            @pl.when(wanted[d][rank][0])
            def _():
                early_buf[d, rank] = jnp.concatenate(
                    [block_buf[d, rank, 0, :, :HALF], block_buf[d, rank, 1, :, :HALF]], axis=1
                ).reshape(HOPS_DEV, NFINE, BLOCKW)
                early_copy(d, rank).start()

        @pl.when(wanted[d][0][0])
        def _():
            def one_hop(hop, carry):
                rows = pl.ds(pl.multiple_of(hop * NFINE, NFINE), NFINE)
                wide = jnp.concatenate([block_buf[d, i // 2, i % 2, rows] for i in range(2 * PAIR)], axis=1)
                turned = lax.dot_general(
                    pick_ref[...], wide, (((1,), (1,)), ((), ())), preferred_element_type=jnp.float32
                )
                late_buf[d, :, hop] = turned.reshape(TM, ROWS, NFINE).astype(jnp.bfloat16)
                return carry

            lax.fori_loop(0, HOPS_DEV, one_hop, 0)
            late_copy(d).start()

    for d, r in order:
        pl.when(wanted[d][r][0])(lambda d=d, r=r: early_copy(d, r).wait())
        if r == 0:
            pl.when(wanted[d][0][0])(lambda d=d: late_copy(d).wait())


def pack(coarse, pick, req_block, req_count, place):
    anywhere = pl.BlockSpec(memory_space=pl.ANY)
    early = jax.ShapeDtypeStruct((PAIR, HOPS_DEV, NFINE, BLOCKW), jnp.bfloat16)
    return pl.pallas_call(
        pack_kernel,
        out_shape=[jax.ShapeDtypeStruct((TM, OWNERS, HOPS_DEV, ROWS, NFINE), jnp.bfloat16)] + [early] * OWNERS,
        grid_spec=pltpu.PrefetchScalarGridSpec(
            num_scalar_prefetch=3,
            grid=(1,),
            in_specs=[anywhere, pl.BlockSpec((TM * ROWS, PAIR * 2 * BLOCKW), lambda i, *refs: (0, 0))],
            out_specs=[anywhere] * (1 + OWNERS),
            scratch_shapes=[
                pltpu.VMEM((OWNERS, PAIR, 2, HOPS_DEV * NFINE, BLOCKW), jnp.bfloat16),
                pltpu.VMEM((OWNERS, TM, HOPS_DEV, ROWS, NFINE), jnp.bfloat16),
                pltpu.VMEM((OWNERS, PAIR, HOPS_DEV, NFINE, BLOCKW), jnp.bfloat16),
                pltpu.SemaphoreType.DMA((OWNERS, PAIR)),
                pltpu.SemaphoreType.DMA((OWNERS,)),
                pltpu.SemaphoreType.DMA((OWNERS, PAIR)),
            ],
        ),
        name="pack",
    )(req_block, req_count, place, coarse, pick)


def in_hbm(array):
    return pltpu.with_memory_space_constraint(array, pltpu.HBM)


def arrival(slot, block_ref, count_ref, place_ref):
    owner = place_ref[0]
    slot = jnp.where(slot < count_ref[owner], slot, 0)
    source = block_ref[owner, slot] // BPC
    rank = jnp.int32(0)
    for other in range(MAXREQ - 1):
        same = (other < slot) & (block_ref[owner, other] // BPC == source)
        rank = rank + same.astype(jnp.int32)
    return (owner - source + OWNERS) % OWNERS, jnp.minimum(rank, PAIR - 1)


def choose_kernel(block_ref, count_ref, place_ref, a0, a1, a2, a3, pick_ref, out_ref, held_ref, out_buf, held_sem, out_sem):
    for slot in range(MAXREQ):
        shift, rank = arrival(slot, block_ref, count_ref, place_ref)
        for own, ref in enumerate((a0, a1, a2, a3)):

            @pl.when(shift == own)
            def _():
                pltpu.make_async_copy(ref.at[rank], held_ref.at[slot], held_sem.at[slot]).start()

    def out_copy(pair, hop):
        return pltpu.make_async_copy(out_buf.at[pair, hop], out_ref.at[:, pair, hop], out_sem.at[pair, hop])

    for pair in range(MAXREQ // 2):
        for slot in (2 * pair, 2 * pair + 1):
            pltpu.make_async_copy(a0.at[0], held_ref.at[slot], held_sem.at[slot]).wait()
        for hop in range(HOPS_DEV):
            both = jnp.concatenate([held_ref[pair * 2, hop], held_ref[pair * 2 + 1, hop]], axis=1)
            turned = lax.dot_general(
                pick_ref[...], both, (((1,), (1,)), ((), ())), preferred_element_type=jnp.float32
            )
            out_buf[pair, hop] = turned.reshape(TM, ROWS, NFINE).astype(jnp.bfloat16)
            out_copy(pair, hop).start()
    for pair in range(MAXREQ // 2):
        for hop in range(HOPS_DEV):
            out_copy(pair, hop).wait()


def choose(arrived, pick, req_block, req_count, place):
    anywhere = pl.BlockSpec(memory_space=pl.ANY)
    return pl.pallas_call(
        choose_kernel,
        out_shape=jax.ShapeDtypeStruct((TM, MAXREQ // 2, HOPS_DEV, ROWS, NFINE), jnp.bfloat16),
        grid_spec=pltpu.PrefetchScalarGridSpec(
            num_scalar_prefetch=3,
            grid=(1,),
            in_specs=[anywhere] * OWNERS + [pl.BlockSpec((TM * ROWS, 2 * BLOCKW), lambda i, *refs: (0, 0))],
            out_specs=anywhere,
            scratch_shapes=[
                pltpu.VMEM((MAXREQ, HOPS_DEV, NFINE, BLOCKW), jnp.bfloat16),
                pltpu.VMEM((MAXREQ // 2, HOPS_DEV, TM, ROWS, NFINE), jnp.bfloat16),
                pltpu.SemaphoreType.DMA((MAXREQ,)),
                pltpu.SemaphoreType.DMA((MAXREQ // 2, HOPS_DEV)),
            ],
        ),
        cost_estimate=pl.CostEstimate(flops=150_000_000_000, transcendentals=0, bytes_accessed=2**22),
        name="choose",
    )(req_block, req_count, place, *map(in_hbm, arrived), pick)


def turn(value, sign):
    return pltpu.roll(value, ROWS // 2, value.ndim - 2) * sign


def dft4(a, b, c, d, sign):
    s02, d02, s13, d13 = a + c, a - c, b + d, turn(b - d, sign)
    return s02 + s13, d02 + d13, s02 - s13, d02 - d13


def dft8(x, sign):
    half = math.sqrt(0.5)
    low = [x[i] + x[i + 4] for i in range(4)]
    high = [x[i] - x[i + 4] for i in range(4)]
    high[1] = (high[1] + turn(high[1], sign)) * half
    high[2] = turn(high[2], sign)
    high[3] = (turn(high[3], sign) - high[3]) * half
    even, odd = dft4(*low, sign), dft4(*high, sign)
    return [pair for both in zip(even, odd) for pair in both]


def transform(load, proto_ref, high_ref, low_ref, out_ref, wide_ref, fir_ref, split_ref):
    sign = jnp.where(lax.broadcasted_iota(jnp.int32, (ROWS, LANES), 0) < ROWS // 2, 1.0, -1.0)
    wide_ref[HOPS:, :, :] = jnp.zeros((FRAMES + TAPS - 1 - HOPS, ROWS, LANES), jnp.float32)
    def taps(tile, carry):
        lanes = pl.ds(pl.multiple_of(tile * LANES, LANES), LANES)
        wide_ref[:HOPS] = load(lanes)
        weights = [jnp.broadcast_to(proto_ref[tap, lanes].reshape(1, LANES), (ROWS, LANES)) for tap in range(TAPS)]

        def fir(step, inner):
            first = step * GROUP
            samples = wide_ref[pl.ds(first, GROUP + TAPS - 1)]
            total = samples[:GROUP] * weights[0]
            for tap in range(1, TAPS):
                total = total + samples[tap : tap + GROUP] * weights[tap]
            fir_ref[pl.ds(first, GROUP), :, lanes] = total
            return inner

        return lax.fori_loop(0, FRAMES // GROUP, fir, carry)

    lax.fori_loop(0, RADIX, taps, 0)

    def butterflies(step, carry):
        first = step * 2
        parts = [fir_ref[pl.ds(first, 2), :, tile * LANES : (tile + 1) * LANES] for tile in range(RADIX)]
        rows = pl.ds(pl.multiple_of(first * ROWS, 2 * ROWS), 2 * ROWS)
        for m1, value in enumerate(dft8(parts, sign)):
            value = value.reshape(2 * ROWS, LANES)
            high = value.astype(jnp.bfloat16)
            split_ref[m1, rows, :LANES] = high
            split_ref[m1, rows, LANES : 2 * LANES] = (value - high.astype(jnp.float32)).astype(jnp.bfloat16)
            split_ref[m1, rows, 2 * LANES :] = high
        return carry

    lax.fori_loop(0, FRAMES // 2, butterflies, 0)
    for m1 in range(RADIX):
        high = high_ref[m1]
        product = jnp.dot(
            split_ref[m1], jnp.concatenate([high, high, low_ref[m1]], axis=0), preferred_element_type=jnp.float32
        )
        cosines = product[:, :LANES].reshape(FRAMES, ROWS, LANES)
        sines = product[:, LANES:].reshape(FRAMES, ROWS, LANES)
        result = (cosines + turn(sines, sign)).astype(jnp.bfloat16)
        out_ref[: FRAMES // HOPS_DEV, :, 0, :, m1 * LANES : (m1 + 1) * LANES] = result.reshape(
            FRAMES // HOPS_DEV, HOPS_DEV, ROWS, LANES
        )


def early_kernel(x_ref, *refs):
    pair = pl.program_id(0)

    def load(lanes):
        return x_ref[:, pair, :, :, lanes].astype(jnp.float32).reshape(HOPS, ROWS, LANES)

    transform(load, *refs)


def late_kernel(block_ref, count_ref, place_ref, a0, a1, a2, a3, proto_ref, high_ref, low_ref, out_ref, wide_ref, fir_ref, split_ref, held_ref, sem):
    pair = pl.program_id(0)

    @pl.when(pair == 0)
    def _():
        for slot in range(MAXREQ):
            shift, _ = arrival(slot, block_ref, count_ref, place_ref)
            for own, ref in enumerate((a0.at[:, 0], a1, a2, a3)):

                @pl.when(shift == own)
                def _():
                    pltpu.make_async_copy(ref, held_ref.at[slot], sem.at[slot]).start()

    for slot in range(2):
        at = pair * 2 + slot
        pltpu.make_async_copy(a1, held_ref.at[at], sem.at[at]).wait()

    ranks = [arrival(slot, block_ref, count_ref, place_ref)[1] for slot in range(MAXREQ)]
    first_rank = jnp.where(pair == 0, ranks[0], ranks[2])
    second_rank = jnp.where(pair == 0, ranks[1], ranks[3])
    is_second = (lax.broadcasted_iota(jnp.int32, (HOPS, ROWS, LANES), 1) // SHARE) % 2 == 1

    def load(lanes):
        first = held_ref[pair * 2, :, :, :, lanes].astype(jnp.float32).reshape(HOPS, ROWS, LANES)
        second = held_ref[pair * 2 + 1, :, :, :, lanes].astype(jnp.float32).reshape(HOPS, ROWS, LANES)
        first = jnp.where(first_rank == 0, first, pltpu.roll(first, ROWS - SHARE, 1))
        second = jnp.where(second_rank == 1, second, pltpu.roll(second, SHARE, 1))
        return jnp.where(is_second, second, first)

    transform(load, proto_ref, high_ref, low_ref, out_ref, wide_ref, fir_ref, split_ref)


def table_specs():
    return [
        pl.BlockSpec((TAPS, NFINE), lambda p, *refs: (0, 0)),
        pl.BlockSpec((RADIX, LANES, 2 * LANES), lambda p, *refs: (0, 0, 0)),
        pl.BlockSpec((RADIX, LANES, 2 * LANES), lambda p, *refs: (0, 0, 0)),
    ]


RESULT = jax.ShapeDtypeStruct((TM, HOPS_DEV, MAXREQ // 2, ROWS, NFINE), jnp.bfloat16)


def result_spec():
    return pl.BlockSpec((TM, HOPS_DEV, 1, ROWS, NFINE), lambda p, *refs: (0, 0, p, 0, 0))


def work_space():
    return [
        pltpu.VMEM((FRAMES + TAPS - 1, ROWS, LANES), jnp.float32),
        pltpu.VMEM((FRAMES, ROWS, NFINE), jnp.float32),
        pltpu.VMEM((RADIX, FRAMES * ROWS, 3 * LANES), jnp.bfloat16),
    ]


def filter_early(gathered, tables):
    return pl.pallas_call(
        early_kernel,
        out_shape=RESULT,
        grid=(MAXREQ // 2,),
        in_specs=[
            pl.BlockSpec(memory_space=pltpu.VMEM),
            *table_specs(),
        ],
        out_specs=result_spec(),
        scratch_shapes=work_space(),
        cost_estimate=COST,
        name="filter_early",
    )(pltpu.with_memory_space_constraint(gathered, pltpu.VMEM), *tables)


def filter_late(arrived, tables, req_block, req_count, place):
    return pl.pallas_call(
        late_kernel,
        out_shape=RESULT,
        grid_spec=pltpu.PrefetchScalarGridSpec(
            num_scalar_prefetch=3,
            grid=(MAXREQ // 2,),
            in_specs=[pl.BlockSpec(memory_space=pl.ANY)] * OWNERS + table_specs(),
            out_specs=result_spec(),
            scratch_shapes=work_space()
            + [
                pltpu.VMEM((MAXREQ, TM, HOPS_DEV, ROWS, NFINE), jnp.bfloat16),
                pltpu.SemaphoreType.DMA((MAXREQ,)),
            ],
        ),
        cost_estimate=COST,
        name="filter_late",
    )(req_block, req_count, place, *map(in_hbm, arrived), *tables)


def final_pick(slot):
    shape = (2 * TM * ROWS, 2 * BLOCKW)
    row, column = (lax.broadcasted_iota(jnp.int32, shape, dim) for dim in range(2))
    place = (row // ROWS) * SHARE + row % SHARE + BLOCKW * ((row // 4) % 2)
    return jnp.where((place == column) & ((row // 2) % 2 == slot), 1.0, 0.0).astype(jnp.bfloat16)


def unpack_kernel(start_ref, frames_ref, count_ref, place_ref, early_ref, late_ref, out_ref, back_buf, rows_ref, turned_ref, pick_ref, sem):
    owner = place_ref[0]
    step = pl.program_id(0)

    def is_active(hop, slot):
        frame = place_ref[1] * HOPS_DEV + hop
        begin = start_ref[owner, slot]
        return (slot < count_ref[owner]) & (frame >= begin) & (frame < begin + frames_ref[owner, slot])

    def back_copies(hop, pair):
        at = hop * (MAXREQ // 2) + pair
        return [
            pltpu.make_async_copy(ref.at[:, hop, pair], back_buf.at[at, half], sem.at[at, half])
            for half, ref in enumerate((early_ref, late_ref))
        ]

    @pl.when(step == 0)
    def _():
        for hop in range(HOPS_DEV):
            for pair in range(MAXREQ // 2):

                @pl.when(is_active(hop, 2 * pair) | is_active(hop, 2 * pair + 1))
                def _():
                    for copy in back_copies(hop, pair):
                        copy.start()

        for which in range(2):
            pick_ref[which] = final_pick(which)

    hop, pair = step // (MAXREQ // 2), step % (MAXREQ // 2)
    active = [is_active(hop, 2 * pair + which) for which in range(2)]

    @pl.when(active[0] | active[1])
    def _():
        for copy in back_copies(hop, pair):
            copy.wait()
        rows_ref[...] = back_buf[step].astype(jnp.float32).reshape(2 * TM * ROWS, NFINE).astype(jnp.bfloat16)

    for which in range(2):

        @pl.when(active[which])
        def _():
            columns = lax.dot_general(
                rows_ref[...], pick_ref[which], (((0,), (0,)), ((), ())), preferred_element_type=jnp.float32
            )
            for m1 in range(RADIX):
                for part in range(2):
                    turned_ref[part, pl.ds(m1, LANES, stride=RADIX), :] = columns[
                        m1 * LANES : (m1 + 1) * LANES, part * BLOCKW : (part + 1) * BLOCKW
                    ]
            out_ref[0, 0, which] = turned_ref[...].astype(jnp.bfloat16)

        @pl.when(jnp.logical_not(active[which]))
        def _():
            out_ref[0, 0, which] = jnp.zeros((2, NFINE, BLOCKW), jnp.bfloat16)


def unpack(early, late, req_start, req_frames, req_count, place):
    anywhere = pl.BlockSpec(memory_space=pl.ANY)
    steps = HOPS_DEV * MAXREQ // 2
    return pl.pallas_call(
        unpack_kernel,
        out_shape=jax.ShapeDtypeStruct((HOPS_DEV, 1, MAXREQ, 2, NFINE, BLOCKW), jnp.bfloat16),
        grid_spec=pltpu.PrefetchScalarGridSpec(
            num_scalar_prefetch=4,
            grid=(steps,),
            in_specs=[anywhere, anywhere],
            out_specs=pl.BlockSpec(
                (1, 1, 2, 2, NFINE, BLOCKW),
                lambda i, *refs: (i // (MAXREQ // 2), 0, i % (MAXREQ // 2), 0, 0, 0),
            ),
            scratch_shapes=[
                pltpu.VMEM((steps, 2, TM, ROWS, NFINE), jnp.bfloat16),
                pltpu.VMEM((2 * TM * ROWS, NFINE), jnp.bfloat16),
                pltpu.VMEM((2, NFINE, BLOCKW), jnp.float32),
                pltpu.VMEM((2, 2 * TM * ROWS, 2 * BLOCKW), jnp.bfloat16),
                pltpu.SemaphoreType.DMA((steps, 2)),
            ],
        ),
        name="unpack",
    )(req_start, req_frames, req_count, place, in_hbm(early), in_hbm(late))


def over_tm(array):
    return lax.all_to_all(array, "tm", split_axis=0, concat_axis=0, tiled=True)


def along_chan(arrays):
    return [arrays[0]] + [
        lax.ppermute(in_hbm(arrays[d]), "chan", [(s, (s + d) % OWNERS) for s in range(OWNERS)])
        for d in range(1, OWNERS)
    ]


def shards(coarse, prototype, req_block, req_start, req_frames, req_count):
    column = lax.axis_index("chan").astype(jnp.int32)
    place = jnp.stack([column, lax.axis_index("tm").astype(jnp.int32)])
    tables = (prototype, *(jnp.asarray(table) for table in dft_tables()))
    late, *early = pack(coarse, jnp.asarray(late_pick()), req_block, req_count, place)
    late = over_tm(late)
    early = choose(along_chan(early), jnp.asarray(early_pick()), req_block, req_count, place)
    late, early = lax.optimization_barrier((late, early))
    early = over_tm(early)
    late = along_chan([late] + [late[:, d] for d in range(1, OWNERS)])
    early = filter_early(early, tables)
    _, *late = lax.optimization_barrier((early, *late))
    early, late = lax.optimization_barrier((over_tm(early), filter_late(late, tables, req_block, req_count, place)))
    late = over_tm(late)
    return unpack(early, late, req_start, req_frames, req_count, place)


def solution(mesh):
    return jax.shard_map(
        shards,
        mesh=mesh,
        in_specs=(P(None, "tm", "chan"), P(), P(), P(), P(), P()),
        out_specs=P("tm", "chan", None, None, None, None),
        check_vma=False,
    )
```

```python
import math

import jax
import jax.numpy as jnp
import ml_dtypes
import numpy as np
from jax import lax
from jax.experimental import pallas as pl
from jax.experimental.pallas import tpu as pltpu
from jax.sharding import PartitionSpec as P

BLOCKW = 128
NFINE = 1024
TAPS = 16
HOPS_DEV = 3
MAXREQ = 4
PAIR = 2
TM = 32
OWNERS = 4
BPC = 8
HOPS = 96
HALF = BLOCKW // 2
SHARE = HALF // TM
ROWS = 8
RADIX = 8
LANES = 128
FRAMES = 84
GROUP = 12
UNROLLED = 42
COST = pl.CostEstimate(flops=18_000_000_000, transcendentals=0, bytes_accessed=2 * MAXREQ * HOPS * 4 * NFINE * 2)


def late_pick():
    pick = np.zeros((TM, 2, PAIR, SHARE, PAIR, 2, BLOCKW), np.float32)
    for device, part, rank, column in np.ndindex(TM, 2, PAIR, SHARE):
        pick[device, part, rank, column, rank, part, HALF + device * SHARE + column] = 1
    return pick.reshape(TM * ROWS, PAIR * 2 * BLOCKW).astype(ml_dtypes.bfloat16)


def early_pick():
    pick = np.zeros((TM, 2, 2, SHARE, 2, 2, HALF), np.float32)
    for device, part, slot, column in np.ndindex(TM, 2, 2, SHARE):
        pick[device, part, slot, column, slot, part, device * SHARE + column] = 1
    return pick.reshape(TM * ROWS, 2 * BLOCKW).astype(ml_dtypes.bfloat16)


def dft_tables():
    k2 = np.arange(LANES)[None, :, None]
    m = np.arange(RADIX)[:, None, None] + RADIX * np.arange(LANES)[None, None, :]
    angles = (k2 * m % NFINE) * (2.0 * math.pi / NFINE)
    table = np.concatenate([np.cos(angles), np.sin(angles)], axis=2) / math.sqrt(NFINE)
    high = table.astype(np.float32).astype(ml_dtypes.bfloat16)
    low = (table - high.astype(np.float64)).astype(np.float32).astype(ml_dtypes.bfloat16)
    return high, low


def wanted_block(shift, rank, block_ref, count_ref, place_ref):
    owner = (place_ref[0] + shift) % OWNERS
    seen = jnp.int32(0)
    chosen = jnp.int32(0)
    for slot in range(MAXREQ):
        block = block_ref[owner, slot]
        mine = (slot < count_ref[owner]) & (block // BPC == place_ref[0])
        chosen = jnp.where(mine & (seen == rank), block % BPC, chosen)
        seen = seen + mine.astype(jnp.int32)
    return seen > rank, chosen


def pack_kernel(block_ref, count_ref, place_ref, x_ref, pick_ref, *refs):
    late_ref, *early_refs = refs[: 1 + OWNERS]
    block_buf, late_buf, early_buf, block_sem, late_sem, early_sem = refs[1 + OWNERS :]
    wanted = [[wanted_block(d, r, block_ref, count_ref, place_ref) for r in range(PAIR)] for d in range(OWNERS)]

    def block_copy(d, r):
        columns = pl.ds(pl.multiple_of(wanted[d][r][1] * BLOCKW, BLOCKW), BLOCKW)
        return pltpu.make_async_copy(x_ref.at[:, :, columns], block_buf.at[d, r], block_sem.at[d, r])

    def late_copy(d):
        return pltpu.make_async_copy(late_buf.at[d], late_ref.at[:, d], late_sem.at[d])

    def early_copy(d, r):
        return pltpu.make_async_copy(early_buf.at[d, r], early_refs[d].at[r], early_sem.at[d, r])

    order = [(d, r) for d in (1, 2, 3, 0) for r in range(PAIR)]
    for d, r in order:
        pl.when(wanted[d][r][0])(lambda d=d, r=r: block_copy(d, r).start())
    for d, r in order:
        if r == 0:
            pl.when(wanted[d][0][0])(lambda d=d: block_copy(d, 0).wait())
            continue

        pl.when(wanted[d][1][0])(lambda d=d: block_copy(d, 1).wait())
        for rank in range(PAIR):

            @pl.when(wanted[d][rank][0])
            def _():
                early_buf[d, rank] = jnp.concatenate(
                    [block_buf[d, rank, 0, :, :HALF], block_buf[d, rank, 1, :, :HALF]], axis=1
                ).reshape(HOPS_DEV, NFINE, BLOCKW)
                early_copy(d, rank).start()

        def turn_blocks(d, ranks):
            def one_hop(hop, carry):
                rows = pl.ds(pl.multiple_of(hop * NFINE, NFINE), NFINE)
                wide = jnp.concatenate([block_buf[d, i // 2, i % 2, rows] for i in range(2 * ranks)], axis=1)
                turned = lax.dot_general(
                    pick_ref[:, : 2 * ranks * BLOCKW],
                    wide,
                    (((1,), (1,)), ((), ())),
                    preferred_element_type=jnp.float32,
                )
                late_buf[d, :, hop] = turned.reshape(TM, ROWS, NFINE).astype(jnp.bfloat16)
                return carry

            lax.fori_loop(0, HOPS_DEV, one_hop, 0)
            late_copy(d).start()

        pl.when(wanted[d][1][0])(lambda d=d: turn_blocks(d, 2))
        pl.when(wanted[d][0][0] & jnp.logical_not(wanted[d][1][0]))(lambda d=d: turn_blocks(d, 1))

    for d, r in order:
        pl.when(wanted[d][r][0])(lambda d=d, r=r: early_copy(d, r).wait())
        if r == 0:
            pl.when(wanted[d][0][0])(lambda d=d: late_copy(d).wait())


def pack(coarse, pick, req_block, req_count, place):
    anywhere = pl.BlockSpec(memory_space=pl.ANY)
    early = jax.ShapeDtypeStruct((PAIR, HOPS_DEV, NFINE, BLOCKW), jnp.bfloat16)
    return pl.pallas_call(
        pack_kernel,
        out_shape=[jax.ShapeDtypeStruct((TM, OWNERS, HOPS_DEV, ROWS, NFINE), jnp.bfloat16)] + [early] * OWNERS,
        grid_spec=pltpu.PrefetchScalarGridSpec(
            num_scalar_prefetch=3,
            grid=(1,),
            in_specs=[anywhere, pl.BlockSpec((TM * ROWS, PAIR * 2 * BLOCKW), lambda i, *refs: (0, 0))],
            out_specs=[anywhere] * (1 + OWNERS),
            scratch_shapes=[
                pltpu.VMEM((OWNERS, PAIR, 2, HOPS_DEV * NFINE, BLOCKW), jnp.bfloat16),
                pltpu.VMEM((OWNERS, TM, HOPS_DEV, ROWS, NFINE), jnp.bfloat16),
                pltpu.VMEM((OWNERS, PAIR, HOPS_DEV, NFINE, BLOCKW), jnp.bfloat16),
                pltpu.SemaphoreType.DMA((OWNERS, PAIR)),
                pltpu.SemaphoreType.DMA((OWNERS,)),
                pltpu.SemaphoreType.DMA((OWNERS, PAIR)),
            ],
        ),
        name="pack",
    )(req_block, req_count, place, coarse, pick)


def in_vmem(array):
    return pltpu.with_memory_space_constraint(array, pltpu.VMEM)


def in_hbm(array):
    return pltpu.with_memory_space_constraint(array, pltpu.HBM)


def arrival(slot, block_ref, count_ref, place_ref):
    owner = place_ref[0]
    slot = jnp.where(slot < count_ref[owner], slot, 0)
    source = block_ref[owner, slot] // BPC
    rank = jnp.int32(0)
    for other in range(MAXREQ - 1):
        same = (other < slot) & (block_ref[owner, other] // BPC == source)
        rank = rank + same.astype(jnp.int32)
    return (owner - source + OWNERS) % OWNERS, jnp.minimum(rank, PAIR - 1)


def choose_kernel(block_ref, count_ref, place_ref, a0, a1, a2, a3, pick_ref, out_ref, held_ref, out_buf, held_sem, out_sem):
    for slot in range(MAXREQ):
        shift, rank = arrival(slot, block_ref, count_ref, place_ref)
        for own, ref in enumerate((a0, a1, a2, a3)):

            @pl.when(shift == own)
            def _():
                pltpu.make_async_copy(ref.at[rank], held_ref.at[slot], held_sem.at[slot]).start()

    def out_copy(pair, hop):
        return pltpu.make_async_copy(out_buf.at[pair, hop], out_ref.at[:, pair, hop], out_sem.at[pair, hop])

    for pair in range(MAXREQ // 2):
        for slot in (2 * pair, 2 * pair + 1):
            pltpu.make_async_copy(a0.at[0], held_ref.at[slot], held_sem.at[slot]).wait()
        for hop in range(HOPS_DEV):
            both = jnp.concatenate([held_ref[pair * 2, hop], held_ref[pair * 2 + 1, hop]], axis=1)
            turned = lax.dot_general(
                pick_ref[...], both, (((1,), (1,)), ((), ())), preferred_element_type=jnp.float32
            )
            out_buf[pair, hop] = turned.reshape(TM, ROWS, NFINE).astype(jnp.bfloat16)
            out_copy(pair, hop).start()
    for pair in range(MAXREQ // 2):
        for hop in range(HOPS_DEV):
            out_copy(pair, hop).wait()


def choose(arrived, pick, req_block, req_count, place):
    anywhere = pl.BlockSpec(memory_space=pl.ANY)
    return pl.pallas_call(
        choose_kernel,
        out_shape=jax.ShapeDtypeStruct((TM, MAXREQ // 2, HOPS_DEV, ROWS, NFINE), jnp.bfloat16),
        grid_spec=pltpu.PrefetchScalarGridSpec(
            num_scalar_prefetch=3,
            grid=(1,),
            in_specs=[anywhere] * OWNERS + [pl.BlockSpec((TM * ROWS, 2 * BLOCKW), lambda i, *refs: (0, 0))],
            out_specs=anywhere,
            scratch_shapes=[
                pltpu.VMEM((MAXREQ, HOPS_DEV, NFINE, BLOCKW), jnp.bfloat16),
                pltpu.VMEM((MAXREQ // 2, HOPS_DEV, TM, ROWS, NFINE), jnp.bfloat16),
                pltpu.SemaphoreType.DMA((MAXREQ,)),
                pltpu.SemaphoreType.DMA((MAXREQ // 2, HOPS_DEV)),
            ],
        ),
        cost_estimate=pl.CostEstimate(flops=150_000_000_000, transcendentals=0, bytes_accessed=2**22),
        name="choose",
    )(req_block, req_count, place, *map(in_hbm, arrived), pick)


def turn(value, sign):
    return pltpu.roll(value, ROWS // 2, value.ndim - 2) * sign


def dft4(a, b, c, d, sign):
    s02, d02, s13, d13 = a + c, a - c, b + d, turn(b - d, sign)
    return s02 + s13, d02 + d13, s02 - s13, d02 - d13


def dft8(x, sign):
    half = math.sqrt(0.5)
    low = [x[i] + x[i + 4] for i in range(4)]
    high = [x[i] - x[i + 4] for i in range(4)]
    high[1] = (high[1] + turn(high[1], sign)) * half
    high[2] = turn(high[2], sign)
    high[3] = (turn(high[3], sign) - high[3]) * half
    even, odd = dft4(*low, sign), dft4(*high, sign)
    return [pair for both in zip(even, odd) for pair in both]


def transform(load, group_size, proto_ref, high_ref, low_ref, out_ref, wide_ref, fir_ref):
    sign = jnp.where(lax.broadcasted_iota(jnp.int32, (ROWS, LANES), 0) < ROWS // 2, 1.0, -1.0)
    wide_ref[:, HOPS:] = jnp.zeros((RADIX, FRAMES + TAPS - 1 - HOPS, ROWS, LANES), jnp.float32)

    def widen(tile, carry):
        wide_ref[tile, :HOPS] = load(pl.ds(pl.multiple_of(tile * LANES, LANES), LANES))
        return carry

    lax.fori_loop(0, RADIX, widen, 0)

    def one_group(group, carry):
        first = group * group_size
        for tile in range(RADIX):
            lanes = slice(tile * LANES, (tile + 1) * LANES)
            total = None
            for tap in range(TAPS):
                weights = jnp.broadcast_to(proto_ref[tap, lanes].reshape(1, LANES), (ROWS, LANES))
                part = wide_ref[tile, pl.ds(first + tap, group_size)] * weights
                total = part if total is None else total + part
            fir_ref[group, tile] = total
        for frame in range(0, group_size, 2):
            parts = [fir_ref[group, tile, frame : frame + 2] for tile in range(RADIX)]
            for m1, value in enumerate(dft8(parts, sign)):
                fir_ref[group, m1, frame : frame + 2] = value
        for m1 in range(RADIX):
            value = fir_ref[group, m1].reshape(group_size * ROWS, LANES)
            top = value.astype(jnp.bfloat16)
            rest = (value - top.astype(jnp.float32)).astype(jnp.bfloat16)
            high = high_ref[m1]
            product = jnp.dot(
                jnp.concatenate([top, rest, top], axis=1),
                jnp.concatenate([high, high, low_ref[m1]], axis=0),
                preferred_element_type=jnp.float32,
            )
            cosines = product[:, :LANES].reshape(group_size, ROWS, LANES)
            sines = product[:, LANES:].reshape(group_size, ROWS, LANES)
            result = (cosines + turn(sines, sign)).astype(jnp.bfloat16)
            devices = group_size // HOPS_DEV
            out_ref[pl.ds(group * devices, devices), :, 0, :, m1 * LANES : (m1 + 1) * LANES] = result.reshape(
                devices, HOPS_DEV, ROWS, LANES
            )
        return carry

    if group_size == UNROLLED:
        for group in range(FRAMES // group_size):
            one_group(group, 0)
    else:
        lax.fori_loop(0, FRAMES // group_size, one_group, 0)


def early_kernel(x_ref, *refs):
    pair = pl.program_id(0)

    def load(lanes):
        return x_ref[:, pair, :, :, lanes].astype(jnp.float32).reshape(HOPS, ROWS, LANES)

    transform(load, UNROLLED, *refs)


def late_kernel(block_ref, count_ref, place_ref, a0, a1, a2, a3, proto_ref, high_ref, low_ref, out_ref, wide_ref, fir_ref, held_ref, sem):
    pair = pl.program_id(0)

    @pl.when(pair == 0)
    def _():
        for slot in range(MAXREQ):
            shift, _ = arrival(slot, block_ref, count_ref, place_ref)
            for own, ref in enumerate((a0.at[:, 0], a1, a2, a3)):

                @pl.when(shift == own)
                def _():
                    pltpu.make_async_copy(ref, held_ref.at[slot], sem.at[slot]).start()

    for slot in range(2):
        at = pair * 2 + slot
        pltpu.make_async_copy(a1, held_ref.at[at], sem.at[at]).wait()

    ranks = [arrival(slot, block_ref, count_ref, place_ref)[1] for slot in range(MAXREQ)]
    first_rank = jnp.where(pair == 0, ranks[0], ranks[2])
    second_rank = jnp.where(pair == 0, ranks[1], ranks[3])
    is_second = (lax.broadcasted_iota(jnp.int32, (HOPS, ROWS, LANES), 1) // SHARE) % 2 == 1

    def load(lanes):
        first = held_ref[pair * 2, :, :, :, lanes].astype(jnp.float32).reshape(HOPS, ROWS, LANES)
        second = held_ref[pair * 2 + 1, :, :, :, lanes].astype(jnp.float32).reshape(HOPS, ROWS, LANES)
        first = jnp.where(first_rank == 0, first, pltpu.roll(first, ROWS - SHARE, 1))
        second = jnp.where(second_rank == 1, second, pltpu.roll(second, SHARE, 1))
        return jnp.where(is_second, second, first)

    transform(load, GROUP, proto_ref, high_ref, low_ref, out_ref, wide_ref, fir_ref)


def table_specs():
    return [
        pl.BlockSpec((TAPS, NFINE), lambda p, *refs: (0, 0)),
        pl.BlockSpec((RADIX, LANES, 2 * LANES), lambda p, *refs: (0, 0, 0)),
        pl.BlockSpec((RADIX, LANES, 2 * LANES), lambda p, *refs: (0, 0, 0)),
    ]


RESULT = jax.ShapeDtypeStruct((TM, HOPS_DEV, MAXREQ // 2, ROWS, NFINE), jnp.bfloat16)


def result_spec():
    return pl.BlockSpec((TM, HOPS_DEV, 1, ROWS, NFINE), lambda p, *refs: (0, 0, p, 0, 0))


def work_space(group_size):
    return [
        pltpu.VMEM((RADIX, FRAMES + TAPS - 1, ROWS, LANES), jnp.float32),
        pltpu.VMEM((FRAMES // group_size, RADIX, group_size, ROWS, LANES), jnp.float32),
    ]


def filter_early(gathered, tables):
    return pl.pallas_call(
        early_kernel,
        out_shape=RESULT,
        grid=(MAXREQ // 2,),
        in_specs=[
            pl.BlockSpec(memory_space=pltpu.VMEM),
            *table_specs(),
        ],
        out_specs=result_spec(),
        scratch_shapes=work_space(UNROLLED),
        cost_estimate=COST,
        name="filter_early",
    )(in_vmem(gathered), *tables)


def filter_late(arrived, tables, req_block, req_count, place):
    return pl.pallas_call(
        late_kernel,
        out_shape=RESULT,
        grid_spec=pltpu.PrefetchScalarGridSpec(
            num_scalar_prefetch=3,
            grid=(MAXREQ // 2,),
            in_specs=[pl.BlockSpec(memory_space=pl.ANY)] * OWNERS + table_specs(),
            out_specs=result_spec(),
            scratch_shapes=work_space(GROUP)
            + [
                pltpu.VMEM((MAXREQ, TM, HOPS_DEV, ROWS, NFINE), jnp.bfloat16),
                pltpu.SemaphoreType.DMA((MAXREQ,)),
            ],
        ),
        cost_estimate=COST,
        compiler_params=pltpu.CompilerParams(vmem_limit_bytes=56 * 2**20),
        name="filter_late",
    )(req_block, req_count, place, *map(in_hbm, arrived), *tables)


def final_pick():
    shape = (TM * ROWS, 2 * BLOCKW)
    row, column = (lax.broadcasted_iota(jnp.int32, shape, dim) for dim in range(2))
    place = (row // ROWS) * SHARE + row % SHARE + HALF * ((row // 4) % 2) + BLOCKW * ((row // 2) % 2)
    return jnp.where(place == column, 1.0, 0.0).astype(jnp.bfloat16)


def is_active(hop, slot, start_ref, frames_ref, count_ref, place_ref):
    owner = place_ref[0]
    frame = place_ref[1] * HOPS_DEV + hop
    begin = start_ref[owner, slot]
    return (slot < count_ref[owner]) & (frame >= begin) & (frame < begin + frames_ref[owner, slot])


def turn_back(back, pick_ref, turned_ref):
    rows = back.astype(jnp.float32).reshape(TM * ROWS, NFINE).astype(jnp.bfloat16)
    columns = lax.dot_general(rows, pick_ref[...], (((0,), (0,)), ((), ())), preferred_element_type=jnp.float32)
    for m1 in range(RADIX):
        for slot in range(2):
            turned_ref[slot, pl.ds(m1, LANES, stride=RADIX), :] = columns[
                m1 * LANES : (m1 + 1) * LANES, slot * BLOCKW : (slot + 1) * BLOCKW
            ]


def unpack_early_kernel(start_ref, frames_ref, count_ref, place_ref, early_ref, out_ref, turned_ref, pick_ref):
    refs = start_ref, frames_ref, count_ref, place_ref
    step = pl.program_id(0)
    hop, pair = step // (MAXREQ // 2), step % (MAXREQ // 2)

    @pl.when(step == 0)
    def _():
        pick_ref[...] = final_pick()

    @pl.when(is_active(hop, 2 * pair, *refs) | is_active(hop, 2 * pair + 1, *refs))
    def _():
        turn_back(early_ref[:, 0, 0], pick_ref, turned_ref)
        out_ref[0] = turned_ref[...].astype(jnp.bfloat16)


def unpack_kernel(start_ref, frames_ref, count_ref, place_ref, part_ref, late_ref, out_ref, turned_ref, pick_ref):
    refs = start_ref, frames_ref, count_ref, place_ref
    step = pl.program_id(0)
    hop, pair = step // (MAXREQ // 2), step % (MAXREQ // 2)

    @pl.when(step == 0)
    def _():
        pick_ref[...] = final_pick()

    @pl.when(is_active(hop, 2 * pair, *refs) | is_active(hop, 2 * pair + 1, *refs))
    def _():
        turn_back(late_ref[:, hop, pair], pick_ref, turned_ref)

    for which in range(2):
        active = is_active(hop, 2 * pair + which, *refs)

        @pl.when(active)
        def _():
            early = part_ref[0, which]
            late = turned_ref[which].astype(jnp.bfloat16)
            out_ref[0, 0, which, 0] = jnp.concatenate([early[:, :HALF], late[:, :HALF]], axis=1)
            out_ref[0, 0, which, 1] = jnp.concatenate([early[:, HALF:], late[:, HALF:]], axis=1)

        @pl.when(jnp.logical_not(active))
        def _():
            out_ref[0, 0, which] = jnp.zeros((2, NFINE, BLOCKW), jnp.bfloat16)


STEPS = HOPS_DEV * MAXREQ // 2


def unpack_early(early, req_start, req_frames, req_count, place):
    return pl.pallas_call(
        unpack_early_kernel,
        out_shape=jax.ShapeDtypeStruct((STEPS, 2, NFINE, BLOCKW), jnp.bfloat16),
        grid_spec=pltpu.PrefetchScalarGridSpec(
            num_scalar_prefetch=4,
            grid=(STEPS,),
            in_specs=[pl.BlockSpec((TM, 1, 1, ROWS, NFINE), lambda i, *refs: (0, i // (MAXREQ // 2), i % (MAXREQ // 2), 0, 0))],
            out_specs=pl.BlockSpec((1, 2, NFINE, BLOCKW), lambda i, *refs: (i, 0, 0, 0)),
            scratch_shapes=[
                pltpu.VMEM((2, NFINE, BLOCKW), jnp.float32),
                pltpu.VMEM((TM * ROWS, 2 * BLOCKW), jnp.bfloat16),
            ],
        ),
        cost_estimate=COST,
        compiler_params=pltpu.CompilerParams(vmem_limit_bytes=52 * 2**20),
        name="unpack_early",
    )(req_start, req_frames, req_count, place, in_hbm(early))


def unpack(part, late, req_start, req_frames, req_count, place):
    resident = pl.BlockSpec(memory_space=pltpu.VMEM)
    return pl.pallas_call(
        unpack_kernel,
        out_shape=jax.ShapeDtypeStruct((HOPS_DEV, 1, MAXREQ, 2, NFINE, BLOCKW), jnp.bfloat16),
        grid_spec=pltpu.PrefetchScalarGridSpec(
            num_scalar_prefetch=4,
            grid=(STEPS,),
            in_specs=[pl.BlockSpec((1, 2, NFINE, BLOCKW), lambda i, *refs: (i, 0, 0, 0)), resident],
            out_specs=pl.BlockSpec(
                (1, 1, 2, 2, NFINE, BLOCKW),
                lambda i, *refs: (i // (MAXREQ // 2), 0, i % (MAXREQ // 2), 0, 0, 0),
            ),
            scratch_shapes=[
                pltpu.VMEM((2, NFINE, BLOCKW), jnp.float32),
                pltpu.VMEM((TM * ROWS, 2 * BLOCKW), jnp.bfloat16),
            ],
        ),
        compiler_params=pltpu.CompilerParams(vmem_limit_bytes=52 * 2**20),
        name="unpack",
    )(req_start, req_frames, req_count, place, in_hbm(part), in_vmem(late))


def over_tm(array):
    return lax.all_to_all(array, "tm", split_axis=0, concat_axis=0, tiled=True)


def along_chan(arrays):
    return [arrays[0]] + [
        lax.ppermute(in_hbm(arrays[d]), "chan", [(s, (s + d) % OWNERS) for s in range(OWNERS)])
        for d in range(1, OWNERS)
    ]


def shards(coarse, prototype, req_block, req_start, req_frames, req_count):
    column = lax.axis_index("chan").astype(jnp.int32)
    place = jnp.stack([column, lax.axis_index("tm").astype(jnp.int32)])
    tables = (prototype, *(jnp.asarray(table) for table in dft_tables()))
    late, *early = pack(coarse, jnp.asarray(late_pick()), req_block, req_count, place)
    late = over_tm(late)
    early = choose(along_chan(early), jnp.asarray(early_pick()), req_block, req_count, place)
    late, early = lax.optimization_barrier((late, early))
    early = over_tm(early)
    late = along_chan([late] + [late[:, d] for d in range(1, OWNERS)])
    early = filter_early(early, tables)
    _, *late = lax.optimization_barrier((early, *late))
    early = over_tm(early)
    _, late = lax.optimization_barrier((early, filter_late(late, tables, req_block, req_count, place)))
    late = over_tm(late)
    part = unpack_early(early, req_start, req_frames, req_count, place)
    return unpack(part, late, req_start, req_frames, req_count, place)


def solution(mesh):
    return jax.shard_map(
        shards,
        mesh=mesh,
        in_specs=(P(None, "tm", "chan"), P(), P(), P(), P(), P()),
        out_specs=P("tm", "chan", None, None, None, None),
        check_vma=False,
    )
```

```python
import math

import jax
import jax.numpy as jnp
import ml_dtypes
import numpy as np
from jax import lax
from jax.experimental import pallas as pl
from jax.experimental.pallas import tpu as pltpu
from jax.sharding import PartitionSpec as P

BLOCKW = 128
NFINE = 1024
TAPS = 16
HOPS_DEV = 3
MAXREQ = 4
PAIR = 2
TM = 32
OWNERS = 4
BPC = 8
HOPS = 96
HALF = BLOCKW // 2
SHARE = HALF // TM
ROWS = 8
RADIX = 8
LANES = 128
FRAMES = 84
GROUP = 12
UNROLLED = 42
COST = pl.CostEstimate(flops=18_000_000_000, transcendentals=0, bytes_accessed=2 * MAXREQ * HOPS * 4 * NFINE * 2)


def late_pick():
    pick = np.zeros((TM, 2, PAIR, SHARE, PAIR, 2, BLOCKW), np.float32)
    for device, part, rank, column in np.ndindex(TM, 2, PAIR, SHARE):
        pick[device, part, rank, column, rank, part, HALF + device * SHARE + column] = 1
    return pick.reshape(TM * ROWS, PAIR * 2 * BLOCKW).astype(ml_dtypes.bfloat16)


def early_pick():
    pick = np.zeros((TM, 2, 2, SHARE, 2, 2, HALF), np.float32)
    for device, part, slot, column in np.ndindex(TM, 2, 2, SHARE):
        pick[device, part, slot, column, slot, part, device * SHARE + column] = 1
    return pick.reshape(TM * ROWS, 2 * BLOCKW).astype(ml_dtypes.bfloat16)


def dft_tables():
    k2 = np.arange(LANES)[None, :, None]
    m = np.arange(RADIX)[:, None, None] + RADIX * np.arange(LANES)[None, None, :]
    angles = (k2 * m % NFINE) * (2.0 * math.pi / NFINE)
    table = np.concatenate([np.cos(angles), np.sin(angles)], axis=2) / math.sqrt(NFINE)
    high = table.astype(np.float32).astype(ml_dtypes.bfloat16)
    low = (table - high.astype(np.float64)).astype(np.float32).astype(ml_dtypes.bfloat16)
    return high, low


def wanted_block(shift, rank, block_ref, count_ref, place_ref):
    owner = (place_ref[0] + shift) % OWNERS
    seen = jnp.int32(0)
    chosen = jnp.int32(0)
    for slot in range(MAXREQ):
        block = block_ref[owner, slot]
        mine = (slot < count_ref[owner]) & (block // BPC == place_ref[0])
        chosen = jnp.where(mine & (seen == rank), block % BPC, chosen)
        seen = seen + mine.astype(jnp.int32)
    return seen > rank, chosen


def some_serves_all(block_ref, count_ref):
    some = jnp.bool_(False)
    for source in range(OWNERS):
        every = jnp.bool_(True)
        for owner in range(OWNERS):
            serves = jnp.bool_(False)
            for slot in range(MAXREQ):
                serves = serves | ((slot < count_ref[owner]) & (block_ref[owner, slot] // BPC == source))
            every = every & serves
        some = some | every
    return some


def pack_kernel(block_ref, count_ref, place_ref, x_ref, pick_ref, *refs):
    plan_ref, late_ref, last_ref, *early_refs = refs[: 3 + OWNERS]
    block_buf, late_buf, early_buf, block_sem, late_sem, early_sem = refs[3 + OWNERS :]
    wanted = [[wanted_block(d, r, block_ref, count_ref, place_ref) for r in range(PAIR)] for d in range(OWNERS)]
    groups = []
    live = jnp.int32(0)
    for d in range(OWNERS):
        groups.append(live)
        plan_ref[d] = live
        live = live + wanted[d][0][0].astype(jnp.int32)

    def block_copy(d, r):
        columns = pl.ds(pl.multiple_of(wanted[d][r][1] * BLOCKW, BLOCKW), BLOCKW)
        return pltpu.make_async_copy(x_ref.at[:, :, columns], block_buf.at[d, r], block_sem.at[d, r])

    def start_late_copy(d):
        @pl.when(groups[d] < OWNERS - 1)
        def _():
            pltpu.make_async_copy(late_buf.at[d], late_ref.at[:, groups[d]], late_sem.at[d]).start()

        @pl.when(groups[d] == OWNERS - 1)
        def _():
            pltpu.make_async_copy(late_buf.at[d], last_ref.at[:, 0], late_sem.at[d]).start()

    def early_copy(d, r):
        return pltpu.make_async_copy(early_buf.at[d, r], early_refs[d].at[r], early_sem.at[d, r])

    order = [(d, r) for d in (1, 2, 3, 0) for r in range(PAIR)]
    for d, r in order:
        pl.when(wanted[d][r][0])(lambda d=d, r=r: block_copy(d, r).start())
    plan_ref[OWNERS] = some_serves_all(block_ref, count_ref).astype(jnp.int32)
    for d, r in order:
        if r == 0:
            pl.when(wanted[d][0][0])(lambda d=d: block_copy(d, 0).wait())
            continue

        pl.when(wanted[d][1][0])(lambda d=d: block_copy(d, 1).wait())
        for rank in range(PAIR):

            @pl.when(wanted[d][rank][0])
            def _():
                early_buf[d, rank] = jnp.concatenate(
                    [block_buf[d, rank, 0, :, :HALF], block_buf[d, rank, 1, :, :HALF]], axis=1
                ).reshape(HOPS_DEV, NFINE, BLOCKW)
                early_copy(d, rank).start()

        def turn_blocks(d, ranks):
            def one_hop(hop, carry):
                rows = pl.ds(pl.multiple_of(hop * NFINE, NFINE), NFINE)
                wide = jnp.concatenate([block_buf[d, i // 2, i % 2, rows] for i in range(2 * ranks)], axis=1)
                turned = lax.dot_general(
                    pick_ref[:, : 2 * ranks * BLOCKW],
                    wide,
                    (((1,), (1,)), ((), ())),
                    preferred_element_type=jnp.float32,
                )
                late_buf[d, :, hop] = turned.reshape(TM, ROWS, NFINE).astype(jnp.bfloat16)
                return carry

            lax.fori_loop(0, HOPS_DEV, one_hop, 0)
            start_late_copy(d)

        pl.when(wanted[d][1][0])(lambda d=d: turn_blocks(d, 2))
        pl.when(wanted[d][0][0] & jnp.logical_not(wanted[d][1][0]))(lambda d=d: turn_blocks(d, 1))

    for d, r in order:
        pl.when(wanted[d][r][0])(lambda d=d, r=r: early_copy(d, r).wait())
        if r == 0:
            pl.when(wanted[d][0][0])(
                lambda d=d: pltpu.make_async_copy(late_buf.at[d], last_ref.at[:, 0], late_sem.at[d]).wait()
            )


def pack(coarse, pick, req_block, req_count, place):
    anywhere = pl.BlockSpec(memory_space=pl.ANY)
    early = jax.ShapeDtypeStruct((PAIR, HOPS_DEV, NFINE, BLOCKW), jnp.bfloat16)
    return pl.pallas_call(
        pack_kernel,
        out_shape=[
            jax.ShapeDtypeStruct((OWNERS + 1,), jnp.int32),
            jax.ShapeDtypeStruct((TM, OWNERS - 1, HOPS_DEV, ROWS, NFINE), jnp.bfloat16),
            jax.ShapeDtypeStruct((TM, 1, HOPS_DEV, ROWS, NFINE), jnp.bfloat16),
        ]
        + [early] * OWNERS,
        grid_spec=pltpu.PrefetchScalarGridSpec(
            num_scalar_prefetch=3,
            grid=(1,),
            in_specs=[anywhere, pl.BlockSpec((TM * ROWS, PAIR * 2 * BLOCKW), lambda i, *refs: (0, 0))],
            out_specs=[pl.BlockSpec(memory_space=pltpu.SMEM)] + [anywhere] * (2 + OWNERS),
            scratch_shapes=[
                pltpu.VMEM((OWNERS, PAIR, 2, HOPS_DEV * NFINE, BLOCKW), jnp.bfloat16),
                pltpu.VMEM((OWNERS, TM, HOPS_DEV, ROWS, NFINE), jnp.bfloat16),
                pltpu.VMEM((OWNERS, PAIR, HOPS_DEV, NFINE, BLOCKW), jnp.bfloat16),
                pltpu.SemaphoreType.DMA((OWNERS, PAIR)),
                pltpu.SemaphoreType.DMA((OWNERS,)),
                pltpu.SemaphoreType.DMA((OWNERS, PAIR)),
            ],
        ),
        name="pack",
    )(req_block, req_count, place, coarse, pick)


def in_vmem(array):
    return pltpu.with_memory_space_constraint(array, pltpu.VMEM)


def in_hbm(array):
    return pltpu.with_memory_space_constraint(array, pltpu.HBM)


def arrival(slot, block_ref, count_ref, place_ref):
    owner = place_ref[0]
    slot = jnp.where(slot < count_ref[owner], slot, 0)
    source = block_ref[owner, slot] // BPC
    rank = jnp.int32(0)
    for other in range(MAXREQ - 1):
        same = (other < slot) & (block_ref[owner, other] // BPC == source)
        rank = rank + same.astype(jnp.int32)
    return (owner - source + OWNERS) % OWNERS, jnp.minimum(rank, PAIR - 1)


def choose_kernel(block_ref, count_ref, place_ref, a0, a1, a2, a3, pick_ref, out_ref, held_ref, out_buf, held_sem, out_sem):
    for slot in range(MAXREQ):
        shift, rank = arrival(slot, block_ref, count_ref, place_ref)
        for own, ref in enumerate((a0, a1, a2, a3)):

            @pl.when(shift == own)
            def _():
                pltpu.make_async_copy(ref.at[rank], held_ref.at[slot], held_sem.at[slot]).start()

    def out_copy(pair, hop):
        return pltpu.make_async_copy(out_buf.at[pair, hop], out_ref.at[:, pair, hop], out_sem.at[pair, hop])

    for pair in range(MAXREQ // 2):
        for slot in (2 * pair, 2 * pair + 1):
            pltpu.make_async_copy(a0.at[0], held_ref.at[slot], held_sem.at[slot]).wait()
        for hop in range(HOPS_DEV):
            both = jnp.concatenate([held_ref[pair * 2, hop], held_ref[pair * 2 + 1, hop]], axis=1)
            turned = lax.dot_general(
                pick_ref[...], both, (((1,), (1,)), ((), ())), preferred_element_type=jnp.float32
            )
            out_buf[pair, hop] = turned.reshape(TM, ROWS, NFINE).astype(jnp.bfloat16)
            out_copy(pair, hop).start()
    for pair in range(MAXREQ // 2):
        for hop in range(HOPS_DEV):
            out_copy(pair, hop).wait()


def choose(arrived, pick, req_block, req_count, place):
    anywhere = pl.BlockSpec(memory_space=pl.ANY)
    return pl.pallas_call(
        choose_kernel,
        out_shape=jax.ShapeDtypeStruct((TM, MAXREQ // 2, HOPS_DEV, ROWS, NFINE), jnp.bfloat16),
        grid_spec=pltpu.PrefetchScalarGridSpec(
            num_scalar_prefetch=3,
            grid=(1,),
            in_specs=[anywhere] * OWNERS + [pl.BlockSpec((TM * ROWS, 2 * BLOCKW), lambda i, *refs: (0, 0))],
            out_specs=anywhere,
            scratch_shapes=[
                pltpu.VMEM((MAXREQ, HOPS_DEV, NFINE, BLOCKW), jnp.bfloat16),
                pltpu.VMEM((MAXREQ // 2, HOPS_DEV, TM, ROWS, NFINE), jnp.bfloat16),
                pltpu.SemaphoreType.DMA((MAXREQ,)),
                pltpu.SemaphoreType.DMA((MAXREQ // 2, HOPS_DEV)),
            ],
        ),
        cost_estimate=pl.CostEstimate(flops=150_000_000_000, transcendentals=0, bytes_accessed=2**22),
        name="choose",
    )(req_block, req_count, place, *map(in_hbm, arrived), pick)


def turn(value, sign):
    return pltpu.roll(value, ROWS // 2, value.ndim - 2) * sign


def dft4(a, b, c, d, sign):
    s02, d02, s13, d13 = a + c, a - c, b + d, turn(b - d, sign)
    return s02 + s13, d02 + d13, s02 - s13, d02 - d13


def dft8(x, sign):
    half = math.sqrt(0.5)
    low = [x[i] + x[i + 4] for i in range(4)]
    high = [x[i] - x[i + 4] for i in range(4)]
    high[1] = (high[1] + turn(high[1], sign)) * half
    high[2] = turn(high[2], sign)
    high[3] = (turn(high[3], sign) - high[3]) * half
    even, odd = dft4(*low, sign), dft4(*high, sign)
    return [pair for both in zip(even, odd) for pair in both]


def transform(load, group_size, proto_ref, high_ref, low_ref, out_ref, wide_ref, fir_ref):
    sign = jnp.where(lax.broadcasted_iota(jnp.int32, (ROWS, LANES), 0) < ROWS // 2, 1.0, -1.0)
    wide_ref[:, HOPS:] = jnp.zeros((RADIX, FRAMES + TAPS - 1 - HOPS, ROWS, LANES), jnp.float32)

    def widen(tile, carry):
        wide_ref[tile, :HOPS] = load(pl.ds(pl.multiple_of(tile * LANES, LANES), LANES))
        return carry

    lax.fori_loop(0, RADIX, widen, 0)

    def one_group(group, carry):
        first = group * group_size
        for tile in range(RADIX):
            lanes = slice(tile * LANES, (tile + 1) * LANES)
            total = None
            for tap in range(TAPS):
                weights = jnp.broadcast_to(proto_ref[tap, lanes].reshape(1, LANES), (ROWS, LANES))
                part = wide_ref[tile, pl.ds(first + tap, group_size)] * weights
                total = part if total is None else total + part
            fir_ref[group, tile] = total
        for frame in range(0, group_size, 2):
            parts = [fir_ref[group, tile, frame : frame + 2] for tile in range(RADIX)]
            for m1, value in enumerate(dft8(parts, sign)):
                fir_ref[group, m1, frame : frame + 2] = value
        for m1 in range(RADIX):
            value = fir_ref[group, m1].reshape(group_size * ROWS, LANES)
            top = value.astype(jnp.bfloat16)
            rest = (value - top.astype(jnp.float32)).astype(jnp.bfloat16)
            high = high_ref[m1]
            product = jnp.dot(
                jnp.concatenate([top, rest, top], axis=1),
                jnp.concatenate([high, high, low_ref[m1]], axis=0),
                preferred_element_type=jnp.float32,
            )
            cosines = product[:, :LANES].reshape(group_size, ROWS, LANES)
            sines = product[:, LANES:].reshape(group_size, ROWS, LANES)
            result = (cosines + turn(sines, sign)).astype(jnp.bfloat16)
            devices = group_size // HOPS_DEV
            out_ref[pl.ds(group * devices, devices), :, 0, :, m1 * LANES : (m1 + 1) * LANES] = result.reshape(
                devices, HOPS_DEV, ROWS, LANES
            )
        return carry

    if group_size == UNROLLED:
        for group in range(FRAMES // group_size):
            one_group(group, 0)
    else:
        lax.fori_loop(0, FRAMES // group_size, one_group, 0)


def early_kernel(x_ref, *refs):
    pair = pl.program_id(0)

    def load(lanes):
        return x_ref[:, pair, :, :, lanes].astype(jnp.float32).reshape(HOPS, ROWS, LANES)

    transform(load, UNROLLED, *refs)


def late_kernel(block_ref, count_ref, place_ref, a0, a1, a2, a3, proto_ref, high_ref, low_ref, out_ref, wide_ref, fir_ref, held_ref, sem):
    pair = pl.program_id(0)

    @pl.when(pair == 0)
    def _():
        for slot in range(MAXREQ):
            shift, _ = arrival(slot, block_ref, count_ref, place_ref)
            for own, ref in enumerate((a0.at[:, 0], a1, a2, a3)):

                @pl.when(shift == own)
                def _():
                    pltpu.make_async_copy(ref, held_ref.at[slot], sem.at[slot]).start()

    for slot in range(2):
        at = pair * 2 + slot
        pltpu.make_async_copy(a1, held_ref.at[at], sem.at[at]).wait()

    ranks = [arrival(slot, block_ref, count_ref, place_ref)[1] for slot in range(MAXREQ)]
    first_rank = jnp.where(pair == 0, ranks[0], ranks[2])
    second_rank = jnp.where(pair == 0, ranks[1], ranks[3])
    is_second = (lax.broadcasted_iota(jnp.int32, (HOPS, ROWS, LANES), 1) // SHARE) % 2 == 1

    def load(lanes):
        first = held_ref[pair * 2, :, :, :, lanes].astype(jnp.float32).reshape(HOPS, ROWS, LANES)
        second = held_ref[pair * 2 + 1, :, :, :, lanes].astype(jnp.float32).reshape(HOPS, ROWS, LANES)
        first = jnp.where(first_rank == 0, first, pltpu.roll(first, ROWS - SHARE, 1))
        second = jnp.where(second_rank == 1, second, pltpu.roll(second, SHARE, 1))
        return jnp.where(is_second, second, first)

    transform(load, GROUP, proto_ref, high_ref, low_ref, out_ref, wide_ref, fir_ref)


def table_specs():
    return [
        pl.BlockSpec((TAPS, NFINE), lambda p, *refs: (0, 0)),
        pl.BlockSpec((RADIX, LANES, 2 * LANES), lambda p, *refs: (0, 0, 0)),
        pl.BlockSpec((RADIX, LANES, 2 * LANES), lambda p, *refs: (0, 0, 0)),
    ]


RESULT = jax.ShapeDtypeStruct((TM, HOPS_DEV, MAXREQ // 2, ROWS, NFINE), jnp.bfloat16)


def result_spec():
    return pl.BlockSpec((TM, HOPS_DEV, 1, ROWS, NFINE), lambda p, *refs: (0, 0, p, 0, 0))


def work_space(group_size):
    return [
        pltpu.VMEM((RADIX, FRAMES + TAPS - 1, ROWS, LANES), jnp.float32),
        pltpu.VMEM((FRAMES // group_size, RADIX, group_size, ROWS, LANES), jnp.float32),
    ]


def filter_early(gathered, tables):
    return pl.pallas_call(
        early_kernel,
        out_shape=RESULT,
        grid=(MAXREQ // 2,),
        in_specs=[
            pl.BlockSpec(memory_space=pltpu.VMEM),
            *table_specs(),
        ],
        out_specs=result_spec(),
        scratch_shapes=work_space(UNROLLED),
        cost_estimate=COST,
        name="filter_early",
    )(in_vmem(gathered), *tables)


def filter_late(arrived, tables, req_block, req_count, place):
    return pl.pallas_call(
        late_kernel,
        out_shape=RESULT,
        grid_spec=pltpu.PrefetchScalarGridSpec(
            num_scalar_prefetch=3,
            grid=(MAXREQ // 2,),
            in_specs=[pl.BlockSpec(memory_space=pl.ANY)] * OWNERS + table_specs(),
            out_specs=result_spec(),
            scratch_shapes=work_space(GROUP)
            + [
                pltpu.VMEM((MAXREQ, TM, HOPS_DEV, ROWS, NFINE), jnp.bfloat16),
                pltpu.SemaphoreType.DMA((MAXREQ,)),
            ],
        ),
        cost_estimate=COST,
        compiler_params=pltpu.CompilerParams(vmem_limit_bytes=56 * 2**20),
        name="filter_late",
    )(req_block, req_count, place, *map(in_hbm, arrived), *tables)


def final_pick():
    shape = (TM * ROWS, 2 * BLOCKW)
    row, column = (lax.broadcasted_iota(jnp.int32, shape, dim) for dim in range(2))
    place = (row // ROWS) * SHARE + row % SHARE + HALF * ((row // 4) % 2) + BLOCKW * ((row // 2) % 2)
    return jnp.where(place == column, 1.0, 0.0).astype(jnp.bfloat16)


def is_active(hop, slot, start_ref, frames_ref, count_ref, place_ref):
    owner = place_ref[0]
    frame = place_ref[1] * HOPS_DEV + hop
    begin = start_ref[owner, slot]
    return (slot < count_ref[owner]) & (frame >= begin) & (frame < begin + frames_ref[owner, slot])


def turn_back(back, pick_ref, turned_ref):
    rows = back.astype(jnp.float32).reshape(TM * ROWS, NFINE).astype(jnp.bfloat16)
    columns = lax.dot_general(rows, pick_ref[...], (((0,), (0,)), ((), ())), preferred_element_type=jnp.float32)
    for m1 in range(RADIX):
        for slot in range(2):
            turned_ref[slot, pl.ds(m1, LANES, stride=RADIX), :] = columns[
                m1 * LANES : (m1 + 1) * LANES, slot * BLOCKW : (slot + 1) * BLOCKW
            ]


def unpack_early_kernel(start_ref, frames_ref, count_ref, place_ref, early_ref, out_ref, turned_ref, pick_ref):
    refs = start_ref, frames_ref, count_ref, place_ref
    step = pl.program_id(0)
    hop, pair = step // (MAXREQ // 2), step % (MAXREQ // 2)

    @pl.when(step == 0)
    def _():
        pick_ref[...] = final_pick()

    @pl.when(is_active(hop, 2 * pair, *refs) | is_active(hop, 2 * pair + 1, *refs))
    def _():
        turn_back(early_ref[:, 0, 0], pick_ref, turned_ref)
        out_ref[0] = turned_ref[...].astype(jnp.bfloat16)


def unpack_kernel(start_ref, frames_ref, count_ref, place_ref, part_ref, late_ref, out_ref, turned_ref, pick_ref):
    refs = start_ref, frames_ref, count_ref, place_ref
    step = pl.program_id(0)
    hop, pair = step // (MAXREQ // 2), step % (MAXREQ // 2)

    @pl.when(step == 0)
    def _():
        pick_ref[...] = final_pick()

    @pl.when(is_active(hop, 2 * pair, *refs) | is_active(hop, 2 * pair + 1, *refs))
    def _():
        turn_back(late_ref[:, hop, pair], pick_ref, turned_ref)

    for which in range(2):
        active = is_active(hop, 2 * pair + which, *refs)

        @pl.when(active)
        def _():
            early = part_ref[0, which]
            late = turned_ref[which].astype(jnp.bfloat16)
            out_ref[0, 0, which, 0] = jnp.concatenate([early[:, :HALF], late[:, :HALF]], axis=1)
            out_ref[0, 0, which, 1] = jnp.concatenate([early[:, HALF:], late[:, HALF:]], axis=1)

        @pl.when(jnp.logical_not(active))
        def _():
            out_ref[0, 0, which] = jnp.zeros((2, NFINE, BLOCKW), jnp.bfloat16)


STEPS = HOPS_DEV * MAXREQ // 2


def unpack_early(early, req_start, req_frames, req_count, place):
    return pl.pallas_call(
        unpack_early_kernel,
        out_shape=jax.ShapeDtypeStruct((STEPS, 2, NFINE, BLOCKW), jnp.bfloat16),
        grid_spec=pltpu.PrefetchScalarGridSpec(
            num_scalar_prefetch=4,
            grid=(STEPS,),
            in_specs=[pl.BlockSpec((TM, 1, 1, ROWS, NFINE), lambda i, *refs: (0, i // (MAXREQ // 2), i % (MAXREQ // 2), 0, 0))],
            out_specs=pl.BlockSpec((1, 2, NFINE, BLOCKW), lambda i, *refs: (i, 0, 0, 0)),
            scratch_shapes=[
                pltpu.VMEM((2, NFINE, BLOCKW), jnp.float32),
                pltpu.VMEM((TM * ROWS, 2 * BLOCKW), jnp.bfloat16),
            ],
        ),
        cost_estimate=COST,
        compiler_params=pltpu.CompilerParams(vmem_limit_bytes=52 * 2**20),
        name="unpack_early",
    )(req_start, req_frames, req_count, place, in_hbm(early))


def unpack(part, late, req_start, req_frames, req_count, place):
    resident = pl.BlockSpec(memory_space=pltpu.VMEM)
    return pl.pallas_call(
        unpack_kernel,
        out_shape=jax.ShapeDtypeStruct((HOPS_DEV, 1, MAXREQ, 2, NFINE, BLOCKW), jnp.bfloat16),
        grid_spec=pltpu.PrefetchScalarGridSpec(
            num_scalar_prefetch=4,
            grid=(STEPS,),
            in_specs=[pl.BlockSpec((1, 2, NFINE, BLOCKW), lambda i, *refs: (i, 0, 0, 0)), resident],
            out_specs=pl.BlockSpec(
                (1, 1, 2, 2, NFINE, BLOCKW),
                lambda i, *refs: (i // (MAXREQ // 2), 0, i % (MAXREQ // 2), 0, 0, 0),
            ),
            scratch_shapes=[
                pltpu.VMEM((2, NFINE, BLOCKW), jnp.float32),
                pltpu.VMEM((TM * ROWS, 2 * BLOCKW), jnp.bfloat16),
            ],
        ),
        compiler_params=pltpu.CompilerParams(vmem_limit_bytes=52 * 2**20),
        name="unpack",
    )(req_start, req_frames, req_count, place, in_hbm(part), in_vmem(late))


def over_tm(array):
    return lax.all_to_all(array, "tm", split_axis=0, concat_axis=0, tiled=True)


def along_chan(arrays):
    return [arrays[0]] + [
        lax.ppermute(in_hbm(arrays[d]), "chan", [(s, (s + d) % OWNERS) for s in range(OWNERS)])
        for d in range(1, OWNERS)
    ]


def shards(coarse, prototype, req_block, req_start, req_frames, req_count):
    column = lax.axis_index("chan").astype(jnp.int32)
    place = jnp.stack([column, lax.axis_index("tm").astype(jnp.int32)])
    tables = (prototype, *(jnp.asarray(table) for table in dft_tables()))
    plan, late, last, *early = pack(coarse, jnp.asarray(late_pick()), req_block, req_count, place)
    late = over_tm(late)
    late, last = lax.optimization_barrier((late, last))
    last = lax.cond(plan[OWNERS] > 0, over_tm, lambda same: same, last)
    early = choose(along_chan(early), jnp.asarray(early_pick()), req_block, req_count, place)
    late, last, early = lax.optimization_barrier((late, last, early))
    early = over_tm(early)
    groups = [
        jnp.where(
            plan[d] < OWNERS - 1,
            lax.dynamic_index_in_dim(late, jnp.minimum(plan[d], OWNERS - 2), 1, keepdims=False),
            last[:, 0],
        )
        for d in range(1, OWNERS)
    ]
    late = along_chan([late] + groups)
    early = filter_early(early, tables)
    _, *late = lax.optimization_barrier((early, *late))
    early = over_tm(early)
    _, late = lax.optimization_barrier((early, filter_late(late, tables, req_block, req_count, place)))
    late = over_tm(late)
    part = unpack_early(early, req_start, req_frames, req_count, place)
    return unpack(part, late, req_start, req_frames, req_count, place)


def solution(mesh):
    return jax.shard_map(
        shards,
        mesh=mesh,
        in_specs=(P(None, "tm", "chan"), P(), P(), P(), P(), P()),
        out_specs=P("tm", "chan", None, None, None, None),
        check_vma=False,
    )
```

```python
import math

import jax
import jax.numpy as jnp
import ml_dtypes
import numpy as np
from jax import lax
from jax.experimental import pallas as pl
from jax.experimental.pallas import tpu as pltpu
from jax.sharding import PartitionSpec as P

BLOCKW = 128
NFINE = 1024
TAPS = 16
HOPS_DEV = 3
MAXREQ = 4
PAIR = 2
TM = 32
OWNERS = 4
BPC = 8
HOPS = 96
HALF = BLOCKW // 2
SHARE = HALF // TM
ROWS = 8
RADIX = 8
LANES = 128
FRAMES = 84
GROUP = 42
COST = pl.CostEstimate(flops=18_000_000_000, transcendentals=0, bytes_accessed=2 * MAXREQ * HOPS * 4 * NFINE * 2)


def share_pick():
    shape = (TM * ROWS, 2 * BLOCKW)
    row, column = (lax.broadcasted_iota(jnp.int32, shape, dim) for dim in range(2))
    place = (row // ROWS) * SHARE + row % SHARE + HALF * ((row // 4) % 2) + BLOCKW * ((row // 2) % 2)
    return jnp.where(place == column, 1.0, 0.0).astype(jnp.bfloat16)


def late_pick():
    shape = (TM * ROWS, PAIR * 2 * BLOCKW)
    row, column = (lax.broadcasted_iota(jnp.int32, shape, dim) for dim in range(2))
    place = HALF + (row // ROWS) * SHARE + row % SHARE + BLOCKW * ((row // 4) % 2) + 2 * BLOCKW * ((row // 2) % 2)
    return jnp.where(place == column, 1.0, 0.0).astype(jnp.bfloat16)


def dft_tables():
    k2 = np.arange(LANES)[None, :, None]
    m = np.arange(RADIX)[:, None, None] + RADIX * np.arange(LANES)[None, None, :]
    angles = (k2 * m % NFINE) * (2.0 * math.pi / NFINE)
    table = np.concatenate([np.cos(angles), np.sin(angles)], axis=2) / math.sqrt(NFINE)
    high = table.astype(np.float32).astype(ml_dtypes.bfloat16)
    low = (table - high.astype(np.float64)).astype(np.float32).astype(ml_dtypes.bfloat16)
    return high, low


def wanted_block(shift, rank, block_ref, count_ref, place_ref):
    owner = (place_ref[0] + shift) % OWNERS
    seen = jnp.int32(0)
    chosen = jnp.int32(0)
    for slot in range(MAXREQ):
        block = block_ref[owner, slot]
        mine = (slot < count_ref[owner]) & (block // BPC == place_ref[0])
        chosen = jnp.where(mine & (seen == rank), block % BPC, chosen)
        seen = seen + mine.astype(jnp.int32)
    return seen > rank, chosen


def some_serves_all(block_ref, count_ref):
    some = jnp.bool_(False)
    for source in range(OWNERS):
        every = jnp.bool_(True)
        for owner in range(OWNERS):
            serves = jnp.bool_(False)
            for slot in range(MAXREQ):
                serves = serves | ((slot < count_ref[owner]) & (block_ref[owner, slot] // BPC == source))
            every = every & serves
        some = some | every
    return some


def pack_kernel(block_ref, count_ref, place_ref, x_ref, *refs):
    plan_ref, late_ref, last_ref, *early_refs = refs[: 3 + OWNERS]
    block_buf, late_buf, early_buf, pick_ref, block_sem, late_sem, early_sem = refs[3 + OWNERS :]
    wanted = [[wanted_block(d, r, block_ref, count_ref, place_ref) for r in range(PAIR)] for d in range(OWNERS)]
    groups = []
    live = jnp.int32(0)
    for d in range(OWNERS):
        groups.append(live)
        plan_ref[d] = live
        live = live + wanted[d][0][0].astype(jnp.int32)

    def block_copy(d, r):
        columns = pl.ds(pl.multiple_of(wanted[d][r][1] * BLOCKW, BLOCKW), BLOCKW)
        return pltpu.make_async_copy(x_ref.at[:, :, columns], block_buf.at[d, r], block_sem.at[d, r])

    def start_late_copy(d):
        @pl.when(groups[d] < OWNERS - 1)
        def _():
            pltpu.make_async_copy(late_buf.at[d], late_ref.at[:, groups[d]], late_sem.at[d]).start()

        @pl.when(groups[d] == OWNERS - 1)
        def _():
            pltpu.make_async_copy(late_buf.at[d], last_ref.at[:, 0], late_sem.at[d]).start()

    def early_copy(d, r):
        return pltpu.make_async_copy(early_buf.at[d, r], early_refs[d].at[r], early_sem.at[d, r])

    order = [(d, r) for d in (1, 2, 3, 0) for r in range(PAIR)]
    for d, r in order:
        pl.when(wanted[d][r][0])(lambda d=d, r=r: block_copy(d, r).start())
    pick_ref[...] = late_pick()
    plan_ref[OWNERS] = some_serves_all(block_ref, count_ref).astype(jnp.int32)
    for d, r in order:
        if r == 0:
            pl.when(wanted[d][0][0])(lambda d=d: block_copy(d, 0).wait())
            continue

        pl.when(wanted[d][1][0])(lambda d=d: block_copy(d, 1).wait())
        for rank in range(PAIR):

            @pl.when(wanted[d][rank][0])
            def _():
                early_buf[d, rank] = jnp.concatenate(
                    [block_buf[d, rank, 0, :, :HALF], block_buf[d, rank, 1, :, :HALF]], axis=1
                ).reshape(HOPS_DEV, NFINE, BLOCKW)
                early_copy(d, rank).start()

        def turn_blocks(d, ranks):
            def one_hop(hop, carry):
                rows = pl.ds(pl.multiple_of(hop * NFINE, NFINE), NFINE)
                wide = jnp.concatenate([block_buf[d, i // 2, i % 2, rows] for i in range(2 * ranks)], axis=1)
                turned = lax.dot_general(
                    pick_ref[:, : 2 * ranks * BLOCKW],
                    wide,
                    (((1,), (1,)), ((), ())),
                    preferred_element_type=jnp.float32,
                )
                late_buf[d, :, hop] = turned.reshape(TM, ROWS, NFINE).astype(jnp.bfloat16)
                return carry

            lax.fori_loop(0, HOPS_DEV, one_hop, 0)
            start_late_copy(d)

        pl.when(wanted[d][1][0])(lambda d=d: turn_blocks(d, 2))
        pl.when(wanted[d][0][0] & jnp.logical_not(wanted[d][1][0]))(lambda d=d: turn_blocks(d, 1))

    for d, r in order:
        pl.when(wanted[d][r][0])(lambda d=d, r=r: early_copy(d, r).wait())
        if r == 0:
            pl.when(wanted[d][0][0])(
                lambda d=d: pltpu.make_async_copy(late_buf.at[d], last_ref.at[:, 0], late_sem.at[d]).wait()
            )


def pack(coarse, req_block, req_count, place):
    anywhere = pl.BlockSpec(memory_space=pl.ANY)
    early = jax.ShapeDtypeStruct((PAIR, HOPS_DEV, NFINE, BLOCKW), jnp.bfloat16)
    return pl.pallas_call(
        pack_kernel,
        out_shape=[
            jax.ShapeDtypeStruct((OWNERS + 1,), jnp.int32),
            jax.ShapeDtypeStruct((TM, OWNERS - 1, HOPS_DEV, ROWS, NFINE), jnp.bfloat16),
            jax.ShapeDtypeStruct((TM, 1, HOPS_DEV, ROWS, NFINE), jnp.bfloat16),
        ]
        + [early] * OWNERS,
        grid_spec=pltpu.PrefetchScalarGridSpec(
            num_scalar_prefetch=3,
            grid=(1,),
            in_specs=[anywhere],
            out_specs=[pl.BlockSpec(memory_space=pltpu.SMEM)] + [anywhere] * (2 + OWNERS),
            scratch_shapes=[
                pltpu.VMEM((OWNERS, PAIR, 2, HOPS_DEV * NFINE, BLOCKW), jnp.bfloat16),
                pltpu.VMEM((OWNERS, TM, HOPS_DEV, ROWS, NFINE), jnp.bfloat16),
                pltpu.VMEM((OWNERS, PAIR, HOPS_DEV, NFINE, BLOCKW), jnp.bfloat16),
                pltpu.VMEM((TM * ROWS, PAIR * 2 * BLOCKW), jnp.bfloat16),
                pltpu.SemaphoreType.DMA((OWNERS, PAIR)),
                pltpu.SemaphoreType.DMA((OWNERS,)),
                pltpu.SemaphoreType.DMA((OWNERS, PAIR)),
            ],
        ),
        name="pack",
    )(req_block, req_count, place, coarse)


def in_vmem(array):
    return pltpu.with_memory_space_constraint(array, pltpu.VMEM)


def in_hbm(array):
    return pltpu.with_memory_space_constraint(array, pltpu.HBM)


def split_kernel(plan_ref, late_ref, last_ref, *refs):
    out_refs, sem = refs[:-1], refs[-1]
    for d, out_ref in enumerate(out_refs, 1):
        group = plan_ref[d]

        @pl.when(group < OWNERS - 1)
        def _():
            pltpu.make_async_copy(late_ref.at[:, group], out_ref, sem.at[d]).start()

        @pl.when(group >= OWNERS - 1)
        def _():
            pltpu.make_async_copy(last_ref.at[:, 0], out_ref, sem.at[d]).start()

    for d, out_ref in enumerate(out_refs, 1):
        pltpu.make_async_copy(last_ref.at[:, 0], out_ref, sem.at[d]).wait()


def split(plan, late, last):
    anywhere = pl.BlockSpec(memory_space=pl.ANY)
    return pl.pallas_call(
        split_kernel,
        out_shape=[jax.ShapeDtypeStruct((TM, HOPS_DEV, ROWS, NFINE), jnp.bfloat16)] * (OWNERS - 1),
        grid_spec=pltpu.PrefetchScalarGridSpec(
            num_scalar_prefetch=1,
            grid=(1,),
            in_specs=[anywhere] * 2,
            out_specs=[anywhere] * (OWNERS - 1),
            scratch_shapes=[pltpu.SemaphoreType.DMA((OWNERS,))],
        ),
        name="split",
    )(plan, in_hbm(late), in_hbm(last))


def arrival(slot, block_ref, count_ref, place_ref):
    owner = place_ref[0]
    slot = jnp.where(slot < count_ref[owner], slot, 0)
    source = block_ref[owner, slot] // BPC
    rank = jnp.int32(0)
    for other in range(MAXREQ - 1):
        same = (other < slot) & (block_ref[owner, other] // BPC == source)
        rank = rank + same.astype(jnp.int32)
    return (owner - source + OWNERS) % OWNERS, jnp.minimum(rank, PAIR - 1)


def choose_kernel(block_ref, count_ref, place_ref, a0, a1, a2, a3, out_ref, held_ref, out_buf, pick_ref, held_sem, out_sem):
    for slot in range(MAXREQ):
        shift, rank = arrival(slot, block_ref, count_ref, place_ref)
        for own, ref in enumerate((a0, a1, a2, a3)):

            @pl.when(shift == own)
            def _():
                pltpu.make_async_copy(ref.at[rank], held_ref.at[slot], held_sem.at[slot]).start()

    pick_ref[...] = share_pick()

    def out_copy(pair, hop):
        return pltpu.make_async_copy(out_buf.at[pair, hop], out_ref.at[:, pair, hop], out_sem.at[pair, hop])

    for pair in range(MAXREQ // 2):
        for slot in (2 * pair, 2 * pair + 1):
            pltpu.make_async_copy(a0.at[0], held_ref.at[slot], held_sem.at[slot]).wait()
        for hop in range(HOPS_DEV):
            both = jnp.concatenate([held_ref[pair * 2, hop], held_ref[pair * 2 + 1, hop]], axis=1)
            turned = lax.dot_general(
                pick_ref[...], both, (((1,), (1,)), ((), ())), preferred_element_type=jnp.float32
            )
            out_buf[pair, hop] = turned.reshape(TM, ROWS, NFINE).astype(jnp.bfloat16)
            out_copy(pair, hop).start()
    for pair in range(MAXREQ // 2):
        for hop in range(HOPS_DEV):
            out_copy(pair, hop).wait()


def choose(arrived, req_block, req_count, place):
    anywhere = pl.BlockSpec(memory_space=pl.ANY)
    return pl.pallas_call(
        choose_kernel,
        out_shape=jax.ShapeDtypeStruct((TM, MAXREQ // 2, HOPS_DEV, ROWS, NFINE), jnp.bfloat16),
        grid_spec=pltpu.PrefetchScalarGridSpec(
            num_scalar_prefetch=3,
            grid=(1,),
            in_specs=[anywhere] * OWNERS,
            out_specs=anywhere,
            scratch_shapes=[
                pltpu.VMEM((MAXREQ, HOPS_DEV, NFINE, BLOCKW), jnp.bfloat16),
                pltpu.VMEM((MAXREQ // 2, HOPS_DEV, TM, ROWS, NFINE), jnp.bfloat16),
                pltpu.VMEM((TM * ROWS, 2 * BLOCKW), jnp.bfloat16),
                pltpu.SemaphoreType.DMA((MAXREQ,)),
                pltpu.SemaphoreType.DMA((MAXREQ // 2, HOPS_DEV)),
            ],
        ),
        cost_estimate=pl.CostEstimate(flops=150_000_000_000, transcendentals=0, bytes_accessed=2**22),
        name="choose",
    )(req_block, req_count, place, *map(in_hbm, arrived))


def turn(value, sign):
    return pltpu.roll(value, ROWS // 2, value.ndim - 2) * sign


def dft4(a, b, c, d, sign):
    s02, d02, s13, d13 = a + c, a - c, b + d, turn(b - d, sign)
    return s02 + s13, d02 + d13, s02 - s13, d02 - d13


def dft8(x, sign):
    half = math.sqrt(0.5)
    low = [x[i] + x[i + 4] for i in range(4)]
    high = [x[i] - x[i + 4] for i in range(4)]
    high[1] = (high[1] + turn(high[1], sign)) * half
    high[2] = turn(high[2], sign)
    high[3] = (turn(high[3], sign) - high[3]) * half
    even, odd = dft4(*low, sign), dft4(*high, sign)
    return [pair for both in zip(even, odd) for pair in both]


def transform(load, proto_ref, high_ref, low_ref, out_ref, wide_ref, fir_ref):
    sign = jnp.where(lax.broadcasted_iota(jnp.int32, (ROWS, LANES), 0) < ROWS // 2, 1.0, -1.0)
    wide_ref[:, HOPS:] = jnp.zeros((RADIX, FRAMES + TAPS - 1 - HOPS, ROWS, LANES), jnp.float32)

    def widen(tile, carry):
        wide_ref[tile, :HOPS] = load(pl.ds(pl.multiple_of(tile * LANES, LANES), LANES))
        return carry

    lax.fori_loop(0, RADIX, widen, 0)

    def one_group(group):
        first = group * GROUP
        for tile in range(RADIX):
            lanes = slice(tile * LANES, (tile + 1) * LANES)
            total = None
            for tap in range(TAPS):
                weights = jnp.broadcast_to(proto_ref[tap, lanes].reshape(1, LANES), (ROWS, LANES))
                part = wide_ref[tile, pl.ds(first + tap, GROUP)] * weights
                total = part if total is None else total + part
            fir_ref[group, tile] = total
        for frame in range(0, GROUP, 2):
            parts = [fir_ref[group, tile, frame : frame + 2] for tile in range(RADIX)]
            for m1, value in enumerate(dft8(parts, sign)):
                fir_ref[group, m1, frame : frame + 2] = value
        for m1 in range(RADIX):
            value = fir_ref[group, m1].reshape(GROUP * ROWS, LANES)
            top = value.astype(jnp.bfloat16)
            rest = (value - top.astype(jnp.float32)).astype(jnp.bfloat16)
            high = high_ref[m1]
            product = jnp.dot(
                jnp.concatenate([top, rest, top], axis=1),
                jnp.concatenate([high, high, low_ref[m1]], axis=0),
                preferred_element_type=jnp.float32,
            )
            cosines = product[:, :LANES].reshape(GROUP, ROWS, LANES)
            sines = product[:, LANES:].reshape(GROUP, ROWS, LANES)
            result = (cosines + turn(sines, sign)).astype(jnp.bfloat16)
            devices = GROUP // HOPS_DEV
            out_ref[pl.ds(group * devices, devices), :, 0, :, m1 * LANES : (m1 + 1) * LANES] = result.reshape(
                devices, HOPS_DEV, ROWS, LANES
            )

    for group in range(FRAMES // GROUP):
        one_group(group)


def early_kernel(x_ref, *refs):
    pair = pl.program_id(0)

    def load(lanes):
        return x_ref[:, pair, :, :, lanes].astype(jnp.float32).reshape(HOPS, ROWS, LANES)

    transform(load, *refs)


def late_kernel(block_ref, count_ref, place_ref, a0, a1, a2, a3, proto_ref, high_ref, low_ref, out_ref, wide_ref, fir_ref, held_ref, sem):
    pair = pl.program_id(0)

    @pl.when(pair == 0)
    def _():
        for slot in range(MAXREQ):
            shift, _ = arrival(slot, block_ref, count_ref, place_ref)
            for own, ref in enumerate((a0.at[:, 0], a1, a2, a3)):

                @pl.when(shift == own)
                def _():
                    pltpu.make_async_copy(ref, held_ref.at[slot], sem.at[slot]).start()

    for slot in range(2):
        at = pair * 2 + slot
        pltpu.make_async_copy(a1, held_ref.at[at], sem.at[at]).wait()

    ranks = [arrival(slot, block_ref, count_ref, place_ref)[1] for slot in range(MAXREQ)]
    first_rank = jnp.where(pair == 0, ranks[0], ranks[2])
    second_rank = jnp.where(pair == 0, ranks[1], ranks[3])
    is_second = (lax.broadcasted_iota(jnp.int32, (HOPS, ROWS, LANES), 1) // SHARE) % 2 == 1

    def load(lanes):
        first = held_ref[pair * 2, :, :, :, lanes].astype(jnp.float32).reshape(HOPS, ROWS, LANES)
        second = held_ref[pair * 2 + 1, :, :, :, lanes].astype(jnp.float32).reshape(HOPS, ROWS, LANES)
        first = jnp.where(first_rank == 0, first, pltpu.roll(first, ROWS - SHARE, 1))
        second = jnp.where(second_rank == 1, second, pltpu.roll(second, SHARE, 1))
        return jnp.where(is_second, second, first)

    transform(load, proto_ref, high_ref, low_ref, out_ref, wide_ref, fir_ref)


def table_specs():
    return [
        pl.BlockSpec((TAPS, NFINE), lambda p, *refs: (0, 0)),
        pl.BlockSpec((RADIX, LANES, 2 * LANES), lambda p, *refs: (0, 0, 0)),
        pl.BlockSpec((RADIX, LANES, 2 * LANES), lambda p, *refs: (0, 0, 0)),
    ]


RESULT = jax.ShapeDtypeStruct((TM, HOPS_DEV, MAXREQ // 2, ROWS, NFINE), jnp.bfloat16)


def result_spec():
    return pl.BlockSpec((TM, HOPS_DEV, 1, ROWS, NFINE), lambda p, *refs: (0, 0, p, 0, 0))


def work_space():
    return [
        pltpu.VMEM((RADIX, FRAMES + TAPS - 1, ROWS, LANES), jnp.float32),
        pltpu.VMEM((FRAMES // GROUP, RADIX, GROUP, ROWS, LANES), jnp.float32),
    ]


def filter_early(gathered, tables):
    return pl.pallas_call(
        early_kernel,
        out_shape=RESULT,
        grid=(MAXREQ // 2,),
        in_specs=[
            pl.BlockSpec(memory_space=pltpu.VMEM),
            *table_specs(),
        ],
        out_specs=result_spec(),
        scratch_shapes=work_space(),
        cost_estimate=COST,
        name="filter_early",
    )(in_vmem(gathered), *tables)


def filter_late(arrived, tables, req_block, req_count, place):
    return pl.pallas_call(
        late_kernel,
        out_shape=RESULT,
        grid_spec=pltpu.PrefetchScalarGridSpec(
            num_scalar_prefetch=3,
            grid=(MAXREQ // 2,),
            in_specs=[pl.BlockSpec(memory_space=pl.ANY)] * OWNERS + table_specs(),
            out_specs=result_spec(),
            scratch_shapes=work_space()
            + [
                pltpu.VMEM((MAXREQ, TM, HOPS_DEV, ROWS, NFINE), jnp.bfloat16),
                pltpu.SemaphoreType.DMA((MAXREQ,)),
            ],
        ),
        cost_estimate=COST,
        compiler_params=pltpu.CompilerParams(vmem_limit_bytes=56 * 2**20),
        name="filter_late",
    )(req_block, req_count, place, *map(in_hbm, arrived), *tables)


def is_active(hop, slot, start_ref, frames_ref, count_ref, place_ref):
    owner = place_ref[0]
    frame = place_ref[1] * HOPS_DEV + hop
    begin = start_ref[owner, slot]
    return (slot < count_ref[owner]) & (frame >= begin) & (frame < begin + frames_ref[owner, slot])


def turn_back(back, pick_ref, turned_ref):
    rows = back.astype(jnp.float32).reshape(TM * ROWS, NFINE).astype(jnp.bfloat16)
    columns = lax.dot_general(rows, pick_ref[...], (((0,), (0,)), ((), ())), preferred_element_type=jnp.float32)
    for m1 in range(RADIX):
        for slot in range(2):
            turned_ref[slot, pl.ds(m1, LANES, stride=RADIX), :] = columns[
                m1 * LANES : (m1 + 1) * LANES, slot * BLOCKW : (slot + 1) * BLOCKW
            ]


def unpack_early_kernel(start_ref, frames_ref, count_ref, place_ref, early_ref, out_ref, turned_ref, pick_ref):
    refs = start_ref, frames_ref, count_ref, place_ref
    step = pl.program_id(0)
    hop, pair = step // (MAXREQ // 2), step % (MAXREQ // 2)

    @pl.when(step == 0)
    def _():
        pick_ref[...] = share_pick()

    @pl.when(is_active(hop, 2 * pair, *refs) | is_active(hop, 2 * pair + 1, *refs))
    def _():
        turn_back(early_ref[:, 0, 0], pick_ref, turned_ref)
        out_ref[0] = turned_ref[...].astype(jnp.bfloat16)


def unpack_kernel(start_ref, frames_ref, count_ref, place_ref, part_ref, late_ref, out_ref, turned_ref, pick_ref):
    refs = start_ref, frames_ref, count_ref, place_ref
    step = pl.program_id(0)
    hop, pair = step // (MAXREQ // 2), step % (MAXREQ // 2)

    @pl.when(step == 0)
    def _():
        pick_ref[...] = share_pick()

    @pl.when(is_active(hop, 2 * pair, *refs) | is_active(hop, 2 * pair + 1, *refs))
    def _():
        turn_back(late_ref[:, hop, pair], pick_ref, turned_ref)

    for which in range(2):
        active = is_active(hop, 2 * pair + which, *refs)

        @pl.when(active)
        def _():
            early = part_ref[0, which]
            late = turned_ref[which].astype(jnp.bfloat16)
            out_ref[0, 0, which, 0] = jnp.concatenate([early[:, :HALF], late[:, :HALF]], axis=1)
            out_ref[0, 0, which, 1] = jnp.concatenate([early[:, HALF:], late[:, HALF:]], axis=1)

        @pl.when(jnp.logical_not(active))
        def _():
            out_ref[0, 0, which] = jnp.zeros((2, NFINE, BLOCKW), jnp.bfloat16)


STEPS = HOPS_DEV * MAXREQ // 2


def unpack_early(early, req_start, req_frames, req_count, place):
    return pl.pallas_call(
        unpack_early_kernel,
        out_shape=jax.ShapeDtypeStruct((STEPS, 2, NFINE, BLOCKW), jnp.bfloat16),
        grid_spec=pltpu.PrefetchScalarGridSpec(
            num_scalar_prefetch=4,
            grid=(STEPS,),
            in_specs=[pl.BlockSpec((TM, 1, 1, ROWS, NFINE), lambda i, *refs: (0, i // (MAXREQ // 2), i % (MAXREQ // 2), 0, 0))],
            out_specs=pl.BlockSpec((1, 2, NFINE, BLOCKW), lambda i, *refs: (i, 0, 0, 0)),
            scratch_shapes=[
                pltpu.VMEM((2, NFINE, BLOCKW), jnp.float32),
                pltpu.VMEM((TM * ROWS, 2 * BLOCKW), jnp.bfloat16),
            ],
        ),
        cost_estimate=COST,
        compiler_params=pltpu.CompilerParams(vmem_limit_bytes=52 * 2**20),
        name="unpack_early",
    )(req_start, req_frames, req_count, place, in_hbm(early))


def unpack(part, late, req_start, req_frames, req_count, place):
    resident = pl.BlockSpec(memory_space=pltpu.VMEM)
    return pl.pallas_call(
        unpack_kernel,
        out_shape=jax.ShapeDtypeStruct((HOPS_DEV, 1, MAXREQ, 2, NFINE, BLOCKW), jnp.bfloat16),
        grid_spec=pltpu.PrefetchScalarGridSpec(
            num_scalar_prefetch=4,
            grid=(STEPS,),
            in_specs=[pl.BlockSpec((1, 2, NFINE, BLOCKW), lambda i, *refs: (i, 0, 0, 0)), resident],
            out_specs=pl.BlockSpec(
                (1, 1, 2, 2, NFINE, BLOCKW),
                lambda i, *refs: (i // (MAXREQ // 2), 0, i % (MAXREQ // 2), 0, 0, 0),
            ),
            scratch_shapes=[
                pltpu.VMEM((2, NFINE, BLOCKW), jnp.float32),
                pltpu.VMEM((TM * ROWS, 2 * BLOCKW), jnp.bfloat16),
            ],
        ),
        compiler_params=pltpu.CompilerParams(vmem_limit_bytes=52 * 2**20),
        name="unpack",
    )(req_start, req_frames, req_count, place, in_hbm(part), in_vmem(late))


def over_tm(array):
    return lax.all_to_all(array, "tm", split_axis=0, concat_axis=0, tiled=True)


def along_chan(arrays):
    return [arrays[0]] + [
        lax.ppermute(in_hbm(arrays[d]), "chan", [(s, (s + d) % OWNERS) for s in range(OWNERS)])
        for d in range(1, OWNERS)
    ]


def shards(coarse, prototype, req_block, req_start, req_frames, req_count):
    column = lax.axis_index("chan").astype(jnp.int32)
    place = jnp.stack([column, lax.axis_index("tm").astype(jnp.int32)])
    tables = (prototype, *(jnp.asarray(table) for table in dft_tables()))
    plan, late, last, *early = pack(coarse, req_block, req_count, place)
    late = over_tm(late)
    late, last = lax.optimization_barrier((late, last))
    last = lax.cond(plan[OWNERS] > 0, over_tm, lambda same: same, last)
    early = choose(along_chan(early), req_block, req_count, place)
    late, last, early = lax.optimization_barrier((late, last, early))
    early = over_tm(early)
    late = along_chan([late, *split(plan, late, last)])
    early = filter_early(early, tables)
    _, *late = lax.optimization_barrier((early, *late))
    early = over_tm(early)
    _, late = lax.optimization_barrier((early, filter_late(late, tables, req_block, req_count, place)))
    late = over_tm(late)
    part = unpack_early(early, req_start, req_frames, req_count, place)
    return unpack(part, late, req_start, req_frames, req_count, place)


def solution(mesh):
    return jax.shard_map(
        shards,
        mesh=mesh,
        in_specs=(P(None, "tm", "chan"), P(), P(), P(), P(), P()),
        out_specs=P("tm", "chan", None, None, None, None),
        check_vma=False,
    )
```

```python
import math

import jax
import jax.numpy as jnp
import ml_dtypes
import numpy as np
from jax import lax
from jax.experimental import pallas as pl
from jax.experimental.pallas import tpu as pltpu
from jax.sharding import PartitionSpec as P

BLOCKW = 128
NFINE = 1024
TAPS = 16
HOPS_DEV = 3
MAXREQ = 4
PAIR = 2
TM = 32
OWNERS = 4
BPC = 8
HOPS = 96
HALF = BLOCKW // 2
SHARE = HALF // TM
ROWS = 8
RADIX = 8
LANES = 128
FRAMES = 84
GROUP = 42
COST = pl.CostEstimate(flops=18_000_000_000, transcendentals=0, bytes_accessed=2 * MAXREQ * HOPS * 4 * NFINE * 2)


def share_pick():
    shape = (TM * ROWS, 2 * BLOCKW)
    row, column = (lax.broadcasted_iota(jnp.int32, shape, dim) for dim in range(2))
    place = (row // ROWS) * SHARE + row % SHARE + HALF * ((row // 4) % 2) + BLOCKW * ((row // 2) % 2)
    return jnp.where(place == column, 1.0, 0.0).astype(jnp.bfloat16)


def late_pick():
    shape = (TM * ROWS, PAIR * 2 * BLOCKW)
    row, column = (lax.broadcasted_iota(jnp.int32, shape, dim) for dim in range(2))
    place = HALF + (row // ROWS) * SHARE + row % SHARE + BLOCKW * ((row // 4) % 2) + 2 * BLOCKW * ((row // 2) % 2)
    return jnp.where(place == column, 1.0, 0.0).astype(jnp.bfloat16)


def dft_tables():
    k2 = np.arange(LANES)[None, :, None]
    m = np.arange(RADIX)[:, None, None] + RADIX * np.arange(LANES)[None, None, :]
    angles = (k2 * m % NFINE) * (2.0 * math.pi / NFINE)
    table = np.concatenate([np.cos(angles), np.sin(angles)], axis=2) / math.sqrt(NFINE)
    high = table.astype(np.float32).astype(ml_dtypes.bfloat16)
    low = (table - high.astype(np.float64)).astype(np.float32).astype(ml_dtypes.bfloat16)
    return high, low


def wanted_block(shift, rank, block_ref, count_ref, place_ref):
    owner = (place_ref[0] + shift) % OWNERS
    seen = jnp.int32(0)
    chosen = jnp.int32(0)
    for slot in range(MAXREQ):
        block = block_ref[owner, slot]
        mine = (slot < count_ref[owner]) & (block // BPC == place_ref[0])
        chosen = jnp.where(mine & (seen == rank), block % BPC, chosen)
        seen = seen + mine.astype(jnp.int32)
    return seen > rank, chosen


def some_serves_all(block_ref, count_ref):
    some = jnp.bool_(False)
    for source in range(OWNERS):
        every = jnp.bool_(True)
        for owner in range(OWNERS):
            serves = jnp.bool_(False)
            for slot in range(MAXREQ):
                serves = serves | ((slot < count_ref[owner]) & (block_ref[owner, slot] // BPC == source))
            every = every & serves
        some = some | every
    return some


def pack_kernel(block_ref, count_ref, place_ref, x_ref, *refs):
    plan_ref, late_ref, last_ref, *early_refs = refs[: 3 + OWNERS]
    block_buf, late_buf, early_buf, pick_ref, block_sem, late_sem, early_sem = refs[3 + OWNERS :]
    wanted = [[wanted_block(d, r, block_ref, count_ref, place_ref) for r in range(PAIR)] for d in range(OWNERS)]
    groups = []
    live = jnp.int32(0)
    for d in range(OWNERS):
        groups.append(live)
        plan_ref[d] = live
        live = live + wanted[d][0][0].astype(jnp.int32)

    def block_copy(d, r):
        columns = pl.ds(pl.multiple_of(wanted[d][r][1] * BLOCKW, BLOCKW), BLOCKW)
        return pltpu.make_async_copy(x_ref.at[:, :, columns], block_buf.at[d, r], block_sem.at[d, r])

    def start_late_copy(d):
        @pl.when(groups[d] < OWNERS - 1)
        def _():
            pltpu.make_async_copy(late_buf.at[d], late_ref.at[:, groups[d]], late_sem.at[d]).start()

        @pl.when(groups[d] == OWNERS - 1)
        def _():
            pltpu.make_async_copy(late_buf.at[d], last_ref.at[:, 0], late_sem.at[d]).start()

    def early_copy(d, r):
        return pltpu.make_async_copy(early_buf.at[d, r], early_refs[d].at[r], early_sem.at[d, r])

    order = [(d, r) for d in (1, 2, 3, 0) for r in range(PAIR)]
    for d, r in order:
        pl.when(wanted[d][r][0])(lambda d=d, r=r: block_copy(d, r).start())
    pick_ref[...] = late_pick()
    plan_ref[OWNERS] = some_serves_all(block_ref, count_ref).astype(jnp.int32)
    for d, r in order:
        if r == 0:
            pl.when(wanted[d][0][0])(lambda d=d: block_copy(d, 0).wait())
            continue

        pl.when(wanted[d][1][0])(lambda d=d: block_copy(d, 1).wait())
        for rank in range(PAIR):

            @pl.when(wanted[d][rank][0])
            def _():
                early_buf[d, rank] = jnp.concatenate(
                    [block_buf[d, rank, 0, :, :HALF], block_buf[d, rank, 1, :, :HALF]], axis=1
                ).reshape(HOPS_DEV, NFINE, BLOCKW)
                early_copy(d, rank).start()

        def turn_blocks(d, ranks):
            def one_hop(hop, carry):
                rows = pl.ds(pl.multiple_of(hop * NFINE, NFINE), NFINE)
                wide = jnp.concatenate([block_buf[d, i // 2, i % 2, rows] for i in range(2 * ranks)], axis=1)
                turned = lax.dot_general(
                    pick_ref[:, : 2 * ranks * BLOCKW],
                    wide,
                    (((1,), (1,)), ((), ())),
                    preferred_element_type=jnp.float32,
                )
                late_buf[d, :, hop] = turned.reshape(TM, ROWS, NFINE).astype(jnp.bfloat16)
                return carry

            lax.fori_loop(0, HOPS_DEV, one_hop, 0)
            start_late_copy(d)

        pl.when(wanted[d][1][0])(lambda d=d: turn_blocks(d, 2))
        pl.when(wanted[d][0][0] & jnp.logical_not(wanted[d][1][0]))(lambda d=d: turn_blocks(d, 1))

    for d, r in order:
        pl.when(wanted[d][r][0])(lambda d=d, r=r: early_copy(d, r).wait())
        if r == 0:
            pl.when(wanted[d][0][0])(
                lambda d=d: pltpu.make_async_copy(late_buf.at[d], last_ref.at[:, 0], late_sem.at[d]).wait()
            )


def pack(coarse, req_block, req_count, place):
    anywhere = pl.BlockSpec(memory_space=pl.ANY)
    early = jax.ShapeDtypeStruct((PAIR, HOPS_DEV, NFINE, BLOCKW), jnp.bfloat16)
    return pl.pallas_call(
        pack_kernel,
        out_shape=[
            jax.ShapeDtypeStruct((OWNERS + 1,), jnp.int32),
            jax.ShapeDtypeStruct((TM, OWNERS - 1, HOPS_DEV, ROWS, NFINE), jnp.bfloat16),
            jax.ShapeDtypeStruct((TM, 1, HOPS_DEV, ROWS, NFINE), jnp.bfloat16),
        ]
        + [early] * OWNERS,
        grid_spec=pltpu.PrefetchScalarGridSpec(
            num_scalar_prefetch=3,
            grid=(1,),
            in_specs=[anywhere],
            out_specs=[pl.BlockSpec(memory_space=pltpu.SMEM)] + [anywhere] * (2 + OWNERS),
            scratch_shapes=[
                pltpu.VMEM((OWNERS, PAIR, 2, HOPS_DEV * NFINE, BLOCKW), jnp.bfloat16),
                pltpu.VMEM((OWNERS, TM, HOPS_DEV, ROWS, NFINE), jnp.bfloat16),
                pltpu.VMEM((OWNERS, PAIR, HOPS_DEV, NFINE, BLOCKW), jnp.bfloat16),
                pltpu.VMEM((TM * ROWS, PAIR * 2 * BLOCKW), jnp.bfloat16),
                pltpu.SemaphoreType.DMA((OWNERS, PAIR)),
                pltpu.SemaphoreType.DMA((OWNERS,)),
                pltpu.SemaphoreType.DMA((OWNERS, PAIR)),
            ],
        ),
        name="pack",
    )(req_block, req_count, place, coarse)


def in_vmem(array):
    return pltpu.with_memory_space_constraint(array, pltpu.VMEM)


def in_hbm(array):
    return pltpu.with_memory_space_constraint(array, pltpu.HBM)


def split_kernel(plan_ref, late_ref, last_ref, *refs):
    *out_refs, held_ref, in_sem, out_sem = refs
    for d in range(1, OWNERS):
        group = plan_ref[d]

        @pl.when(group < OWNERS - 1)
        def _():
            pltpu.make_async_copy(late_ref.at[:, group], held_ref.at[d - 1], in_sem.at[d - 1]).start()

        @pl.when(group >= OWNERS - 1)
        def _():
            pltpu.make_async_copy(last_ref.at[:, 0], held_ref.at[d - 1], in_sem.at[d - 1]).start()

    for at, out_ref in enumerate(out_refs):
        pltpu.make_async_copy(last_ref.at[:, 0], held_ref.at[at], in_sem.at[at]).wait()
        pltpu.make_async_copy(held_ref.at[at], out_ref, out_sem.at[at]).start()
    for at, out_ref in enumerate(out_refs):
        pltpu.make_async_copy(held_ref.at[at], out_ref, out_sem.at[at]).wait()


def split(plan, late, last):
    anywhere = pl.BlockSpec(memory_space=pl.ANY)
    return pl.pallas_call(
        split_kernel,
        out_shape=[jax.ShapeDtypeStruct((TM, HOPS_DEV, ROWS, NFINE), jnp.bfloat16)] * (OWNERS - 1),
        grid_spec=pltpu.PrefetchScalarGridSpec(
            num_scalar_prefetch=1,
            grid=(1,),
            in_specs=[anywhere] * 2,
            out_specs=[anywhere] * (OWNERS - 1),
            scratch_shapes=[
                pltpu.VMEM((OWNERS - 1, TM, HOPS_DEV, ROWS, NFINE), jnp.bfloat16),
                pltpu.SemaphoreType.DMA((OWNERS - 1,)),
                pltpu.SemaphoreType.DMA((OWNERS - 1,)),
            ],
        ),
        name="split",
    )(plan, in_hbm(late), in_hbm(last))


def arrival(slot, block_ref, count_ref, place_ref):
    owner = place_ref[0]
    slot = jnp.where(slot < count_ref[owner], slot, 0)
    source = block_ref[owner, slot] // BPC
    rank = jnp.int32(0)
    for other in range(MAXREQ - 1):
        same = (other < slot) & (block_ref[owner, other] // BPC == source)
        rank = rank + same.astype(jnp.int32)
    return (owner - source + OWNERS) % OWNERS, jnp.minimum(rank, PAIR - 1)


def choose_kernel(block_ref, count_ref, place_ref, a0, a1, a2, a3, out_ref, held_ref, out_buf, pick_ref, held_sem, out_sem):
    for slot in range(MAXREQ):
        shift, rank = arrival(slot, block_ref, count_ref, place_ref)
        for own, ref in enumerate((a0, a1, a2, a3)):

            @pl.when(shift == own)
            def _():
                pltpu.make_async_copy(ref.at[rank], held_ref.at[slot], held_sem.at[slot]).start()

    pick_ref[...] = share_pick()

    def out_copy(pair, hop):
        return pltpu.make_async_copy(out_buf.at[pair, hop], out_ref.at[:, pair, hop], out_sem.at[pair, hop])

    for pair in range(MAXREQ // 2):
        for slot in (2 * pair, 2 * pair + 1):
            pltpu.make_async_copy(a0.at[0], held_ref.at[slot], held_sem.at[slot]).wait()
        for hop in range(HOPS_DEV):
            both = jnp.concatenate([held_ref[pair * 2, hop], held_ref[pair * 2 + 1, hop]], axis=1)
            turned = lax.dot_general(
                pick_ref[...], both, (((1,), (1,)), ((), ())), preferred_element_type=jnp.float32
            )
            out_buf[pair, hop] = turned.reshape(TM, ROWS, NFINE).astype(jnp.bfloat16)
            out_copy(pair, hop).start()
    for pair in range(MAXREQ // 2):
        for hop in range(HOPS_DEV):
            out_copy(pair, hop).wait()


def choose(arrived, req_block, req_count, place):
    anywhere = pl.BlockSpec(memory_space=pl.ANY)
    return pl.pallas_call(
        choose_kernel,
        out_shape=jax.ShapeDtypeStruct((TM, MAXREQ // 2, HOPS_DEV, ROWS, NFINE), jnp.bfloat16),
        grid_spec=pltpu.PrefetchScalarGridSpec(
            num_scalar_prefetch=3,
            grid=(1,),
            in_specs=[anywhere] * OWNERS,
            out_specs=anywhere,
            scratch_shapes=[
                pltpu.VMEM((MAXREQ, HOPS_DEV, NFINE, BLOCKW), jnp.bfloat16),
                pltpu.VMEM((MAXREQ // 2, HOPS_DEV, TM, ROWS, NFINE), jnp.bfloat16),
                pltpu.VMEM((TM * ROWS, 2 * BLOCKW), jnp.bfloat16),
                pltpu.SemaphoreType.DMA((MAXREQ,)),
                pltpu.SemaphoreType.DMA((MAXREQ // 2, HOPS_DEV)),
            ],
        ),
        cost_estimate=pl.CostEstimate(flops=150_000_000_000, transcendentals=0, bytes_accessed=2**22),
        name="choose",
    )(req_block, req_count, place, *map(in_hbm, arrived))


def turn(value, sign):
    return pltpu.roll(value, ROWS // 2, value.ndim - 2) * sign


def dft4(a, b, c, d, sign):
    s02, d02, s13, d13 = a + c, a - c, b + d, turn(b - d, sign)
    return s02 + s13, d02 + d13, s02 - s13, d02 - d13


def dft8(x, sign):
    half = math.sqrt(0.5)
    low = [x[i] + x[i + 4] for i in range(4)]
    high = [x[i] - x[i + 4] for i in range(4)]
    high[1] = (high[1] + turn(high[1], sign)) * half
    high[2] = turn(high[2], sign)
    high[3] = (turn(high[3], sign) - high[3]) * half
    even, odd = dft4(*low, sign), dft4(*high, sign)
    return [pair for both in zip(even, odd) for pair in both]


def transform(load, proto_ref, high_ref, low_ref, out_ref, wide_ref, fir_ref):
    sign = jnp.where(lax.broadcasted_iota(jnp.int32, (ROWS, LANES), 0) < ROWS // 2, 1.0, -1.0)
    wide_ref[:, HOPS:] = jnp.zeros((RADIX, FRAMES + TAPS - 1 - HOPS, ROWS, LANES), jnp.float32)

    def widen(tile, carry):
        wide_ref[tile, :HOPS] = load(pl.ds(pl.multiple_of(tile * LANES, LANES), LANES))
        return carry

    lax.fori_loop(0, RADIX, widen, 0)

    def one_group(group):
        first = group * GROUP
        for tile in range(RADIX):
            lanes = slice(tile * LANES, (tile + 1) * LANES)
            total = None
            for tap in range(TAPS):
                weights = jnp.broadcast_to(proto_ref[tap, lanes].reshape(1, LANES), (ROWS, LANES))
                part = wide_ref[tile, pl.ds(first + tap, GROUP)] * weights
                total = part if total is None else total + part
            fir_ref[group, tile] = total
        for frame in range(0, GROUP, 2):
            parts = [fir_ref[group, tile, frame : frame + 2] for tile in range(RADIX)]
            for m1, value in enumerate(dft8(parts, sign)):
                fir_ref[group, m1, frame : frame + 2] = value
        for m1 in range(RADIX):
            value = fir_ref[group, m1].reshape(GROUP * ROWS, LANES)
            top = value.astype(jnp.bfloat16)
            rest = (value - top.astype(jnp.float32)).astype(jnp.bfloat16)
            high = high_ref[m1]
            product = jnp.dot(
                jnp.concatenate([top, rest, top], axis=1),
                jnp.concatenate([high, high, low_ref[m1]], axis=0),
                preferred_element_type=jnp.float32,
            )
            cosines = product[:, :LANES].reshape(GROUP, ROWS, LANES)
            sines = product[:, LANES:].reshape(GROUP, ROWS, LANES)
            result = (cosines + turn(sines, sign)).astype(jnp.bfloat16)
            devices = GROUP // HOPS_DEV
            out_ref[pl.ds(group * devices, devices), :, 0, :, m1 * LANES : (m1 + 1) * LANES] = result.reshape(
                devices, HOPS_DEV, ROWS, LANES
            )

    for group in range(FRAMES // GROUP):
        one_group(group)


def early_kernel(x_ref, *refs):
    pair = pl.program_id(0)

    def load(lanes):
        return x_ref[:, pair, :, :, lanes].astype(jnp.float32).reshape(HOPS, ROWS, LANES)

    transform(load, *refs)


def late_kernel(block_ref, count_ref, place_ref, a0, a1, a2, a3, proto_ref, high_ref, low_ref, out_ref, wide_ref, fir_ref, held_ref, sem):
    pair = pl.program_id(0)

    @pl.when(pair == 0)
    def _():
        for slot in range(MAXREQ):
            shift, _ = arrival(slot, block_ref, count_ref, place_ref)
            for own, ref in enumerate((a0.at[:, 0], a1, a2, a3)):

                @pl.when(shift == own)
                def _():
                    pltpu.make_async_copy(ref, held_ref.at[slot], sem.at[slot]).start()

    for slot in range(2):
        at = pair * 2 + slot
        pltpu.make_async_copy(a1, held_ref.at[at], sem.at[at]).wait()

    ranks = [arrival(slot, block_ref, count_ref, place_ref)[1] for slot in range(MAXREQ)]
    first_rank = jnp.where(pair == 0, ranks[0], ranks[2])
    second_rank = jnp.where(pair == 0, ranks[1], ranks[3])
    is_second = (lax.broadcasted_iota(jnp.int32, (HOPS, ROWS, LANES), 1) // SHARE) % 2 == 1

    def load(lanes):
        first = held_ref[pair * 2, :, :, :, lanes].astype(jnp.float32).reshape(HOPS, ROWS, LANES)
        second = held_ref[pair * 2 + 1, :, :, :, lanes].astype(jnp.float32).reshape(HOPS, ROWS, LANES)
        first = jnp.where(first_rank == 0, first, pltpu.roll(first, ROWS - SHARE, 1))
        second = jnp.where(second_rank == 1, second, pltpu.roll(second, SHARE, 1))
        return jnp.where(is_second, second, first)

    transform(load, proto_ref, high_ref, low_ref, out_ref, wide_ref, fir_ref)


def table_specs():
    return [
        pl.BlockSpec((TAPS, NFINE), lambda p, *refs: (0, 0)),
        pl.BlockSpec((RADIX, LANES, 2 * LANES), lambda p, *refs: (0, 0, 0)),
        pl.BlockSpec((RADIX, LANES, 2 * LANES), lambda p, *refs: (0, 0, 0)),
    ]


RESULT = jax.ShapeDtypeStruct((TM, HOPS_DEV, MAXREQ // 2, ROWS, NFINE), jnp.bfloat16)


def result_spec():
    return pl.BlockSpec((TM, HOPS_DEV, 1, ROWS, NFINE), lambda p, *refs: (0, 0, p, 0, 0))


def work_space():
    return [
        pltpu.VMEM((RADIX, FRAMES + TAPS - 1, ROWS, LANES), jnp.float32),
        pltpu.VMEM((FRAMES // GROUP, RADIX, GROUP, ROWS, LANES), jnp.float32),
    ]


def filter_early(gathered, tables):
    return pl.pallas_call(
        early_kernel,
        out_shape=RESULT,
        grid=(MAXREQ // 2,),
        in_specs=[
            pl.BlockSpec(memory_space=pltpu.VMEM),
            *table_specs(),
        ],
        out_specs=result_spec(),
        scratch_shapes=work_space(),
        cost_estimate=COST,
        name="filter_early",
    )(in_vmem(gathered), *tables)


def filter_late(arrived, tables, req_block, req_count, place):
    return pl.pallas_call(
        late_kernel,
        out_shape=RESULT,
        grid_spec=pltpu.PrefetchScalarGridSpec(
            num_scalar_prefetch=3,
            grid=(MAXREQ // 2,),
            in_specs=[pl.BlockSpec(memory_space=pl.ANY)] * OWNERS + table_specs(),
            out_specs=result_spec(),
            scratch_shapes=work_space()
            + [
                pltpu.VMEM((MAXREQ, TM, HOPS_DEV, ROWS, NFINE), jnp.bfloat16),
                pltpu.SemaphoreType.DMA((MAXREQ,)),
            ],
        ),
        cost_estimate=COST,
        compiler_params=pltpu.CompilerParams(vmem_limit_bytes=56 * 2**20),
        name="filter_late",
    )(req_block, req_count, place, *map(in_hbm, arrived), *tables)


def is_active(hop, slot, start_ref, frames_ref, count_ref, place_ref):
    owner = place_ref[0]
    frame = place_ref[1] * HOPS_DEV + hop
    begin = start_ref[owner, slot]
    return (slot < count_ref[owner]) & (frame >= begin) & (frame < begin + frames_ref[owner, slot])


def turn_back(back, pick_ref, turned_ref):
    rows = back.astype(jnp.float32).reshape(TM * ROWS, NFINE).astype(jnp.bfloat16)
    columns = lax.dot_general(rows, pick_ref[...], (((0,), (0,)), ((), ())), preferred_element_type=jnp.float32)
    for m1 in range(RADIX):
        for slot in range(2):
            turned_ref[slot, pl.ds(m1, LANES, stride=RADIX), :] = columns[
                m1 * LANES : (m1 + 1) * LANES, slot * BLOCKW : (slot + 1) * BLOCKW
            ]


def unpack_early_kernel(start_ref, frames_ref, count_ref, place_ref, early_ref, out_ref, turned_ref, pick_ref):
    refs = start_ref, frames_ref, count_ref, place_ref
    step = pl.program_id(0)
    hop, pair = step // (MAXREQ // 2), step % (MAXREQ // 2)

    @pl.when(step == 0)
    def _():
        pick_ref[...] = share_pick()

    @pl.when(is_active(hop, 2 * pair, *refs) | is_active(hop, 2 * pair + 1, *refs))
    def _():
        turn_back(early_ref[:, 0, 0], pick_ref, turned_ref)
        out_ref[0] = turned_ref[...].astype(jnp.bfloat16)


def unpack_kernel(start_ref, frames_ref, count_ref, place_ref, part_ref, late_ref, out_ref, turned_ref, pick_ref):
    refs = start_ref, frames_ref, count_ref, place_ref
    step = pl.program_id(0)
    hop, pair = step // (MAXREQ // 2), step % (MAXREQ // 2)

    @pl.when(step == 0)
    def _():
        pick_ref[...] = share_pick()

    @pl.when(is_active(hop, 2 * pair, *refs) | is_active(hop, 2 * pair + 1, *refs))
    def _():
        turn_back(late_ref[:, hop, pair], pick_ref, turned_ref)

    for which in range(2):
        active = is_active(hop, 2 * pair + which, *refs)

        @pl.when(active)
        def _():
            early = part_ref[0, which]
            late = turned_ref[which].astype(jnp.bfloat16)
            out_ref[0, 0, which, 0] = jnp.concatenate([early[:, :HALF], late[:, :HALF]], axis=1)
            out_ref[0, 0, which, 1] = jnp.concatenate([early[:, HALF:], late[:, HALF:]], axis=1)

        @pl.when(jnp.logical_not(active))
        def _():
            out_ref[0, 0, which] = jnp.zeros((2, NFINE, BLOCKW), jnp.bfloat16)


STEPS = HOPS_DEV * MAXREQ // 2


def unpack_early(early, req_start, req_frames, req_count, place):
    return pl.pallas_call(
        unpack_early_kernel,
        out_shape=jax.ShapeDtypeStruct((STEPS, 2, NFINE, BLOCKW), jnp.bfloat16),
        grid_spec=pltpu.PrefetchScalarGridSpec(
            num_scalar_prefetch=4,
            grid=(STEPS,),
            in_specs=[pl.BlockSpec((TM, 1, 1, ROWS, NFINE), lambda i, *refs: (0, i // (MAXREQ // 2), i % (MAXREQ // 2), 0, 0))],
            out_specs=pl.BlockSpec((1, 2, NFINE, BLOCKW), lambda i, *refs: (i, 0, 0, 0)),
            scratch_shapes=[
                pltpu.VMEM((2, NFINE, BLOCKW), jnp.float32),
                pltpu.VMEM((TM * ROWS, 2 * BLOCKW), jnp.bfloat16),
            ],
        ),
        cost_estimate=COST,
        compiler_params=pltpu.CompilerParams(vmem_limit_bytes=52 * 2**20),
        name="unpack_early",
    )(req_start, req_frames, req_count, place, in_hbm(early))


def unpack(part, late, req_start, req_frames, req_count, place):
    resident = pl.BlockSpec(memory_space=pltpu.VMEM)
    return pl.pallas_call(
        unpack_kernel,
        out_shape=jax.ShapeDtypeStruct((HOPS_DEV, 1, MAXREQ, 2, NFINE, BLOCKW), jnp.bfloat16),
        grid_spec=pltpu.PrefetchScalarGridSpec(
            num_scalar_prefetch=4,
            grid=(STEPS,),
            in_specs=[pl.BlockSpec((1, 2, NFINE, BLOCKW), lambda i, *refs: (i, 0, 0, 0)), resident],
            out_specs=pl.BlockSpec(
                (1, 1, 2, 2, NFINE, BLOCKW),
                lambda i, *refs: (i // (MAXREQ // 2), 0, i % (MAXREQ // 2), 0, 0, 0),
            ),
            scratch_shapes=[
                pltpu.VMEM((2, NFINE, BLOCKW), jnp.float32),
                pltpu.VMEM((TM * ROWS, 2 * BLOCKW), jnp.bfloat16),
            ],
        ),
        compiler_params=pltpu.CompilerParams(vmem_limit_bytes=52 * 2**20),
        name="unpack",
    )(req_start, req_frames, req_count, place, in_hbm(part), in_vmem(late))


def over_tm(array):
    return lax.all_to_all(array, "tm", split_axis=0, concat_axis=0, tiled=True)


def along_chan(arrays):
    return [arrays[0]] + [
        lax.ppermute(in_hbm(arrays[d]), "chan", [(s, (s + d) % OWNERS) for s in range(OWNERS)])
        for d in range(1, OWNERS)
    ]


def shards(coarse, prototype, req_block, req_start, req_frames, req_count):
    column = lax.axis_index("chan").astype(jnp.int32)
    place = jnp.stack([column, lax.axis_index("tm").astype(jnp.int32)])
    tables = (prototype, *(jnp.asarray(table) for table in dft_tables()))
    plan, late, last, *early = pack(coarse, req_block, req_count, place)
    late = over_tm(late)
    late, last = lax.optimization_barrier((late, last))
    last = lax.cond(plan[OWNERS] > 0, over_tm, lambda same: same, last)
    early = choose(along_chan(early), req_block, req_count, place)
    late, last, early = lax.optimization_barrier((late, last, early))
    early = over_tm(early)
    late = along_chan([late, *split(plan, late, last)])
    early = filter_early(early, tables)
    _, *late = lax.optimization_barrier((early, *late))
    early = over_tm(early)
    _, late = lax.optimization_barrier((early, filter_late(late, tables, req_block, req_count, place)))
    late = over_tm(late)
    part = unpack_early(early, req_start, req_frames, req_count, place)
    return unpack(part, late, req_start, req_frames, req_count, place)


def solution(mesh):
    return jax.shard_map(
        shards,
        mesh=mesh,
        in_specs=(P(None, "tm", "chan"), P(), P(), P(), P(), P()),
        out_specs=P("tm", "chan", None, None, None, None),
        check_vma=False,
    )
```
